256 devices in a mesh: branch: 4 (over y_hi, core), dap: 64 (over x, z, y_lo).
Axes of the slice: x: 4, y: 4 (y_hi: 2, y_lo: 2; y = y_hi * 2 + y_lo), z: 8, core: 2. Of those that a mesh axis runs over, the one named last changes fastest.
Arguments:
- alignment: bfloat16 [512, 512, 256], P('dap'), may hold values from -24 to 24
- pair_rep: bfloat16 [512, 512, 128], P('dap', 'branch'), may hold values from -6 to 6
- align_mask: int32 [512, 512], replicated, may hold values from 0 to 1, as said below
- residue_mask: int32 [512], replicated, may hold values from 0 to 1, as said below
- bias_weight: bfloat16 [128, 8], replicated, may hold values from -1 to 1
- row_proj_weight: bfloat16 [4, 256, 256], P(None, None, 'branch'), may hold values from -0.375 to 0.375
- row_out_weight: bfloat16 [256, 256], replicated, may hold values from -1 to 1
- column_proj_weight: bfloat16 [4, 256, 256], P(None, None, 'branch'), may hold values from -0.375 to 0.375
- column_out_weight: bfloat16 [256, 256], replicated, may hold values from -1 to 1
- outer_factor_weight: bfloat16 [256, 64], replicated, may hold values from -0.375 to 0.375
- outer_out: bfloat16 [1024, 128], replicated, may hold values from -0.375 to 0.375
Outputs:
- updated_alignment: bfloat16 [512, 512, 256], P(None, 'dap')
- pair_out: bfloat16 [512, 512, 128], P('dap', 'branch')
The draws below stay inside these ranges and needn't reach their ends.
Inputs may be any that keep to these rules, and one draw needn't show every extreme that they name: `align_mask`: the first alignment is all ones; in every other alignment the ones form one contiguous run of residues that is never empty. `residue_mask`: ones on a leading run of residues and zeros after it; both values occur.
All inputs are finite; a program needn't handle non-finite values.
Results may differ from the reference program's by a relative error of at most 0.0085.
Values may be sent and summed in bfloat16 or wider, within the bound.
A program may use at most 128 MiB of HBM per device.

```python
import math
import jax
import jax.numpy as jnp
from jax import lax

ALIGN_CHANNELS = 256
PAIR_DIM = 128
ATTN_HEAD_COUNT = 8
HEAD_CHANNELS = 32
FACTOR_CHANNELS = 32
SEQUENCE_COUNT = 512
RESIDUE_COUNT = 512


def draw_alignment(key, part):
    random_keys = jax.random.split(key, 2)
    shared_setup = jax.random.normal(random_keys[0], (RESIDUE_COUNT, ALIGN_CHANNELS), jnp.float32)
    random_noise = jax.random.normal(random_keys[1], (SEQUENCE_COUNT, RESIDUE_COUNT, ALIGN_CHANNELS), jnp.float32)
    values = 0.8 * shared_setup[None, :, :] + random_noise
    return jnp.clip(values, -24.0, 24.0).astype(jnp.bfloat16)


def draw_align_mask(key, part):
    random_keys = jax.random.split(jax.random.fold_in(key, 11), 2)
    least = max(RESIDUE_COUNT // 4, 1)
    first = jax.random.randint(random_keys[0], (SEQUENCE_COUNT, 1), 0, RESIDUE_COUNT - least + 1)
    length = jax.random.randint(random_keys[1], (SEQUENCE_COUNT, 1), least, RESIDUE_COUNT + 1 - first)
    position = jnp.arange(RESIDUE_COUNT, dtype=jnp.int32)[None, :]
    live = jnp.logical_and(position >= first, position < first + length)
    leading = jnp.arange(SEQUENCE_COUNT, dtype=jnp.int32)[:, None] == 0
    return jnp.logical_or(live, leading).astype(jnp.int32)


def draw_residue_mask(key, part):
    length = jax.random.randint(jax.random.fold_in(key, 23), (), RESIDUE_COUNT // 2, RESIDUE_COUNT)
    return (jnp.arange(RESIDUE_COUNT, dtype=jnp.int32) < length).astype(jnp.int32)


def block_scale(own_key, shape, cuts, low, top_value):
    level = 1.0
    for dim, parts in cuts:
        draws = jax.random.uniform(jax.random.fold_in(jax.random.fold_in(own_key, 6), dim), (parts,), jnp.float32, low / len(cuts), top_value / len(cuts))
        level = level * jnp.repeat(jnp.exp(draws), shape[dim] // parts).reshape((-1,) + (1,) * (len(shape) - 1 - dim))
    return level


def gaussian(rng, shape, scale, most, cuts=(), kind=jnp.bfloat16):
    drawn = scale * jax.random.normal(rng, shape, jnp.float32)
    if cuts:
        drawn = drawn * block_scale(rng, shape, cuts, -0.22, 0.18)
    return jnp.clip(drawn, -most, most).astype(kind)


def setup_inputs(seed: int = 0) -> dict:
    key_of = jax.random.split(jax.random.key(seed), 12)
    alignment = draw_alignment(jax.random.fold_in(key_of[11], 71), 0)
    pair_rep = gaussian(key_of[1], (RESIDUE_COUNT, RESIDUE_COUNT, PAIR_DIM), 1.0, 6.0, ((0, 64), (1, 4)))
    align_mask = draw_align_mask(jax.random.fold_in(key_of[11], 71), 0)
    residue_mask = draw_residue_mask(jax.random.fold_in(key_of[11], 71), 0)
    bias_weight = gaussian(key_of[4], (PAIR_DIM, ATTN_HEAD_COUNT), (PAIR_DIM // 4) ** -0.5, 1.0)
    row_proj_weight = gaussian(key_of[5], (4, ALIGN_CHANNELS, ATTN_HEAD_COUNT * HEAD_CHANNELS), ALIGN_CHANNELS ** -0.5, 0.375, ((2, 4),))
    row_out_weight = gaussian(key_of[6], (ATTN_HEAD_COUNT * HEAD_CHANNELS, ALIGN_CHANNELS), HEAD_CHANNELS ** -0.5, 1.0)
    column_proj_weight = gaussian(key_of[7], (4, ALIGN_CHANNELS, ATTN_HEAD_COUNT * HEAD_CHANNELS), ALIGN_CHANNELS ** -0.5, 0.375, ((2, 4),))
    column_out_weight = gaussian(key_of[8], (ATTN_HEAD_COUNT * HEAD_CHANNELS, ALIGN_CHANNELS), HEAD_CHANNELS ** -0.5, 1.0)
    outer_factor_weight = gaussian(key_of[9], (ALIGN_CHANNELS, 2 * FACTOR_CHANNELS), ALIGN_CHANNELS ** -0.5, 0.375)
    outer_out = gaussian(key_of[10], (FACTOR_CHANNELS * FACTOR_CHANNELS, PAIR_DIM), (FACTOR_CHANNELS * FACTOR_CHANNELS // 4) ** -0.5, 0.375)
    return dict(alignment=alignment, pair_rep=pair_rep, align_mask=align_mask, residue_mask=residue_mask, bias_weight=bias_weight, row_proj_weight=row_proj_weight, row_out_weight=row_out_weight, column_proj_weight=column_proj_weight, column_out_weight=column_out_weight, outer_factor_weight=outer_factor_weight, outer_out=outer_out)


norm_eps = 1e-05
count_eps = 0.001

def layer_normalize(values):
    centre = lax.optimization_barrier(jnp.mean(values, axis=-1, keepdims=True))
    centred = values - centre
    spread = lax.optimization_barrier(jnp.mean(centred * centred, axis=-1, keepdims=True))
    return centred * lax.rsqrt(spread + norm_eps)

def attend_heads(inputs, key_mask, proj_weight, out_weight, score_bias):
    normed = layer_normalize(inputs.astype(jnp.float32)).astype(jnp.bfloat16)

    def attend_one(operands):
        current, normed_row, mask_row = operands
        length = current.shape[0]
        projected = jnp.einsum('lc,kcd->kld', normed_row.astype(jnp.float32), proj_weight.astype(jnp.float32))
        triple = lax.optimization_barrier(projected[:3].astype(jnp.bfloat16)).astype(jnp.float32)
        queries = triple[0].reshape(length, ATTN_HEAD_COUNT, HEAD_CHANNELS)
        key_rows = triple[1].reshape(length, ATTN_HEAD_COUNT, HEAD_CHANNELS)
        value_rows = triple[2].reshape(length, ATTN_HEAD_COUNT, HEAD_CHANNELS)
        scores = jnp.einsum('ihd,jhd->hij', queries, key_rows) / math.sqrt(HEAD_CHANNELS)
        if score_bias is not None:
            scores = scores + score_bias.astype(jnp.float32)
        raised = jnp.exp(scores) * mask_row[None, None, :]
        weights = raised / lax.optimization_barrier(jnp.sum(raised, axis=-1, keepdims=True))
        weights = lax.optimization_barrier(weights.astype(jnp.bfloat16)).astype(jnp.float32)
        attended_rows = jnp.einsum('hij,jhd->ihd', weights, value_rows).reshape(length, ATTN_HEAD_COUNT * HEAD_CHANNELS)
        gating = jax.nn.sigmoid(projected[3])
        heads_out = (attended_rows * gating).astype(jnp.bfloat16)
        update = jnp.dot(heads_out, out_weight, preferred_element_type=jnp.float32)
        return (current.astype(jnp.float32) + update).astype(jnp.bfloat16)
    return lax.map(attend_one, (inputs, normed, key_mask))

def reference(alignment, pair_rep, align_mask, residue_mask, bias_weight, row_proj_weight, row_out_weight, column_proj_weight, column_out_weight, outer_factor_weight, outer_out):
    float_mask = align_mask.astype(jnp.float32)
    res_float = residue_mask.astype(jnp.float32)
    pair_normed = layer_normalize(pair_rep.astype(jnp.float32)).astype(jnp.bfloat16)
    pair_score_bias = jnp.einsum('ijc,ch->hij', pair_normed.astype(jnp.float32), bias_weight.astype(jnp.float32)).astype(jnp.bfloat16)
    row_alignment = attend_heads(alignment, float_mask, row_proj_weight, row_out_weight, pair_score_bias)
    transposed_rows = jnp.swapaxes(row_alignment, 0, 1)
    column_alignment = attend_heads(transposed_rows, jnp.swapaxes(float_mask, 0, 1), column_proj_weight, column_out_weight, None)
    updated_alignment = jnp.swapaxes(column_alignment, 0, 1)
    outer_mean_normed = layer_normalize(updated_alignment.astype(jnp.float32)).astype(jnp.bfloat16)
    factor_pairs = jnp.einsum('src,ce->sre', outer_mean_normed.astype(jnp.float32), outer_factor_weight.astype(jnp.float32))
    factor_pairs = (factor_pairs * float_mask[:, :, None]).astype(jnp.bfloat16)
    left_side = factor_pairs[:, :, :FACTOR_CHANNELS]
    right_side = factor_pairs[:, :, FACTOR_CHANNELS:].astype(jnp.float32)
    counts = jnp.dot(float_mask.T, float_mask, preferred_element_type=jnp.float32, precision=lax.Precision.HIGHEST)
    outer_weight = outer_out.astype(jnp.float32)

    def outer_row(operands):
        left_row, count_row, pair_row, live_one = operands
        outer = jnp.einsum('sc,sje->jce', left_row.astype(jnp.float32), right_side)
        outer = outer.reshape(right_side.shape[1], FACTOR_CHANNELS * FACTOR_CHANNELS)
        update = jnp.dot(outer, outer_weight, precision=lax.Precision.HIGHEST)
        update = update / (count_row[:, None] + count_eps) * (live_one * res_float)[:, None]
        return (pair_row.astype(jnp.float32) + update).astype(jnp.bfloat16)
    pair_out = lax.map(outer_row, (jnp.swapaxes(left_side, 0, 1), counts, pair_rep, res_float))
    return (updated_alignment, pair_out)
```

```python
import functools
import math

import jax
import jax.numpy as jnp
from jax import lax
from jax.experimental import pallas as pl
from jax.experimental.pallas import tpu as pltpu
from jax.sharding import PartitionSpec as P

HEADS = 8
HEAD = 32
FACTOR = 32
norm_eps = 1e-05
count_eps = 0.001
SCALE = 1.0 / math.sqrt(HEAD)
F32 = jnp.float32
BF16 = jnp.bfloat16
MESH = pl.DeviceIdType.MESH
VMEM_LIMIT = 60 * 1024 * 1024
SEQS = 512
TILE = 128
NT = (((1,), (1,)), ((), ()))
TN = (((0,), (1,)), ((), ()))


def normalize(values):
    centre = jnp.mean(values, axis=-1, keepdims=True)
    centred = values - centre
    spread = jnp.mean(centred * centred, axis=-1, keepdims=True)
    return centred * lax.rsqrt(spread + norm_eps)


def dot(a, b, dims=(((1,), (0,)), ((), ()))):
    return lax.dot_general(a, b, dims, preferred_element_type=F32)


def lane_block(rows, index):
    lanes = lax.broadcasted_iota(jnp.int32, (rows, 128), 1)
    return (lanes // HEAD == index).astype(F32)


def attend(q_s, k_s, g_s, rhs_s, o_s, bias_of, mask_of):
    def run(stable):
        def tile(step, extremes):
            rows = pl.ds(pl.multiple_of(step * TILE, TILE), TILE)
            q = q_s[rows, :]
            total = None
            for n in range(4):
                qn = q * lane_block(TILE, n).astype(BF16)
                scores = dot(qn, k_s[...], NT) * SCALE
                if bias_of is not None:
                    scores = scores + bias_of(step, n)
                if stable:
                    scores = jnp.where(mask_of(n) > 0.0, scores, -1e30)
                    scores = scores - jnp.max(scores, axis=1, keepdims=True)
                raised = jnp.exp(scores).astype(BF16)
                part = dot(raised, rhs_s[n * SEQS : (n + 1) * SEQS, :])
                total = part if total is None else total + part
            sums = total[:, 128:]
            o_s[rows, :] = total[:, :128] / sums * g_s[rows, :]
            low, high = extremes
            folded = sums.reshape(TILE // 8, 8, 128)
            return jnp.minimum(low, jnp.min(folded, axis=0)), jnp.maximum(
                high, jnp.max(folded, axis=0)
            )

        start = (jnp.full((8, 128), 1.0, F32), jnp.full((8, 128), 1.0, F32))
        return lax.fori_loop(0, SEQS // TILE, tile, start)

    low, high = run(False)
    fine = jnp.logical_and(jnp.min(low) > 1e-30, jnp.max(high) < 1e30)

    @pl.when(jnp.logical_not(fine))
    def _():
        run(True)


def fill_rhs(rhs_s, values, mask):
    for n in range(4):
        block = mask * lane_block(SEQS, n)
        rhs_s[n * SEQS : (n + 1) * SEQS, :128] = (values * block).astype(BF16)
        rhs_s[n * SEQS : (n + 1) * SEQS, 128:] = block.astype(BF16)


def bias_kernel(pair_ref, weight_ref, out_ref):
    rows, cols, width = pair_ref.shape
    x = pair_ref[...].astype(F32).reshape(rows * cols, width)
    normed = normalize(x).astype(BF16)
    res = dot(weight_ref[...], normed, TN)
    for i in range(rows):
        out_ref[:, i, :] = res[:, i * cols : (i + 1) * cols].astype(BF16)


def row_kernel(
    x_ref, w_ref, bias_ref, maskcol_ref, maskrow_ref, out_ref, q_s, k_s, g_s, rhs_s, o_s, buf
):
    pair = pl.program_id(0)
    normed = [normalize(x_ref[p].astype(F32)).astype(BF16) for p in range(2)]
    both = jnp.concatenate(normed, axis=1)
    q_s[...] = dot(both, w_ref[:, :128]).astype(BF16)
    k_s[...] = dot(both, w_ref[:, 128:256]).astype(BF16)
    values = dot(both, w_ref[:, 256:384]).astype(BF16).astype(F32)
    fill_rhs(rhs_s, values, maskcol_ref[0].astype(F32))
    g_s[...] = jax.nn.sigmoid(dot(both, w_ref[:, 384:]))

    def bias_of(step, n):
        pieces = []
        for b in range(4):
            piece = bias_ref[pl.ds(step * (TILE // 8), TILE // 8), b, n % 2]
            pieces.append(piece.astype(F32).reshape(TILE, 128))
        return jnp.concatenate(pieces, axis=1)

    attend(q_s, k_s, g_s, rhs_s, o_s, bias_of, lambda n: maskrow_ref[0, n // 2 : n // 2 + 1, :])
    for k in range(2):
        buf[pl.ds(pair * 2 + k, 256, stride=8), :] = o_s[pl.ds(k, 256, stride=2), :]

    @pl.when(pair == pl.num_programs(0) - 1)
    def _():
        out_ref[...] = buf[...].reshape(256, 8, 128).astype(BF16)


def column_kernel(
    a_ref,
    res_ref,
    wrow_ref,
    wcol_ref,
    wout_ref,
    wfac_ref,
    maskcol_ref,
    maskrow_ref,
    upd_ref,
    left_ref,
    right_ref,
    x_s,
    msa_s,
    n_s,
    q_s,
    k_s,
    g_s,
    rhs_s,
    o_s,
    heads_s,
):
    k = pl.program_id(0)

    @pl.when(k == 0)
    def _():
        pieces = [a_ref[:, b].astype(F32).reshape(SEQS, 128).astype(BF16) for b in range(4)]
        x = dot(jnp.concatenate(pieces, axis=1), wrow_ref[...])
        for j in range(4):
            x_s[j] = x[:, j * 128 : (j + 1) * 128]

    mine = [x_s[j, pl.ds(k, 256, stride=2), :] for j in range(4)]
    rows = jnp.concatenate(
        [jnp.concatenate(mine[:2], axis=1), jnp.concatenate(mine[2:], axis=1)], axis=0
    )
    msa = (rows + res_ref[0].astype(F32)).astype(BF16).astype(F32)
    msa_s[...] = msa
    n_s[...] = normalize(msa).astype(BF16)
    for group in range(2):
        lanes = slice(group * 128, group * 128 + 128)

        def project(part):
            at = part * 256 + group * 128
            return dot(n_s[...], wcol_ref[:, at : at + 128])

        q_s[...] = project(0).astype(BF16)
        k_s[...] = project(1).astype(BF16)
        values = project(2).astype(BF16).astype(F32)
        fill_rhs(rhs_s, values, maskcol_ref[0].astype(F32))
        g_s[...] = jax.nn.sigmoid(project(3))
        attend(q_s, k_s, g_s, rhs_s, o_s, None, lambda n: maskrow_ref[0])
        heads_s[:, lanes] = o_s[...].astype(BF16)
    updated = (msa_s[...] + dot(heads_s[...], wout_ref[...])).astype(BF16)
    upd_ref[0] = updated
    outer = normalize(updated.astype(F32)).astype(BF16)
    factors = dot(wfac_ref[...], outer, TN) * maskrow_ref[0]
    left_ref[0] = factors[:FACTOR].astype(BF16)
    right_ref[0] = factors[FACTOR:].astype(BF16)


def place():
    branch = lax.axis_index("branch")
    dap = lax.axis_index("dap")
    return dict(
        branch=branch,
        dap=dap,
        y_hi=branch // 2,
        core=branch % 2,
        x=dap // 16,
        z=(dap // 2) % 8,
        y_lo=dap % 2,
    )


def outer_kernel(
    left_ref,
    right_ref,
    upd_ref,
    weight_ref,
    gather_ref,
    pair_ref,
    l_s,
    lp_s,
    r_s,
    perm_s,
    wide_s,
    lhs_s,
    send_s,
    l_send,
    l_recv,
    r_send,
    r_recv,
    f_send,
    f_recv,
    u_send,
    u_recv,
    p_send,
    p_recv,
):
    at = place()
    branch, dap, y_hi, core = at["branch"], at["dap"], at["y_hi"], at["core"]
    x, z, y_lo = at["x"], at["z"], at["y_lo"]
    barrier = pltpu.get_barrier_semaphore()

    def greet(index, _):
        other_b = index // 8
        other_d = (index // 2) % 4 * 16 + z * 2 + index % 2
        other = jnp.logical_or(other_b != branch, other_d != dap)

        @pl.when(other)
        def _():
            pl.semaphore_signal(barrier, 1, device_id=(other_b, other_d), device_id_type=MESH)

        return 0

    lax.fori_loop(0, 32, greet, 0)

    def greet_line(index, _):
        other_z = index // 2

        @pl.when(other_z != z)
        def _():
            pl.semaphore_signal(
                barrier,
                1,
                device_id=(y_hi * 2 + index % 2, x * 16 + other_z * 2 + y_lo),
                device_id_type=MESH,
            )

        return 0

    lax.fori_loop(0, 16, greet_line, 0)
    pl.semaphore_wait(barrier, 31 + 14)

    def send(src, dst, send_sem, recv_sem, to):
        other = jnp.logical_or(to[0] != branch, to[1] != dap)

        @pl.when(other)
        def _():
            pltpu.make_async_remote_copy(
                src, dst, send_sem, recv_sem, device_id=to, device_id_type=MESH
            ).start()

        @pl.when(jnp.logical_not(other))
        def _():
            pltpu.make_async_copy(src, dst, recv_sem).start()

    def sent(src, send_sem, to):
        other = jnp.logical_or(to[0] != branch, to[1] != dap)

        @pl.when(other)
        def _():
            pltpu.make_async_copy(src, src, send_sem).wait()

    def arrived(dst, recv_sem):
        pltpu.make_async_copy(dst, dst, recv_sem).wait()

    def to_left(slot):
        return ((slot % 4) // 2 * 2 + y_lo, slot // 4 * 16 + z * 2 + slot % 2)

    def to_right(slot):
        return (branch, x * 16 + slot * 2 + y_lo)

    def to_branch(slot):
        return (slot, dap)

    def to_pair(slot):
        return (x, slot * 16 + z * 2 + core)

    partner = (y_hi * 2 + 1 - core, dap)
    my_left = x * 4 + branch
    for slot in range(8):
        send(right_ref, r_s.at[z, core], r_send.at[slot], r_recv.at[z, core], to_right(slot))
    for slot in range(16):
        send(left_ref, l_s.at[my_left], l_send.at[slot], l_recv.at[my_left], to_left(slot))
    for slot in range(4):
        send(upd_ref, gather_ref.at[branch], u_send.at[slot], u_recv.at[branch], to_branch(slot))

    wide_s[...] = jnp.zeros_like(wide_s)

    def widen(c, _):
        block = weight_ref[pl.ds(pl.multiple_of(c * 32, 32), 32), :]
        for j in range(4):
            rows = pl.ds(pl.multiple_of(c * 128 + j * 32, 32), 32)
            wide_s[rows, j * 128 : (j + 1) * 128] = block
        return 0

    lax.fori_loop(0, 32, widen, 0)

    def permute(c, _):
        source = lax.broadcasted_iota(jnp.int32, (32, 1024), 1)
        wanted = lax.broadcasted_iota(jnp.int32, (32, 1024), 0) * 32 + c
        rows = pl.ds(pl.multiple_of(c * 32, 32), 32)
        perm_s[rows, :] = (source == wanted).astype(F32).astype(BF16)
        return 0

    lax.fori_loop(0, 32, permute, 0)

    for slot in range(8):
        arrived(r_s.at[slot, core], r_recv.at[slot, core])
        pltpu.make_async_remote_copy(
            r_s.at[slot, core],
            r_s.at[slot, core],
            f_send.at[slot],
            f_recv.at[slot],
            device_id=partner,
            device_id_type=MESH,
        ).start()
    for slot in range(16):
        arrived(l_s.at[slot], l_recv.at[slot])
    lefts = l_s[...].reshape(1024, SEQS)

    def reorder(c, _):
        rows = pl.ds(pl.multiple_of(c * 128, 128), 128)
        lp_s[rows, :] = dot(perm_s[rows, :], lefts).astype(BF16)
        return 0

    lax.fori_loop(0, 8, reorder, 0)
    for slot in range(8):
        arrived(r_s.at[slot, 1 - core], f_recv.at[slot])
    rights = r_s[...].reshape(1024, SEQS)

    for cp in range(16):
        block = dot(lp_s[cp * 64 : (cp + 1) * 64, :], rights, NT)
        for c2 in range(2):
            tiles = [
                block[c2 * 32 + xi * 8 : c2 * 32 + xi * 8 + 8, jg * 128 : jg * 128 + 128]
                for xi in range(4)
                for jg in range(8)
            ]
            lanes = (cp * 2 + c2) * 128
            lhs_s[:, lanes : lanes + 128] = jnp.concatenate(tiles, axis=0).astype(BF16)
    for xi in range(4):
        update = dot(lhs_s[xi * 64 : (xi + 1) * 64, :], wide_s[...])
        send_s[xi] = update.reshape(8, 8, 512).astype(BF16)
    for slot in range(4):
        send(
            send_s.at[slot],
            pair_ref.at[y_hi * 2 + y_lo],
            p_send.at[slot],
            p_recv.at[y_hi * 2 + y_lo],
            to_pair(slot),
        )
    for slot in range(8):
        sent(right_ref, r_send.at[slot], to_right(slot))
        pltpu.make_async_copy(r_s.at[slot, core], r_s.at[slot, core], f_send.at[slot]).wait()
    for slot in range(16):
        sent(left_ref, l_send.at[slot], to_left(slot))
    for slot in range(4):
        sent(upd_ref, u_send.at[slot], to_branch(slot))
        sent(send_s.at[slot], p_send.at[slot], to_pair(slot))
        arrived(gather_ref.at[slot], u_recv.at[slot])
        arrived(pair_ref.at[slot], p_recv.at[slot])


def whole(shape):
    return pl.BlockSpec(shape, lambda *_: (0,) * len(shape))


def per_device(
    alignment,
    pair_rep,
    align_mask,
    residue_mask,
    bias_weight,
    row_proj_weight,
    row_out_weight,
    column_proj_weight,
    column_out_weight,
    outer_factor_weight,
    outer_out,
):
    branch = lax.axis_index("branch")
    dap = lax.axis_index("dap")
    vmem = pltpu.VMEM
    params = pltpu.CompilerParams(vmem_limit_bytes=VMEM_LIMIT)

    bias_block = pl.pallas_call(
        bias_kernel,
        out_shape=jax.ShapeDtypeStruct((HEADS, 8, 128), BF16),
        compiler_params=params,
        name="pair_bias",
    )(pair_rep, bias_weight)
    spread = jnp.broadcast_to(bias_block.reshape(1, 4, 2, 8, 128), (64, 4, 2, 8, 128))
    bias = lax.all_to_all(
        spread.reshape(256, 2, 8, 128), ("dap", "branch"), split_axis=0, concat_axis=0, tiled=True
    ).reshape(64, 4, 2, 8, 128)

    by_owner = alignment.reshape(8, 64, 4, 2, 256)
    mine = lax.dynamic_slice_in_dim(by_owner, branch, 1, 2)[:, :, 0]
    mine = jnp.transpose(mine.reshape(4, 2, 64, 2, 256), (2, 3, 1, 0, 4))
    moved = lax.all_to_all(mine, "dap", split_axis=0, concat_axis=0, tiled=True)
    residual = jnp.transpose(moved, (1, 2, 0, 3, 4)).reshape(2, SEQS, 256)

    wcol = jnp.broadcast_to(column_proj_weight[None], (4, 4, 256, 64))
    wcol = lax.all_to_all(wcol, "branch", split_axis=0, concat_axis=0, tiled=True)
    wcol = jnp.transpose(wcol, (2, 1, 0, 3)).reshape(256, 1024)

    half = jnp.transpose(row_proj_weight, (1, 0, 2))
    none = jnp.zeros_like(half)
    wrow = jnp.concatenate(
        [jnp.concatenate([half, none], axis=2), jnp.concatenate([none, half], axis=2)], axis=0
    ).reshape(512, 512)
    out_half = row_out_weight.reshape(4, 64, 256)
    out_none = jnp.zeros_like(out_half)
    wrow_out = jnp.concatenate(
        [
            jnp.concatenate([out_half, out_none], axis=2),
            jnp.concatenate([out_none, out_half], axis=2),
        ],
        axis=1,
    ).reshape(512, 512)

    seq_mask = lax.dynamic_slice_in_dim(align_mask, dap * 8, 8, 0).astype(F32)
    row_mask = seq_mask.reshape(4, 2, SEQS)
    row_maskcol = jnp.repeat(jnp.transpose(row_mask, (0, 2, 1)), 64, axis=2).astype(BF16)
    res_mask = lax.dynamic_slice_in_dim(align_mask, dap * 8 + branch * 2, 2, 1).astype(F32)
    res_mask = jnp.transpose(res_mask.reshape(256, 2, 2), (2, 1, 0)).reshape(2, 1, SEQS)
    col_maskcol = jnp.broadcast_to(res_mask.reshape(2, SEQS, 1), (2, SEQS, 128)).astype(BF16)

    attend_scratch = [
        vmem((SEQS, 128), BF16),
        vmem((SEQS, 128), BF16),
        vmem((SEQS, 128), F32),
        vmem((4 * SEQS, 256), BF16),
        vmem((SEQS, 128), F32),
    ]
    heads = pl.pallas_call(
        row_kernel,
        grid=(4,),
        in_specs=[
            pl.BlockSpec((2, SEQS, 256), lambda i: (i, 0, 0)),
            whole((512, 512)),
            whole((64, 4, 2, 8, 128)),
            pl.BlockSpec((1, SEQS, 128), lambda i: (i, 0, 0)),
            pl.BlockSpec((1, 2, SEQS), lambda i: (i, 0, 0)),
        ],
        out_specs=whole((256, 8, 128)),
        out_shape=jax.ShapeDtypeStruct((256, 8, 128), BF16),
        scratch_shapes=attend_scratch + [vmem((2048, 128), F32)],
        compiler_params=params,
        name="row_attention",
    )(alignment, wrow, bias, row_maskcol, row_mask)
    got = lax.all_to_all(heads, ("dap", "branch"), split_axis=0, concat_axis=0, tiled=True)

    updated, left, right = pl.pallas_call(
        column_kernel,
        grid=(2,),
        in_specs=[
            whole((64, 4, 8, 128)),
            pl.BlockSpec((1, SEQS, 256), lambda i: (i, 0, 0)),
            whole((512, 512)),
            whole((256, 1024)),
            whole((256, 256)),
            whole((256, 64)),
            pl.BlockSpec((1, SEQS, 128), lambda i: (i, 0, 0)),
            pl.BlockSpec((1, 1, SEQS), lambda i: (i, 0, 0)),
        ],
        out_specs=(
            pl.BlockSpec((1, SEQS, 256), lambda i: (i, 0, 0)),
            pl.BlockSpec((1, FACTOR, SEQS), lambda i: (i, 0, 0)),
            pl.BlockSpec((1, FACTOR, SEQS), lambda i: (i, 0, 0)),
        ),
        out_shape=(
            jax.ShapeDtypeStruct((2, SEQS, 256), BF16),
            jax.ShapeDtypeStruct((2, FACTOR, SEQS), BF16),
            jax.ShapeDtypeStruct((2, FACTOR, SEQS), BF16),
        ),
        scratch_shapes=[
            vmem((4, SEQS, 128), F32),
            vmem((SEQS, 256), F32),
            vmem((SEQS, 256), BF16),
        ]
        + attend_scratch
        + [vmem((SEQS, 256), BF16)],
        compiler_params=params,
        name="column_attention",
    )(
        got.reshape(64, 4, 8, 128),
        residual,
        wrow_out,
        wcol,
        column_out_weight,
        outer_factor_weight,
        col_maskcol,
        res_mask,
    )

    dma = pltpu.SemaphoreType.DMA
    gathered, pairs = pl.pallas_call(
        outer_kernel,
        in_specs=[pl.BlockSpec(memory_space=vmem)] * 4,
        out_specs=(pl.BlockSpec(memory_space=vmem),) * 2,
        out_shape=(
            jax.ShapeDtypeStruct((4, 2 * SEQS, 256), BF16),
            jax.ShapeDtypeStruct((4, 8, 8, 512), BF16),
        ),
        scratch_shapes=[
            vmem((16, 64, SEQS), BF16),
            vmem((1024, SEQS), BF16),
            vmem((8, 2, 64, SEQS), BF16),
            vmem((1024, 1024), BF16),
            vmem((4096, 512), BF16),
            vmem((256, 4096), BF16),
            vmem((4, 8, 8, 512), BF16),
            dma((16,)),
            dma((16,)),
            dma((8,)),
            dma((8, 2)),
            dma((8,)),
            dma((8,)),
            dma((4,)),
            dma((4,)),
            dma((4,)),
            dma((4,)),
        ],
        compiler_params=pltpu.CompilerParams(
            vmem_limit_bytes=VMEM_LIMIT, collective_id=0, has_side_effects=True
        ),
        name="outer_product",
    )(
        left.reshape(2 * FACTOR, SEQS),
        right.reshape(2 * FACTOR, SEQS),
        updated.reshape(2 * SEQS, 256),
        outer_out,
    )

    rows = jnp.transpose(gathered.reshape(4, 2, 2, 256, 256), (3, 2, 0, 1, 4))
    updated_alignment = rows.reshape(SEQS, 8, 256)

    mask_rows = lax.dynamic_slice_in_dim(align_mask, dap * 8, 8, 1).astype(BF16)
    mask_cols = lax.dynamic_slice_in_dim(align_mask, branch * 128, 128, 1).astype(BF16)
    counts = jnp.einsum("si,sj->ij", mask_rows, mask_cols, preferred_element_type=F32)
    res_float = residue_mask.astype(F32)
    live_rows = lax.dynamic_slice_in_dim(res_float, dap * 8, 8, 0)
    live_cols = lax.dynamic_slice_in_dim(res_float, branch * 128, 128, 0)
    factor = live_rows[:, None] * live_cols[None, :] / (counts + count_eps)
    update = jnp.transpose(pairs.reshape(2, 2, 8, 8, 4, 128), (3, 2, 1, 0, 4, 5))
    update = update.reshape(8, 128, 128).astype(F32)
    pair_out = (pair_rep.astype(F32) + update * factor[:, :, None]).astype(BF16)
    return (updated_alignment, pair_out)


def solution(mesh):
    placed = (
        P("dap", None, None),
        P("dap", "branch", None),
        P(),
        P(),
        P(),
        P(None, None, "branch"),
        P(),
        P(None, None, "branch"),
        P(),
        P(),
        P(),
    )
    return jax.shard_map(
        per_device,
        mesh=mesh,
        in_specs=placed,
        out_specs=(P(None, "dap", None), P("dap", "branch", None)),
        check_vma=False,
    )
```

```python
import functools
import math

import jax
import jax.numpy as jnp
from jax import lax
from jax.experimental import pallas as pl
from jax.experimental.pallas import tpu as pltpu
from jax.sharding import PartitionSpec as P

HEADS = 8
HEAD = 32
FACTOR = 32
norm_eps = 1e-05
count_eps = 0.001
LOG2E = math.log2(math.e)
QUERY_SCALE = LOG2E / math.sqrt(HEAD)
F32 = jnp.float32
BF16 = jnp.bfloat16
MESH = pl.DeviceIdType.MESH
VMEM_LIMIT = 60 * 1024 * 1024
SEQS = 512
TILE = 256
NT = (((1,), (1,)), ((), ()))
TN = (((0,), (1,)), ((), ()))


def normalize(values):
    centre = jnp.mean(values, axis=-1, keepdims=True)
    centred = values - centre
    spread = jnp.mean(centred * centred, axis=-1, keepdims=True)
    return centred * lax.rsqrt(spread + norm_eps)


def dot(a, b, dims=(((1,), (0,)), ((), ()))):
    return lax.dot_general(a, b, dims, preferred_element_type=F32)


def lane_block(index):
    lanes = lax.broadcasted_iota(jnp.int32, (1, 128), 1)
    return (lanes // HEAD == index).astype(F32).astype(BF16)


def attend(q_s, k_s, g_s, rhs_s, o_s, bias_of, mask_of):
    def run(stable):
        def tile(step, extremes):
            rows = pl.ds(pl.multiple_of(step * TILE, TILE), TILE)
            q = q_s[rows, :]
            total = None
            for n in range(4):
                scores = dot(q * lane_block(n), k_s[...], NT)
                if bias_of is not None:
                    scores = scores + bias_of(step, n)
                if stable:
                    scores = jnp.where(mask_of(n) > 0.0, scores, -1e30)
                    scores = scores - jnp.max(scores, axis=1, keepdims=True)
                raised = jnp.exp2(scores).astype(BF16)
                part = dot(raised, rhs_s[n * SEQS : (n + 1) * SEQS, :])
                total = part if total is None else total + part
            sums = total[:, 128:]
            o_s[rows, :] = total[:, :128] / sums * g_s[rows, :]
            low, high = extremes
            folded = sums.reshape(TILE // 8, 8, 128)
            return jnp.minimum(low, jnp.min(folded, axis=0)), jnp.maximum(
                high, jnp.max(folded, axis=0)
            )

        start = (jnp.full((8, 128), 1.0, F32), jnp.full((8, 128), 1.0, F32))
        return lax.fori_loop(0, SEQS // TILE, tile, start)

    low, high = run(False)
    fine = jnp.logical_and(jnp.min(low) > 1e-30, jnp.max(high) < 1e30)

    @pl.when(jnp.logical_not(fine))
    def _():
        run(True)


def fill_values(rhs_s, values, mask):
    masked = values * mask
    for n in range(4):
        rhs_s[n * SEQS : (n + 1) * SEQS, :128] = masked * lane_block(n)


def fill_ones(rhs_s, mask):
    for n in range(4):
        rhs_s[n * SEQS : (n + 1) * SEQS, 128:] = mask * lane_block(n)


def place():
    branch = lax.axis_index("branch")
    dap = lax.axis_index("dap")
    return dict(
        branch=branch,
        dap=dap,
        y_hi=branch // 2,
        core=branch % 2,
        x=dap // 16,
        z=(dap // 2) % 8,
        y_lo=dap % 2,
    )


def signal(semaphore, to):
    pl.semaphore_signal(semaphore, 1, device_id=to, device_id_type=MESH)


def remote(src, dst, send_sem, recv_sem, to):
    pltpu.make_async_remote_copy(
        src, dst, send_sem, recv_sem, device_id=to, device_id_type=MESH
    ).start()


def arrived(dst, semaphore):
    pltpu.make_async_copy(dst, dst, semaphore).wait()


def bias_kernel(
    pair_ref,
    weight_ref,
    wcol_ref,
    bias_ref,
    wall_ref,
    block_s,
    p_send,
    p_recv,
    up_send,
    down_send,
    z_recv,
    w_send,
    w_recv,
):
    at = place()
    branch, dap, x, z, y_lo = at["branch"], at["dap"], at["x"], at["z"], at["y_lo"]
    barrier = pltpu.get_barrier_semaphore()

    def to_plane(slot):
        return (slot % 4, slot // 8 * 16 + z * 2 + slot // 4 % 2)

    def line(other_z):
        return (branch, x * 16 + other_z * 2 + y_lo)

    mine = x * 8 + y_lo * 4 + branch

    def greet(slot, _):
        @pl.when(slot != mine)
        def _():
            signal(barrier, to_plane(slot))

        return 0

    lax.fori_loop(0, 32, greet, 0)

    def greet_line(other_z, _):
        @pl.when(other_z != z)
        def _():
            signal(barrier, line(other_z))

        return 0

    lax.fori_loop(0, 8, greet_line, 0)

    rows, cols, width = pair_ref.shape
    values = pair_ref[...].astype(F32).reshape(rows * cols, width)
    normed = normalize(values).astype(BF16)
    res = dot(weight_ref[...], normed, TN)
    for i in range(rows):
        tile = res[:, i * cols : (i + 1) * cols].astype(BF16)
        block_s[:, :, i, :] = tile.reshape(4, 2, cols)
    pl.semaphore_wait(barrier, 31 + 7)

    def post(slot, _):
        target = bias_ref.at[z, :, x, y_lo, branch]

        @pl.when(slot != mine)
        def _():
            remote(block_s.at[slot % 4], target, p_send.at[slot], p_recv.at[mine], to_plane(slot))

        @pl.when(slot == mine)
        def _():
            pltpu.make_async_copy(block_s.at[branch], target, p_recv.at[mine]).start()

        return 0

    lax.fori_loop(0, 32, post, 0)
    across = (lax.rem(branch + 2, 4), dap)
    partner = (branch // 2 * 2 + 1 - branch % 2, dap)
    far = lax.rem(branch + 2, 4)
    remote(wcol_ref, wall_ref.at[branch], w_send.at[0], w_recv.at[0], partner)
    remote(wcol_ref, wall_ref.at[branch], w_send.at[1], w_recv.at[1], across)
    own = pltpu.make_async_copy(wcol_ref, wall_ref.at[branch], w_recv.at[3])
    own.start()

    def collect(slot, _):
        arrived(bias_ref.at[z, :, slot // 8, slot // 4 % 2, slot % 4], p_recv.at[slot])
        return 0

    lax.fori_loop(0, 32, collect, 0)

    def chunk(other_z, c):
        return bias_ref.at[other_z, c // 2, pl.ds(c % 2 * 2, 2)]

    up, down = lax.rem(z + 1, 8), lax.rem(z + 7, 8)

    def pass_up(t, c):
        source = lax.rem(z + 8 - t, 8)
        region = chunk(source, c)
        remote(region, region, up_send.at[t, c], z_recv.at[source, c], line(up))

    def pass_down(t, c):
        source = lax.rem(z + t, 8)
        region = chunk(source, c)
        remote(region, region, down_send.at[t, c], z_recv.at[source, c], line(down))

    for c in range(4):
        pass_up(0, c)
        pass_down(0, c)
    for t in range(1, 4):
        for c in range(4):
            below, above = lax.rem(z + 8 - t, 8), lax.rem(z + t, 8)
            arrived(chunk(below, c), z_recv.at[below, c])
            if t < 3 or c < 2:
                pass_up(t, c)
            arrived(chunk(above, c), z_recv.at[above, c])
            if t < 3 or c >= 2:
                pass_down(t, c)
    arrived(wall_ref.at[far], w_recv.at[1])
    remote(wall_ref.at[far], wall_ref.at[far], w_send.at[2], w_recv.at[2], partner)
    opposite = lax.rem(z + 4, 8)
    for c in range(4):
        arrived(chunk(opposite, c), z_recv.at[opposite, c])
    for t in range(4):
        for c in range(4):
            if t < 3 or c < 2:
                arrived(chunk(z, c), up_send.at[t, c])
            if t < 3 or c >= 2:
                arrived(chunk(z, c), down_send.at[t, c])

    def drain(slot, _):
        @pl.when(slot != mine)
        def _():
            arrived(block_s.at[0], p_send.at[slot])

        return 0

    lax.fori_loop(0, 32, drain, 0)
    own.wait()
    for n in range(3):
        arrived(wcol_ref, w_send.at[n])
    arrived(wcol_ref, w_recv.at[0])
    arrived(wcol_ref, w_recv.at[2])


def row_kernel(
    x_ref, w_ref, bias_ref, maskcol_ref, maskrow_ref, out_ref, q_s, k_s, g_s, rhs_s, o_s, buf, bias_s
):
    pair = pl.program_id(0)
    normed = [normalize(x_ref[p].astype(F32)).astype(BF16) for p in range(2)]
    both = jnp.concatenate(normed, axis=1)
    projected = dot(both, w_ref[...])
    q_s[...] = (projected[:, :128] * QUERY_SCALE).astype(BF16)
    k_s[...] = projected[:, 128:256].astype(BF16)
    fill_values(rhs_s, projected[:, 256:384].astype(BF16), maskcol_ref[0])
    fill_ones(rhs_s, maskcol_ref[0])
    g_s[...] = jax.nn.sigmoid(projected[:, 384:])

    @pl.when(pair == 0)
    def _():
        for x in range(4):
            for h in range(2):
                for b in range(4):
                    piece = bias_ref[:, h, x, :, b].astype(F32).reshape(128, 128)
                    bias_s[h, x * 128 : x * 128 + 128, b * 128 : b * 128 + 128] = piece * LOG2E

    def bias_of(step, n):
        return bias_s[n % 2, pl.ds(pl.multiple_of(step * TILE, TILE), TILE), :]

    attend(q_s, k_s, g_s, rhs_s, o_s, bias_of, lambda n: maskrow_ref[0, n // 2 : n // 2 + 1, :])
    for k in range(2):
        buf[pl.ds(pair * 2 + k, 256, stride=8), :] = o_s[pl.ds(k, 256, stride=2), :]

    @pl.when(pair == pl.num_programs(0) - 1)
    def _():
        out_ref[...] = buf[...].reshape(256, 8, 128).astype(BF16)


def column_kernel(
    a_ref,
    res_ref,
    wrow_ref,
    wcol_ref,
    wout_ref,
    wfac_ref,
    maskcol_ref,
    maskrow_ref,
    upd_ref,
    left_ref,
    right_ref,
    x_s,
    msa_s,
    n_s,
    q_s,
    k_s,
    g_s,
    rhs_s,
    o_s,
    heads_s,
):
    k = pl.program_id(0)

    @pl.when(k == 0)
    def _():
        pieces = [a_ref[:, b].astype(F32).reshape(SEQS, 128).astype(BF16) for b in range(4)]
        x = dot(jnp.concatenate(pieces, axis=1), wrow_ref[...])
        for j in range(4):
            x_s[j] = x[:, j * 128 : (j + 1) * 128]

    mine = [x_s[j, pl.ds(k, 256, stride=2), :] for j in range(4)]
    rows = jnp.concatenate(
        [jnp.concatenate(mine[:2], axis=1), jnp.concatenate(mine[2:], axis=1)], axis=0
    )
    msa = (rows + res_ref[0].astype(F32)).astype(BF16).astype(F32)
    msa_s[...] = msa
    n_s[...] = normalize(msa).astype(BF16)
    fill_ones(rhs_s, maskcol_ref[0])
    for group in range(2):
        lanes = slice(group * 128, group * 128 + 128)

        def project(part):
            at = part * 256 + group * 128
            return dot(n_s[...], wcol_ref[:, at : at + 128])

        q_s[...] = (project(0) * QUERY_SCALE).astype(BF16)
        k_s[...] = project(1).astype(BF16)
        fill_values(rhs_s, project(2).astype(BF16), maskcol_ref[0])
        g_s[...] = jax.nn.sigmoid(project(3))
        attend(q_s, k_s, g_s, rhs_s, o_s, None, lambda n: maskrow_ref[0])
        heads_s[:, lanes] = o_s[...].astype(BF16)
    updated = (msa_s[...] + dot(heads_s[...], wout_ref[...])).astype(BF16)
    upd_ref[0] = updated
    outer = normalize(updated.astype(F32)).astype(BF16)
    factors = dot(wfac_ref[...], outer, TN) * maskrow_ref[0]
    left_ref[0] = factors[:FACTOR].astype(BF16)
    right_ref[0] = factors[FACTOR:].astype(BF16)


def outer_kernel(
    left_ref,
    right_ref,
    upd_ref,
    weight_ref,
    gather_ref,
    pair_ref,
    l_s,
    lp_s,
    r_s,
    perm_s,
    wide_s,
    lhs_s,
    send_s,
    relay_s,
    l_send,
    l_recv,
    up_send,
    down_send,
    x_recv,
    r_send,
    r_recv,
    f_send,
    f_recv,
    u_send,
    u_recv,
    p_send,
    p_recv,
):
    at = place()
    branch, dap, y_hi, core = at["branch"], at["dap"], at["y_hi"], at["core"]
    x, z, y_lo = at["x"], at["z"], at["y_lo"]
    barrier = pltpu.get_barrier_semaphore()

    def greet(index, _):
        to = (index // 8, (index // 2) % 4 * 16 + z * 2 + index % 2)

        @pl.when(jnp.logical_or(to[0] != branch, to[1] != dap))
        def _():
            signal(barrier, to)

        return 0

    lax.fori_loop(0, 32, greet, 0)

    def greet_line(index, _):
        other_z = index // 2

        @pl.when(other_z != z)
        def _():
            signal(barrier, (y_hi * 2 + index % 2, x * 16 + other_z * 2 + y_lo))

        return 0

    lax.fori_loop(0, 16, greet_line, 0)
    pl.semaphore_wait(barrier, 31 + 14)

    def elsewhere(to):
        return jnp.logical_or(to[0] != branch, to[1] != dap)

    def send(src, dst, send_sem, recv_sem, to):
        other = elsewhere(to)

        @pl.when(other)
        def _():
            remote(src, dst, send_sem, recv_sem, to)

        @pl.when(jnp.logical_not(other))
        def _():
            pltpu.make_async_copy(src, dst, recv_sem).start()

    def sent(src, send_sem, to):
        @pl.when(elsewhere(to))
        def _():
            arrived(src, send_sem)

    def to_left(slot):
        return (slot // 2 * 2 + y_lo, x * 16 + z * 2 + slot % 2)

    def to_right(slot):
        return (branch, x * 16 + slot * 2 + y_lo)

    def to_pair(slot):
        return (x, slot * 16 + z * 2 + core)

    def x_line(other_x):
        return (branch, other_x * 16 + z * 2 + y_lo)

    def y_line(step):
        other = lax.rem(y_hi * 2 + y_lo + step, 4)
        return (other // 2 * 2 + core, x * 16 + z * 2 + other % 2)

    partner = (y_hi * 2 + 1 - core, dap)
    far = lax.rem(branch + 2, 4)
    for slot in range(4):
        send(left_ref, l_s.at[x, branch], l_send.at[slot], l_recv.at[branch], to_left(slot))
    for slot in range(8):
        send(right_ref, r_s.at[z, core], r_send.at[slot], r_recv.at[z, core], to_right(slot))

    def rows_of(way, piece):
        return pl.ds(way * 512 + piece * 256, 256)

    steps = (1, 3)
    for piece in range(2):
        for way in range(2):
            remote(
                upd_ref.at[rows_of(way, piece)],
                relay_s.at[way, piece],
                u_send.at[0, way, piece],
                u_recv.at[0, way, piece],
                y_line(steps[way]),
            )
    remote(upd_ref, gather_ref.at[branch], u_send.at[3, 0, 0], u_recv.at[3, 0, 0], partner)
    own = pltpu.make_async_copy(upd_ref, gather_ref.at[branch], u_recv.at[3, 0, 1])
    own.start()

    wide_s[...] = jnp.zeros_like(wide_s)

    def widen(c, _):
        block = weight_ref[pl.ds(pl.multiple_of(c * 32, 32), 32), :]
        for j in range(4):
            rows = pl.ds(pl.multiple_of(c * 128 + j * 32, 32), 32)
            wide_s[rows, j * 128 : (j + 1) * 128] = block
        return 0

    lax.fori_loop(0, 32, widen, 0)

    def permute(c, _):
        source = lax.broadcasted_iota(jnp.int32, (32, 1024), 1)
        wanted = lax.broadcasted_iota(jnp.int32, (32, 1024), 0) * 32 + c
        rows = pl.ds(pl.multiple_of(c * 32, 32), 32)
        perm_s[rows, :] = (source == wanted).astype(F32).astype(BF16)
        return 0

    lax.fori_loop(0, 32, permute, 0)

    above, below = lax.rem(x + 1, 4), lax.rem(x + 3, 4)

    def half(other_x, h):
        return l_s.at[other_x, pl.ds(h * 2, 2)]

    def pass_x(origin, h, send_sem, to):
        region = half(origin, h)
        remote(region, region, send_sem, x_recv.at[origin, h], x_line(to))

    for slot in range(4):
        arrived(l_s.at[x, slot], l_recv.at[slot])
    for h in range(2):
        pass_x(x, h, up_send.at[h], above)
        pass_x(x, 1 - h, down_send.at[1 - h], below)

    def relay(way, piece):
        region = relay_s.at[way, piece]
        arrived(region, u_recv.at[0, way, piece])
        to = y_line(steps[way])
        remote(
            region,
            gather_ref.at[lax.rem(to[0] + 2, 4), rows_of(way, piece)],
            u_send.at[1, way, piece],
            u_recv.at[1, way, piece],
            to,
        )

    for way in range(2):
        relay(way, 0)
    for slot in range(8):
        arrived(r_s.at[slot, core], r_recv.at[slot, core])
        remote(r_s.at[slot, core], r_s.at[slot, core], f_send.at[slot], f_recv.at[slot], partner)
    arrived(half(below, 0), x_recv.at[below, 0])
    pass_x(below, 0, up_send.at[2], above)
    arrived(half(above, 1), x_recv.at[above, 1])
    pass_x(above, 1, down_send.at[2], below)
    for way in range(2):
        relay(way, 1)
    arrived(half(below, 1), x_recv.at[below, 1])
    arrived(half(above, 0), x_recv.at[above, 0])
    opposite = lax.rem(x + 2, 4)
    for h in range(2):
        arrived(half(opposite, h), x_recv.at[opposite, h])
    lefts = l_s[...].reshape(1024, SEQS)
    lp_s[...] = dot(perm_s[...], lefts).astype(BF16)
    for slot in range(8):
        arrived(r_s.at[slot, 1 - core], f_recv.at[slot])

    def contract(jc, _):
        rights = r_s[pl.ds(jc * 2, 2)].reshape(256, SEQS)
        block = dot(lp_s[...], rights, NT)
        for c in range(32):
            for xi in range(4):
                rows = slice(c * 32 + xi * 8, c * 32 + xi * 8 + 8)
                tile = jnp.concatenate([block[rows, :128], block[rows, 128:]], axis=0)
                lhs_s[xi, jc, :, c * 128 : c * 128 + 128] = tile.astype(BF16)
        return 0

    lax.fori_loop(0, 4, contract, 0)
    update = dot(lhs_s[...].reshape(256, 4096), wide_s[...])
    send_s[...] = update.reshape(4, 8, 8, 512).astype(BF16)
    for slot in range(4):
        send(
            send_s.at[slot],
            pair_ref.at[y_hi * 2 + y_lo],
            p_send.at[slot],
            p_recv.at[y_hi * 2 + y_lo],
            to_pair(slot),
        )
    for piece in range(2):
        for way in range(2):
            region = gather_ref.at[far, rows_of(way, piece)]
            arrived(region, u_recv.at[1, way, piece])
            remote(region, region, u_send.at[2, way, piece], u_recv.at[2, way, piece], partner)
    for slot in range(8):
        sent(right_ref, r_send.at[slot], to_right(slot))
        arrived(right_ref, f_send.at[slot])
    for slot in range(4):
        sent(left_ref, l_send.at[slot], to_left(slot))
        sent(send_s.at[slot], p_send.at[slot], to_pair(slot))
    for n in range(3):
        arrived(half(x, 0), up_send.at[n])
        arrived(half(x, 0), down_send.at[n])
    for way in range(2):
        for piece in range(2):
            for stage in range(3):
                arrived(relay_s.at[way, piece], u_send.at[stage, way, piece])
            arrived(relay_s.at[way, piece], u_recv.at[2, way, piece])
    arrived(upd_ref, u_send.at[3, 0, 0])
    arrived(upd_ref, u_recv.at[3, 0, 0])
    own.wait()
    for slot in range(4):
        arrived(pair_ref.at[slot], p_recv.at[slot])


def whole(shape):
    return pl.BlockSpec(shape, lambda *_: (0,) * len(shape))


def per_device(
    alignment,
    pair_rep,
    align_mask,
    residue_mask,
    bias_weight,
    row_proj_weight,
    row_out_weight,
    column_proj_weight,
    column_out_weight,
    outer_factor_weight,
    outer_out,
):
    branch = lax.axis_index("branch")
    dap = lax.axis_index("dap")
    vmem = pltpu.VMEM
    params = pltpu.CompilerParams(vmem_limit_bytes=VMEM_LIMIT)

    dma = pltpu.SemaphoreType.DMA
    wcol_mine = jnp.transpose(column_proj_weight, (1, 0, 2)).reshape(256, 256)
    bias, wcol = pl.pallas_call(
        bias_kernel,
        in_specs=[pl.BlockSpec(memory_space=vmem)] * 3,
        out_specs=(pl.BlockSpec(memory_space=vmem),) * 2,
        out_shape=(
            jax.ShapeDtypeStruct((8, 2, 4, 2, 4, 8, 128), BF16),
            jax.ShapeDtypeStruct((4, 256, 256), BF16),
        ),
        scratch_shapes=[
            vmem((4, 2, 8, 128), BF16),
            dma((32,)),
            dma((32,)),
            dma((4, 4)),
            dma((4, 4)),
            dma((8, 4)),
            dma((3,)),
            dma((4,)),
        ],
        compiler_params=pltpu.CompilerParams(
            vmem_limit_bytes=VMEM_LIMIT, collective_id=1, has_side_effects=True
        ),
        name="pair_bias",
    )(pair_rep, bias_weight, wcol_mine)
    wcol = jnp.transpose(wcol.reshape(4, 256, 4, 64), (1, 2, 0, 3)).reshape(256, 1024)

    by_owner = alignment.reshape(8, 64, 4, 2, 256)
    mine = lax.dynamic_slice_in_dim(by_owner, branch, 1, 2)[:, :, 0]
    mine = jnp.transpose(mine.reshape(4, 2, 64, 2, 256), (2, 3, 1, 0, 4))
    moved = lax.all_to_all(mine, "dap", split_axis=0, concat_axis=0, tiled=True)
    residual = jnp.transpose(moved, (1, 2, 0, 3, 4)).reshape(2, SEQS, 256)

    half = jnp.transpose(row_proj_weight, (1, 0, 2))
    none = jnp.zeros_like(half)
    wrow = jnp.concatenate(
        [jnp.concatenate([half, none], axis=2), jnp.concatenate([none, half], axis=2)], axis=0
    ).reshape(512, 512)
    out_half = row_out_weight.reshape(4, 64, 256)
    out_none = jnp.zeros_like(out_half)
    wrow_out = jnp.concatenate(
        [
            jnp.concatenate([out_half, out_none], axis=2),
            jnp.concatenate([out_none, out_half], axis=2),
        ],
        axis=1,
    ).reshape(512, 512)

    seq_mask = lax.dynamic_slice_in_dim(align_mask, dap * 8, 8, 0).astype(F32)
    row_mask = seq_mask.reshape(4, 2, SEQS)
    row_maskcol = jnp.repeat(jnp.transpose(row_mask, (0, 2, 1)), 64, axis=2).astype(BF16)
    res_mask = lax.dynamic_slice_in_dim(align_mask, dap * 8 + branch * 2, 2, 1).astype(F32)
    res_mask = jnp.transpose(res_mask.reshape(256, 2, 2), (2, 1, 0)).reshape(2, 1, SEQS)
    col_maskcol = jnp.broadcast_to(res_mask.reshape(2, SEQS, 1), (2, SEQS, 128)).astype(BF16)

    attend_scratch = [
        vmem((SEQS, 128), BF16),
        vmem((SEQS, 128), BF16),
        vmem((SEQS, 128), F32),
        vmem((4 * SEQS, 256), BF16),
        vmem((SEQS, 128), F32),
    ]
    heads = pl.pallas_call(
        row_kernel,
        grid=(4,),
        in_specs=[
            pl.BlockSpec((2, SEQS, 256), lambda i: (i, 0, 0)),
            whole((512, 512)),
            whole((8, 2, 4, 2, 4, 8, 128)),
            pl.BlockSpec((1, SEQS, 128), lambda i: (i, 0, 0)),
            pl.BlockSpec((1, 2, SEQS), lambda i: (i, 0, 0)),
        ],
        out_specs=whole((256, 8, 128)),
        out_shape=jax.ShapeDtypeStruct((256, 8, 128), BF16),
        scratch_shapes=attend_scratch + [vmem((2048, 128), F32), vmem((2, SEQS, SEQS), F32)],
        compiler_params=params,
        name="row_attention",
    )(alignment, wrow, bias, row_maskcol, row_mask)
    got = lax.all_to_all(heads, ("dap", "branch"), split_axis=0, concat_axis=0, tiled=True)

    updated, left, right = pl.pallas_call(
        column_kernel,
        grid=(2,),
        in_specs=[
            whole((64, 4, 8, 128)),
            pl.BlockSpec((1, SEQS, 256), lambda i: (i, 0, 0)),
            whole((512, 512)),
            whole((256, 1024)),
            whole((256, 256)),
            whole((256, 64)),
            pl.BlockSpec((1, SEQS, 128), lambda i: (i, 0, 0)),
            pl.BlockSpec((1, 1, SEQS), lambda i: (i, 0, 0)),
        ],
        out_specs=(
            pl.BlockSpec((1, SEQS, 256), lambda i: (i, 0, 0)),
            pl.BlockSpec((1, FACTOR, SEQS), lambda i: (i, 0, 0)),
            pl.BlockSpec((1, FACTOR, SEQS), lambda i: (i, 0, 0)),
        ),
        out_shape=(
            jax.ShapeDtypeStruct((2, SEQS, 256), BF16),
            jax.ShapeDtypeStruct((2, FACTOR, SEQS), BF16),
            jax.ShapeDtypeStruct((2, FACTOR, SEQS), BF16),
        ),
        scratch_shapes=[
            vmem((4, SEQS, 128), F32),
            vmem((SEQS, 256), F32),
            vmem((SEQS, 256), BF16),
        ]
        + attend_scratch
        + [vmem((SEQS, 256), BF16)],
        compiler_params=params,
        name="column_attention",
    )(
        got.reshape(64, 4, 8, 128),
        residual,
        wrow_out,
        wcol,
        column_out_weight,
        outer_factor_weight,
        col_maskcol,
        res_mask,
    )

    gathered, pairs = pl.pallas_call(
        outer_kernel,
        in_specs=[pl.BlockSpec(memory_space=vmem)] * 4,
        out_specs=(pl.BlockSpec(memory_space=vmem),) * 2,
        out_shape=(
            jax.ShapeDtypeStruct((4, 2 * SEQS, 256), BF16),
            jax.ShapeDtypeStruct((4, 8, 8, 512), BF16),
        ),
        scratch_shapes=[
            vmem((4, 4, 64, SEQS), BF16),
            vmem((1024, SEQS), BF16),
            vmem((8, 2, 64, SEQS), BF16),
            vmem((1024, 1024), BF16),
            vmem((4096, 512), BF16),
            vmem((4, 4, 16, 4096), BF16),
            vmem((4, 8, 8, 512), BF16),
            vmem((2, 2, 256, 256), BF16),
            dma((4,)),
            dma((4,)),
            dma((3,)),
            dma((3,)),
            dma((4, 2)),
            dma((8,)),
            dma((8, 2)),
            dma((8,)),
            dma((8,)),
            dma((4, 2, 2)),
            dma((4, 2, 2)),
            dma((4,)),
            dma((4,)),
        ],
        compiler_params=pltpu.CompilerParams(
            vmem_limit_bytes=VMEM_LIMIT, collective_id=0, has_side_effects=True
        ),
        name="outer_product",
    )(
        left.reshape(2 * FACTOR, SEQS),
        right.reshape(2 * FACTOR, SEQS),
        updated.reshape(2 * SEQS, 256),
        outer_out,
    )

    rows = jnp.transpose(gathered.reshape(4, 2, 2, 256, 256), (3, 2, 0, 1, 4))
    updated_alignment = rows.reshape(SEQS, 8, 256)

    mask_rows = lax.dynamic_slice_in_dim(align_mask, dap * 8, 8, 1).astype(BF16)
    mask_cols = lax.dynamic_slice_in_dim(align_mask, branch * 128, 128, 1).astype(BF16)
    counts = jnp.einsum("si,sj->ij", mask_rows, mask_cols, preferred_element_type=F32)
    res_float = residue_mask.astype(F32)
    live_rows = lax.dynamic_slice_in_dim(res_float, dap * 8, 8, 0)
    live_cols = lax.dynamic_slice_in_dim(res_float, branch * 128, 128, 0)
    factor = live_rows[:, None] * live_cols[None, :] / (counts + count_eps)
    update = jnp.transpose(pairs.reshape(2, 2, 8, 8, 4, 128), (3, 2, 1, 0, 4, 5))
    update = update.reshape(8, 128, 128).astype(F32)
    pair_out = (pair_rep.astype(F32) + update * factor[:, :, None]).astype(BF16)
    return (updated_alignment, pair_out)


def solution(mesh):
    placed = (
        P("dap", None, None),
        P("dap", "branch", None),
        P(),
        P(),
        P(),
        P(None, None, "branch"),
        P(),
        P(None, None, "branch"),
        P(),
        P(),
        P(),
    )
    return jax.shard_map(
        per_device,
        mesh=mesh,
        in_specs=placed,
        out_specs=(P(None, "dap", None), P("dap", "branch", None)),
        check_vma=False,
    )
```

```python
import functools
import math

import jax
import jax.numpy as jnp
from jax import lax
from jax.experimental import pallas as pl
from jax.experimental.pallas import tpu as pltpu
from jax.sharding import PartitionSpec as P

HEADS = 8
HEAD = 32
FACTOR = 32
norm_eps = 1e-05
count_eps = 0.001
LOG2E = math.log2(math.e)
QUERY_SCALE = LOG2E / math.sqrt(HEAD)
F32 = jnp.float32
BF16 = jnp.bfloat16
MESH = pl.DeviceIdType.MESH
VMEM_LIMIT = 60 * 1024 * 1024
SEQS = 512
TILE = 256
NT = (((1,), (1,)), ((), ()))
TN = (((0,), (1,)), ((), ()))


def normalize(values):
    centre = jnp.mean(values, axis=-1, keepdims=True)
    centred = values - centre
    spread = jnp.mean(centred * centred, axis=-1, keepdims=True)
    return centred * lax.rsqrt(spread + norm_eps)


def dot(a, b, dims=(((1,), (0,)), ((), ()))):
    return lax.dot_general(a, b, dims, preferred_element_type=F32)


def lane_block(index):
    lanes = lax.broadcasted_iota(jnp.int32, (1, 128), 1)
    return (lanes // HEAD == index).astype(F32).astype(BF16)


def attend(q_s, k_s, g_s, rhs_s, o_s, bias_of, mask_of):
    def run(stable):
        def tile(step, extremes):
            rows = pl.ds(pl.multiple_of(step * TILE, TILE), TILE)
            q = q_s[rows, :]
            total = None
            for n in range(4):
                scores = dot(q * lane_block(n), k_s[...], NT)
                if bias_of is not None:
                    scores = scores + bias_of(step, n)
                if stable:
                    scores = jnp.where(mask_of(n) > 0.0, scores, -1e30)
                    scores = scores - jnp.max(scores, axis=1, keepdims=True)
                raised = jnp.exp2(scores).astype(BF16)
                part = dot(raised, rhs_s[n * SEQS : (n + 1) * SEQS, :])
                total = part if total is None else total + part
            sums = total[:, 128:]
            o_s[rows, :] = total[:, :128] / sums * g_s[rows, :]
            low, high = extremes
            folded = sums.reshape(TILE // 8, 8, 128)
            return jnp.minimum(low, jnp.min(folded, axis=0)), jnp.maximum(
                high, jnp.max(folded, axis=0)
            )

        start = (jnp.full((8, 128), 1.0, F32), jnp.full((8, 128), 1.0, F32))
        return lax.fori_loop(0, SEQS // TILE, tile, start)

    low, high = run(False)
    fine = jnp.logical_and(jnp.min(low) > 1e-30, jnp.max(high) < 1e30)

    @pl.when(jnp.logical_not(fine))
    def _():
        run(True)


def fill_values(rhs_s, values, mask):
    masked = values * mask
    for n in range(4):
        rhs_s[n * SEQS : (n + 1) * SEQS, :128] = masked * lane_block(n)


def fill_ones(rhs_s, mask):
    for n in range(4):
        rhs_s[n * SEQS : (n + 1) * SEQS, 128:] = mask * lane_block(n)


def place():
    branch = lax.axis_index("branch")
    dap = lax.axis_index("dap")
    return dict(
        branch=branch,
        dap=dap,
        y_hi=branch // 2,
        core=branch % 2,
        x=dap // 16,
        z=(dap // 2) % 8,
        y_lo=dap % 2,
    )


def signal(semaphore, to):
    pl.semaphore_signal(semaphore, 1, device_id=to, device_id_type=MESH)


def remote(src, dst, send_sem, recv_sem, to):
    pltpu.make_async_remote_copy(
        src, dst, send_sem, recv_sem, device_id=to, device_id_type=MESH
    ).start()


def arrived(dst, semaphore):
    pltpu.make_async_copy(dst, dst, semaphore).wait()


def attend_tile(q, k, rhs_s, lane_masks, extra):
    total = None
    for n in range(4):
        scores = dot(q * lane_masks[n], k, NT) + extra(n)
        scores = scores - jnp.max(scores, axis=1, keepdims=True)
        raised = jnp.exp2(scores).astype(BF16)
        part = dot(raised, rhs_s[n * SEQS : (n + 1) * SEQS, :])
        total = part if total is None else total + part
    return total[:, :128] / total[:, 128:]


def front_kernel(
    pair_ref,
    weight_ref,
    wcol_ref,
    x_ref,
    wrow_ref,
    off_ref,
    heads_ref,
    resid_ref,
    wall_ref,
    block_s,
    bias_s,
    wide_s,
    q_s,
    k_s,
    g_s,
    rhs_s,
    x_s,
    res_s,
    resb_s,
    o_s,
    buf_s,
    out_s,
    p_send,
    p_recv,
    up_send,
    down_send,
    z_recv,
    w_send,
    w_recv,
    res_send,
    res_recv,
    out_send,
    out_recv,
):
    at = place()
    branch, dap, x, z, y_lo = at["branch"], at["dap"], at["x"], at["z"], at["y_lo"]
    barrier = pltpu.get_barrier_semaphore()
    me = dap * 4 + branch

    def device(slot):
        return (slot % 4, slot // 4)

    def greet(slot, _):
        @pl.when(slot != me)
        def _():
            signal(barrier, device(slot))

        return 0

    lax.fori_loop(0, 256, greet, 0)

    def to_plane(slot):
        return (slot % 4, slot // 8 * 16 + z * 2 + slot // 4 % 2)

    def line(other_z):
        return (branch, x * 16 + other_z * 2 + y_lo)

    mine = x * 8 + y_lo * 4 + branch
    rows, cols, width = pair_ref.shape
    values = pair_ref[...].astype(F32).reshape(rows * cols, width)
    normed = normalize(values).astype(BF16)
    res = dot(weight_ref[...], normed, TN)
    for i in range(rows):
        tile = res[:, i * cols : (i + 1) * cols].astype(BF16)
        block_s[:, :, i, :] = tile.reshape(4, 2, cols)
    pl.semaphore_wait(barrier, 255)

    def post(slot, _):
        target = bias_s.at[z, :, x, y_lo, branch]

        @pl.when(slot != mine)
        def _():
            remote(block_s.at[slot % 4], target, p_send.at[slot], p_recv.at[mine], to_plane(slot))

        @pl.when(slot == mine)
        def _():
            pltpu.make_async_copy(block_s.at[branch], target, p_recv.at[mine]).start()

        return 0

    lax.fori_loop(0, 32, post, 0)
    across = (lax.rem(branch + 2, 4), dap)
    partner = (branch // 2 * 2 + 1 - branch % 2, dap)
    far = lax.rem(branch + 2, 4)
    remote(wcol_ref, wall_ref.at[branch], w_send.at[0], w_recv.at[0], partner)
    remote(wcol_ref, wall_ref.at[branch], w_send.at[1], w_recv.at[1], across)
    own = pltpu.make_async_copy(wcol_ref, wall_ref.at[branch], w_recv.at[3])
    own.start()

    def project(sp, _):
        normed = []
        for p in range(2):
            value = x_ref[sp * 2 + p].astype(F32)
            for side in range(2):
                x_s[side] = value[:, side * 128 : side * 128 + 128]
                for k in range(2):
                    res_s[side, pl.ds(sp * 4 + k * 2 + p, 64, stride=16), :] = x_s[
                        side, pl.ds(branch * 2 + k, 64, stride=8), :
                    ]
            normed.append(normalize(value).astype(BF16))
        both = jnp.concatenate(normed, axis=1)
        projected = dot(both, wrow_ref[...])
        q_s[sp] = (projected[:, :128] * QUERY_SCALE).astype(BF16)
        k_s[sp] = projected[:, 128:256].astype(BF16)
        values = projected[:, 256:384].astype(BF16)
        g_s[sp] = jax.nn.sigmoid(projected[:, 384:])
        for n in range(4):
            rhs_s[sp, n * SEQS : (n + 1) * SEQS, :128] = values * lane_block(n)
            rhs_s[sp, n * SEQS : (n + 1) * SEQS, 128:] = jnp.broadcast_to(
                lane_block(n), (SEQS, 128)
            )
        return 0

    lax.fori_loop(0, 4, project, 0)
    for side in range(2):
        resb_s[:, :, side * 128 : side * 128 + 128] = (
            res_s[side].reshape(64, 16, 128).astype(BF16)
        )

    def collect(slot, _):
        arrived(bias_s.at[z, :, slot // 8, slot // 4 % 2, slot % 4], p_recv.at[slot])
        return 0

    lax.fori_loop(0, 32, collect, 0)

    def chunk(other_z, c):
        return bias_s.at[other_z, c // 2, pl.ds(c % 2 * 2, 2)]

    up, down = lax.rem(z + 1, 8), lax.rem(z + 7, 8)

    def pass_up(t, c):
        source = lax.rem(z + 8 - t, 8)
        region = chunk(source, c)
        remote(region, region, up_send.at[t, c], z_recv.at[source, c], line(up))

    def pass_down(t, c):
        source = lax.rem(z + t, 8)
        region = chunk(source, c)
        remote(region, region, down_send.at[t, c], z_recv.at[source, c], line(down))

    for c in range(4):
        pass_up(0, c)
        pass_down(0, c)
    for t in range(1, 4):
        for c in range(4):
            below, above = lax.rem(z + 8 - t, 8), lax.rem(z + t, 8)
            arrived(chunk(below, c), z_recv.at[below, c])
            if t < 3 or c < 2:
                pass_up(t, c)
            arrived(chunk(above, c), z_recv.at[above, c])
            if t < 3 or c >= 2:
                pass_down(t, c)
    arrived(wall_ref.at[far], w_recv.at[1])
    remote(wall_ref.at[far], wall_ref.at[far], w_send.at[2], w_recv.at[2], partner)

    def post_res(slot, _):
        target = resid_ref.at[dap]

        @pl.when(slot != dap)
        def _():
            remote(resb_s.at[slot], target, res_send, res_recv, (branch, slot))

        @pl.when(slot == dap)
        def _():
            pltpu.make_async_copy(resb_s.at[slot], target, res_recv).start()

        return 0

    lax.fori_loop(0, 64, post_res, 0)
    opposite = lax.rem(z + 4, 8)
    for c in range(4):
        arrived(chunk(opposite, c), z_recv.at[opposite, c])

    for xx in range(4):
        for h in range(2):
            for b in range(4):
                piece = bias_s[:, h, xx, :, b].astype(F32).reshape(128, 128)
                wide_s[h, xx * 128 : xx * 128 + 128, b * 128 : b * 128 + 128] = piece * LOG2E

    def step(t, _):
        other_x = lax.rem(x + t, 4)
        span = pl.ds(pl.multiple_of(other_x * 128, 128), 128)
        masks = [lane_block(n) for n in range(4)]

        def some(u, _):
            for v in range(2):
                sp = u * 2 + v

                def extra(n):
                    return wide_s[n % 2, span, :] + off_ref[sp, pl.ds(n // 2, 1), :]

                out = attend_tile(q_s[sp, span, :], k_s[sp], rhs_s.at[sp], masks, extra)
                o_s[v] = out * g_s[sp, span, :]
                for k in range(2):
                    buf_s[pl.ds(sp * 2 + k, 64, stride=8), :] = o_s[v, pl.ds(k, 64, stride=2), :]
            return 0

        lax.fori_loop(0, 2, some, 0)
        base = other_x * 64
        out_s[pl.ds(base, 64)] = buf_s[...].reshape(64, 8, 128).astype(BF16)

        def post_out(j, _):
            slot = base + j

            @pl.when(slot != me)
            def _():
                remote(out_s.at[slot], heads_ref.at[me], out_send, out_recv, device(slot))

            @pl.when(slot == me)
            def _():
                pltpu.make_async_copy(out_s.at[slot], heads_ref.at[me], out_recv).start()

            return 0

        lax.fori_loop(0, 64, post_out, 0)
        return 0

    lax.fori_loop(0, 4, step, 0)

    for t in range(4):
        for c in range(4):
            if t < 3 or c < 2:
                arrived(chunk(z, c), up_send.at[t, c])
            if t < 3 or c >= 2:
                arrived(chunk(z, c), down_send.at[t, c])

    def drain(slot, _):
        @pl.when(slot != mine)
        def _():
            arrived(block_s.at[0], p_send.at[slot])

        return 0

    lax.fori_loop(0, 32, drain, 0)
    own.wait()
    for n in range(3):
        arrived(wcol_ref, w_send.at[n])
    arrived(wcol_ref, w_recv.at[0])
    arrived(wcol_ref, w_recv.at[2])
    arrived(resb_s.at[pl.ds(0, 63)], res_send)
    arrived(resid_ref, res_recv)
    arrived(out_s.at[pl.ds(0, 255)], out_send)
    arrived(heads_ref, out_recv)


def column_kernel(
    a_ref,
    res_ref,
    wrow_ref,
    wcol_ref,
    wout_ref,
    wfac_ref,
    maskcol_ref,
    maskrow_ref,
    upd_ref,
    left_ref,
    right_ref,
    x_s,
    res_s,
    msa_s,
    n_s,
    q_s,
    k_s,
    g_s,
    rhs_s,
    o_s,
    heads_s,
):
    k = pl.program_id(0)

    @pl.when(k == 0)
    def _():
        pieces = [a_ref[:, b].astype(F32).reshape(SEQS, 128).astype(BF16) for b in range(4)]
        x = dot(jnp.concatenate(pieces, axis=1), wrow_ref[...])
        for j in range(4):
            x_s[j] = x[:, j * 128 : (j + 1) * 128]
        for side in range(2):
            block = res_ref[:, :, side * 128 : side * 128 + 128].astype(F32)
            res_s[side] = block.reshape(1024, 128)

    mine = [x_s[j, pl.ds(k, 256, stride=2), :] for j in range(4)]
    rows = jnp.concatenate(
        [jnp.concatenate(mine[:2], axis=1), jnp.concatenate(mine[2:], axis=1)], axis=0
    )
    base = jnp.concatenate(
        [
            jnp.concatenate(
                [res_s[side, pl.ds(k * 2 + p, 256, stride=4), :] for side in range(2)], axis=1
            )
            for p in range(2)
        ],
        axis=0,
    )
    msa = (rows + base).astype(BF16).astype(F32)
    msa_s[...] = msa
    n_s[...] = normalize(msa).astype(BF16)
    fill_ones(rhs_s, maskcol_ref[0])
    for group in range(2):
        lanes = slice(group * 128, group * 128 + 128)

        def project(part):
            at = part * 256 + group * 128
            return dot(n_s[...], wcol_ref[:, at : at + 128])

        q_s[...] = (project(0) * QUERY_SCALE).astype(BF16)
        k_s[...] = project(1).astype(BF16)
        fill_values(rhs_s, project(2).astype(BF16), maskcol_ref[0])
        g_s[...] = jax.nn.sigmoid(project(3))
        attend(q_s, k_s, g_s, rhs_s, o_s, None, lambda n: maskrow_ref[0])
        heads_s[:, lanes] = o_s[...].astype(BF16)
    updated = (msa_s[...] + dot(heads_s[...], wout_ref[...])).astype(BF16)
    upd_ref[0] = updated
    outer = normalize(updated.astype(F32)).astype(BF16)
    factors = dot(wfac_ref[...], outer, TN) * maskrow_ref[0]
    left_ref[0] = factors[:FACTOR].astype(BF16)
    right_ref[0] = factors[FACTOR:].astype(BF16)


def outer_kernel(
    left_ref,
    right_ref,
    upd_ref,
    weight_ref,
    gather_ref,
    pair_ref,
    l_s,
    lp_s,
    r_s,
    perm_s,
    wide_s,
    lhs_s,
    send_s,
    relay_s,
    l_send,
    l_recv,
    up_send,
    down_send,
    x_recv,
    r_send,
    r_recv,
    f_send,
    f_recv,
    u_send,
    u_recv,
    p_send,
    p_recv,
):
    at = place()
    branch, dap, y_hi, core = at["branch"], at["dap"], at["y_hi"], at["core"]
    x, z, y_lo = at["x"], at["z"], at["y_lo"]
    barrier = pltpu.get_barrier_semaphore()

    def greet(index, _):
        to = (index // 8, (index // 2) % 4 * 16 + z * 2 + index % 2)

        @pl.when(jnp.logical_or(to[0] != branch, to[1] != dap))
        def _():
            signal(barrier, to)

        return 0

    lax.fori_loop(0, 32, greet, 0)

    def greet_line(index, _):
        other_z = index // 2

        @pl.when(other_z != z)
        def _():
            signal(barrier, (y_hi * 2 + index % 2, x * 16 + other_z * 2 + y_lo))

        return 0

    lax.fori_loop(0, 16, greet_line, 0)
    pl.semaphore_wait(barrier, 31 + 14)

    def elsewhere(to):
        return jnp.logical_or(to[0] != branch, to[1] != dap)

    def send(src, dst, send_sem, recv_sem, to):
        other = elsewhere(to)

        @pl.when(other)
        def _():
            remote(src, dst, send_sem, recv_sem, to)

        @pl.when(jnp.logical_not(other))
        def _():
            pltpu.make_async_copy(src, dst, recv_sem).start()

    def sent(src, send_sem, to):
        @pl.when(elsewhere(to))
        def _():
            arrived(src, send_sem)

    def to_left(slot):
        return (slot // 2 * 2 + y_lo, x * 16 + z * 2 + slot % 2)

    def to_right(slot):
        return (branch, x * 16 + slot * 2 + y_lo)

    def to_pair(slot):
        return (x, slot * 16 + z * 2 + core)

    def x_line(other_x):
        return (branch, other_x * 16 + z * 2 + y_lo)

    def y_line(step):
        other = lax.rem(y_hi * 2 + y_lo + step, 4)
        return (other // 2 * 2 + core, x * 16 + z * 2 + other % 2)

    partner = (y_hi * 2 + 1 - core, dap)
    far = lax.rem(branch + 2, 4)
    for slot in range(4):
        send(left_ref, l_s.at[x, branch], l_send.at[slot], l_recv.at[branch], to_left(slot))
    for slot in range(8):
        send(right_ref, r_s.at[z, core], r_send.at[slot], r_recv.at[z, core], to_right(slot))

    def rows_of(way, piece):
        return pl.ds(way * 512 + piece * 256, 256)

    steps = (1, 3)
    for piece in range(2):
        for way in range(2):
            remote(
                upd_ref.at[rows_of(way, piece)],
                relay_s.at[way, piece],
                u_send.at[0, way, piece],
                u_recv.at[0, way, piece],
                y_line(steps[way]),
            )
    remote(upd_ref, gather_ref.at[branch], u_send.at[3, 0, 0], u_recv.at[3, 0, 0], partner)
    own = pltpu.make_async_copy(upd_ref, gather_ref.at[branch], u_recv.at[3, 0, 1])
    own.start()

    wide_s[...] = jnp.zeros_like(wide_s)

    def widen(c, _):
        block = weight_ref[pl.ds(pl.multiple_of(c * 32, 32), 32), :]
        for j in range(4):
            rows = pl.ds(pl.multiple_of(c * 128 + j * 32, 32), 32)
            wide_s[rows, j * 128 : (j + 1) * 128] = block
        return 0

    lax.fori_loop(0, 32, widen, 0)

    def permute(c, _):
        source = lax.broadcasted_iota(jnp.int32, (32, 1024), 1)
        wanted = lax.broadcasted_iota(jnp.int32, (32, 1024), 0) * 32 + c
        rows = pl.ds(pl.multiple_of(c * 32, 32), 32)
        perm_s[rows, :] = (source == wanted).astype(F32).astype(BF16)
        return 0

    lax.fori_loop(0, 32, permute, 0)

    above, below = lax.rem(x + 1, 4), lax.rem(x + 3, 4)

    def half(other_x, h):
        return l_s.at[other_x, pl.ds(h * 2, 2)]

    def pass_x(origin, h, send_sem, to):
        region = half(origin, h)
        remote(region, region, send_sem, x_recv.at[origin, h], x_line(to))

    for slot in range(4):
        arrived(l_s.at[x, slot], l_recv.at[slot])
    for h in range(2):
        pass_x(x, h, up_send.at[h], above)
        pass_x(x, 1 - h, down_send.at[1 - h], below)

    def relay(way, piece):
        region = relay_s.at[way, piece]
        arrived(region, u_recv.at[0, way, piece])
        to = y_line(steps[way])
        remote(
            region,
            gather_ref.at[lax.rem(to[0] + 2, 4), rows_of(way, piece)],
            u_send.at[1, way, piece],
            u_recv.at[1, way, piece],
            to,
        )

    for way in range(2):
        relay(way, 0)
    for slot in range(8):
        arrived(r_s.at[slot, core], r_recv.at[slot, core])
        remote(r_s.at[slot, core], r_s.at[slot, core], f_send.at[slot], f_recv.at[slot], partner)
    arrived(half(below, 0), x_recv.at[below, 0])
    pass_x(below, 0, up_send.at[2], above)
    arrived(half(above, 1), x_recv.at[above, 1])
    pass_x(above, 1, down_send.at[2], below)
    for way in range(2):
        relay(way, 1)
    arrived(half(below, 1), x_recv.at[below, 1])
    arrived(half(above, 0), x_recv.at[above, 0])
    opposite = lax.rem(x + 2, 4)
    for h in range(2):
        arrived(half(opposite, h), x_recv.at[opposite, h])
    lefts = l_s[...].reshape(1024, SEQS)
    lp_s[...] = dot(perm_s[...], lefts).astype(BF16)
    for slot in range(8):
        arrived(r_s.at[slot, 1 - core], f_recv.at[slot])

    def contract(jc, _):
        rights = r_s[pl.ds(jc * 2, 2)].reshape(256, SEQS)
        block = dot(lp_s[...], rights, NT)
        for c in range(32):
            for xi in range(4):
                rows = slice(c * 32 + xi * 8, c * 32 + xi * 8 + 8)
                tile = jnp.concatenate([block[rows, :128], block[rows, 128:]], axis=0)
                lhs_s[xi, jc, :, c * 128 : c * 128 + 128] = tile.astype(BF16)
        return 0

    lax.fori_loop(0, 4, contract, 0)
    update = dot(lhs_s[...].reshape(256, 4096), wide_s[...])
    send_s[...] = update.reshape(4, 8, 8, 512).astype(BF16)
    for slot in range(4):
        send(
            send_s.at[slot],
            pair_ref.at[y_hi * 2 + y_lo],
            p_send.at[slot],
            p_recv.at[y_hi * 2 + y_lo],
            to_pair(slot),
        )
    for piece in range(2):
        for way in range(2):
            region = gather_ref.at[far, rows_of(way, piece)]
            arrived(region, u_recv.at[1, way, piece])
            remote(region, region, u_send.at[2, way, piece], u_recv.at[2, way, piece], partner)
    for slot in range(8):
        sent(right_ref, r_send.at[slot], to_right(slot))
        arrived(right_ref, f_send.at[slot])
    for slot in range(4):
        sent(left_ref, l_send.at[slot], to_left(slot))
        sent(send_s.at[slot], p_send.at[slot], to_pair(slot))
    for n in range(3):
        arrived(half(x, 0), up_send.at[n])
        arrived(half(x, 0), down_send.at[n])
    for way in range(2):
        for piece in range(2):
            for stage in range(3):
                arrived(relay_s.at[way, piece], u_send.at[stage, way, piece])
            arrived(relay_s.at[way, piece], u_recv.at[2, way, piece])
    arrived(upd_ref, u_send.at[3, 0, 0])
    arrived(upd_ref, u_recv.at[3, 0, 0])
    own.wait()
    for slot in range(4):
        arrived(pair_ref.at[slot], p_recv.at[slot])


def whole(shape):
    return pl.BlockSpec(shape, lambda *_: (0,) * len(shape))


def per_device(
    alignment,
    pair_rep,
    align_mask,
    residue_mask,
    bias_weight,
    row_proj_weight,
    row_out_weight,
    column_proj_weight,
    column_out_weight,
    outer_factor_weight,
    outer_out,
):
    branch = lax.axis_index("branch")
    dap = lax.axis_index("dap")
    vmem = pltpu.VMEM
    params = pltpu.CompilerParams(vmem_limit_bytes=VMEM_LIMIT)

    dma = pltpu.SemaphoreType.DMA
    half = jnp.transpose(row_proj_weight, (1, 0, 2))
    none = jnp.zeros_like(half)
    wrow = jnp.concatenate(
        [jnp.concatenate([half, none], axis=2), jnp.concatenate([none, half], axis=2)], axis=0
    ).reshape(512, 512)
    out_half = row_out_weight.reshape(4, 64, 256)
    out_none = jnp.zeros_like(out_half)
    wrow_out = jnp.concatenate(
        [
            jnp.concatenate([out_half, out_none], axis=2),
            jnp.concatenate([out_none, out_half], axis=2),
        ],
        axis=1,
    ).reshape(512, 512)

    seq_mask = lax.dynamic_slice_in_dim(align_mask, dap * 8, 8, 0).astype(F32)
    offset = ((seq_mask - 1.0) * 1e30).reshape(4, 2, SEQS)
    wcol_mine = jnp.transpose(column_proj_weight, (1, 0, 2)).reshape(256, 256)
    res_mask = lax.dynamic_slice_in_dim(align_mask, dap * 8 + branch * 2, 2, 1).astype(F32)
    res_mask = jnp.transpose(res_mask.reshape(256, 2, 2), (2, 1, 0)).reshape(2, 1, SEQS)
    col_maskcol = jnp.broadcast_to(res_mask.reshape(2, SEQS, 1), (2, SEQS, 128)).astype(BF16)

    attend_scratch = [
        vmem((SEQS, 128), BF16),
        vmem((SEQS, 128), BF16),
        vmem((SEQS, 128), F32),
        vmem((4 * SEQS, 256), BF16),
        vmem((SEQS, 128), F32),
    ]
    got, residual, wcol = pl.pallas_call(
        front_kernel,
        in_specs=[pl.BlockSpec(memory_space=vmem)] * 6,
        out_specs=(pl.BlockSpec(memory_space=vmem),) * 3,
        out_shape=(
            jax.ShapeDtypeStruct((256, 8, 128), BF16),
            jax.ShapeDtypeStruct((64, 16, 256), BF16),
            jax.ShapeDtypeStruct((4, 256, 256), BF16),
        ),
        scratch_shapes=[
            vmem((4, 2, 8, 128), BF16),
            vmem((8, 2, 4, 2, 4, 8, 128), BF16),
            vmem((2, SEQS, SEQS), F32),
            vmem((4, SEQS, 128), BF16),
            vmem((4, SEQS, 128), BF16),
            vmem((4, SEQS, 128), F32),
            vmem((4, 4 * SEQS, 256), BF16),
            vmem((2, SEQS, 128), F32),
            vmem((2, 1024, 128), F32),
            vmem((64, 16, 256), BF16),
            vmem((2, 128, 128), F32),
            vmem((SEQS, 128), F32),
            vmem((256, 8, 128), BF16),
            dma((32,)),
            dma((32,)),
            dma((4, 4)),
            dma((4, 4)),
            dma((8, 4)),
            dma((3,)),
            dma((4,)),
            dma,
            dma,
            dma,
            dma,
        ],
        compiler_params=pltpu.CompilerParams(
            vmem_limit_bytes=VMEM_LIMIT, collective_id=1, has_side_effects=True
        ),
        name="row_attention",
    )(pair_rep, bias_weight, wcol_mine, alignment, wrow, offset)
    wcol = jnp.transpose(wcol.reshape(4, 256, 4, 64), (1, 2, 0, 3)).reshape(256, 1024)

    updated, left, right = pl.pallas_call(
        column_kernel,
        grid=(2,),
        in_specs=[
            whole((64, 4, 8, 128)),
            whole((64, 16, 256)),
            whole((512, 512)),
            whole((256, 1024)),
            whole((256, 256)),
            whole((256, 64)),
            pl.BlockSpec((1, SEQS, 128), lambda i: (i, 0, 0)),
            pl.BlockSpec((1, 1, SEQS), lambda i: (i, 0, 0)),
        ],
        out_specs=(
            pl.BlockSpec((1, SEQS, 256), lambda i: (i, 0, 0)),
            pl.BlockSpec((1, FACTOR, SEQS), lambda i: (i, 0, 0)),
            pl.BlockSpec((1, FACTOR, SEQS), lambda i: (i, 0, 0)),
        ),
        out_shape=(
            jax.ShapeDtypeStruct((2, SEQS, 256), BF16),
            jax.ShapeDtypeStruct((2, FACTOR, SEQS), BF16),
            jax.ShapeDtypeStruct((2, FACTOR, SEQS), BF16),
        ),
        scratch_shapes=[
            vmem((4, SEQS, 128), F32),
            vmem((2, 1024, 128), F32),
            vmem((SEQS, 256), F32),
            vmem((SEQS, 256), BF16),
        ]
        + attend_scratch
        + [vmem((SEQS, 256), BF16)],
        compiler_params=params,
        name="column_attention",
    )(
        got.reshape(64, 4, 8, 128),
        residual,
        wrow_out,
        wcol,
        column_out_weight,
        outer_factor_weight,
        col_maskcol,
        res_mask,
    )

    gathered, pairs = pl.pallas_call(
        outer_kernel,
        in_specs=[pl.BlockSpec(memory_space=vmem)] * 4,
        out_specs=(pl.BlockSpec(memory_space=vmem),) * 2,
        out_shape=(
            jax.ShapeDtypeStruct((4, 2 * SEQS, 256), BF16),
            jax.ShapeDtypeStruct((4, 8, 8, 512), BF16),
        ),
        scratch_shapes=[
            vmem((4, 4, 64, SEQS), BF16),
            vmem((1024, SEQS), BF16),
            vmem((8, 2, 64, SEQS), BF16),
            vmem((1024, 1024), BF16),
            vmem((4096, 512), BF16),
            vmem((4, 4, 16, 4096), BF16),
            vmem((4, 8, 8, 512), BF16),
            vmem((2, 2, 256, 256), BF16),
            dma((4,)),
            dma((4,)),
            dma((3,)),
            dma((3,)),
            dma((4, 2)),
            dma((8,)),
            dma((8, 2)),
            dma((8,)),
            dma((8,)),
            dma((4, 2, 2)),
            dma((4, 2, 2)),
            dma((4,)),
            dma((4,)),
        ],
        compiler_params=pltpu.CompilerParams(
            vmem_limit_bytes=VMEM_LIMIT, collective_id=0, has_side_effects=True
        ),
        name="outer_product",
    )(
        left.reshape(2 * FACTOR, SEQS),
        right.reshape(2 * FACTOR, SEQS),
        updated.reshape(2 * SEQS, 256),
        outer_out,
    )

    rows = jnp.transpose(gathered.reshape(4, 2, 2, 256, 256), (3, 2, 0, 1, 4))
    updated_alignment = rows.reshape(SEQS, 8, 256)

    mask_rows = lax.dynamic_slice_in_dim(align_mask, dap * 8, 8, 1).astype(BF16)
    mask_cols = lax.dynamic_slice_in_dim(align_mask, branch * 128, 128, 1).astype(BF16)
    counts = jnp.einsum("si,sj->ij", mask_rows, mask_cols, preferred_element_type=F32)
    res_float = residue_mask.astype(F32)
    live_rows = lax.dynamic_slice_in_dim(res_float, dap * 8, 8, 0)
    live_cols = lax.dynamic_slice_in_dim(res_float, branch * 128, 128, 0)
    factor = live_rows[:, None] * live_cols[None, :] / (counts + count_eps)
    update = jnp.transpose(pairs.reshape(2, 2, 8, 8, 4, 128), (3, 2, 1, 0, 4, 5))
    update = update.reshape(8, 128, 128).astype(F32)
    pair_out = (pair_rep.astype(F32) + update * factor[:, :, None]).astype(BF16)
    return (updated_alignment, pair_out)


def solution(mesh):
    placed = (
        P("dap", None, None),
        P("dap", "branch", None),
        P(),
        P(),
        P(),
        P(None, None, "branch"),
        P(),
        P(None, None, "branch"),
        P(),
        P(),
        P(),
    )
    return jax.shard_map(
        per_device,
        mesh=mesh,
        in_specs=placed,
        out_specs=(P(None, "dap", None), P("dap", "branch", None)),
        check_vma=False,
    )
```

```python
import functools
import math

import jax
import jax.numpy as jnp
from jax import lax
from jax.experimental import pallas as pl
from jax.experimental.pallas import tpu as pltpu
from jax.sharding import PartitionSpec as P

HEADS = 8
HEAD = 32
FACTOR = 32
norm_eps = 1e-05
count_eps = 0.001
LOG2E = math.log2(math.e)
QUERY_SCALE = LOG2E / math.sqrt(HEAD)
F32 = jnp.float32
BF16 = jnp.bfloat16
MESH = pl.DeviceIdType.MESH
VMEM_LIMIT = 60 * 1024 * 1024
SEQS = 512
TILE = 256
NT = (((1,), (1,)), ((), ()))
TN = (((0,), (1,)), ((), ()))


def normalize(values):
    centre = jnp.mean(values, axis=-1, keepdims=True)
    centred = values - centre
    spread = jnp.mean(centred * centred, axis=-1, keepdims=True)
    return centred * lax.rsqrt(spread + norm_eps)


def dot(a, b, dims=(((1,), (0,)), ((), ()))):
    return lax.dot_general(a, b, dims, preferred_element_type=F32)


def lane_block(index):
    lanes = lax.broadcasted_iota(jnp.int32, (1, 128), 1)
    return (lanes // HEAD == index).astype(F32).astype(BF16)


def attend(q_s, k_s, g_s, rhs_s, o_s, bias_of, mask_of):
    def run(stable):
        def tile(step, extremes):
            rows = pl.ds(pl.multiple_of(step * TILE, TILE), TILE)
            q = q_s[rows, :]
            total = None
            for n in range(4):
                scores = dot(q * lane_block(n), k_s[...], NT)
                if bias_of is not None:
                    scores = scores + bias_of(step, n)
                if stable:
                    scores = jnp.where(mask_of(n) > 0.0, scores, -1e30)
                    scores = scores - jnp.max(scores, axis=1, keepdims=True)
                raised = jnp.exp2(scores).astype(BF16)
                part = dot(raised, rhs_s[n * SEQS : (n + 1) * SEQS, :])
                total = part if total is None else total + part
            sums = total[:, 128:]
            o_s[rows, :] = total[:, :128] / sums * g_s[rows, :]
            low, high = extremes
            folded = sums.reshape(TILE // 8, 8, 128)
            return jnp.minimum(low, jnp.min(folded, axis=0)), jnp.maximum(
                high, jnp.max(folded, axis=0)
            )

        start = (jnp.full((8, 128), 1.0, F32), jnp.full((8, 128), 1.0, F32))
        return lax.fori_loop(0, SEQS // TILE, tile, start)

    low, high = run(False)
    fine = jnp.logical_and(jnp.min(low) > 1e-30, jnp.max(high) < 1e30)

    @pl.when(jnp.logical_not(fine))
    def _():
        run(True)


def fill_values(rhs_s, values, mask):
    masked = values * mask
    for n in range(4):
        rhs_s[n * SEQS : (n + 1) * SEQS, :128] = masked * lane_block(n)


def fill_ones(rhs_s, mask):
    for n in range(4):
        rhs_s[n * SEQS : (n + 1) * SEQS, 128:] = mask * lane_block(n)


def place():
    branch = lax.axis_index("branch")
    dap = lax.axis_index("dap")
    return dict(
        branch=branch,
        dap=dap,
        y_hi=branch // 2,
        core=branch % 2,
        x=dap // 16,
        z=(dap // 2) % 8,
        y_lo=dap % 2,
    )


def z_turn(z, turn):
    reach = (turn + 1) // 2
    odd = turn % 2
    return lax.rem(z + odd * reach + (1 - odd) * (8 - reach), 8)


def signal(semaphore, to):
    pl.semaphore_signal(semaphore, 1, device_id=to, device_id_type=MESH)


def remote(src, dst, send_sem, recv_sem, to):
    pltpu.make_async_remote_copy(
        src, dst, send_sem, recv_sem, device_id=to, device_id_type=MESH
    ).start()


def arrived(dst, semaphore):
    pltpu.make_async_copy(dst, dst, semaphore).wait()


def attend_tile(q, k, rhs_s, lane_masks, extra):
    total = None
    for n in range(4):
        scores = dot(q * lane_masks[n], k, NT) + extra(n)
        scores = scores - jnp.max(scores, axis=1, keepdims=True)
        raised = jnp.exp2(scores).astype(BF16)
        part = dot(raised, rhs_s[n * SEQS : (n + 1) * SEQS, :])
        total = part if total is None else total + part
    return total[:, :128] / total[:, 128:]


def front_kernel(
    pair_ref,
    weight_ref,
    wcol_ref,
    x_ref,
    wrow_ref,
    off_ref,
    heads_ref,
    resid_ref,
    wall_ref,
    block_s,
    line_s,
    bias_s,
    wide_s,
    q_s,
    k_s,
    g_s,
    rhs_s,
    x_s,
    res_s,
    resb_s,
    o_s,
    buf_s,
    out_s,
    ready,
    p_send,
    p_recv,
    z_send,
    z_recv,
    w_send,
    w_recv,
    res_send,
    res_recv,
    out_send,
    out_recv,
):
    at = place()
    branch, dap, x, z, y_lo = at["branch"], at["dap"], at["x"], at["z"], at["y_lo"]
    barrier = pltpu.get_barrier_semaphore()
    me = dap * 4 + branch
    mine = x * 8 + y_lo * 4 + branch

    def plane_device(other_x, other_y, other_b):
        return (other_b, other_x * 16 + z * 2 + other_y)

    def line(other_z):
        return (branch, x * 16 + other_z * 2 + y_lo)

    def in_plane(act):
        def each(step_x, _):
            other_x = lax.rem(x + step_x, 4)
            for step_y in range(2):
                other_y = lax.rem(y_lo + step_y, 2)
                for step in range(1, 4):
                    other_b = lax.rem(branch + step, 4)
                    act(other_x * 8 + other_y * 4 + other_b, other_x, other_y, other_b)

                @pl.when(jnp.logical_or(other_x != x, other_y != y_lo))
                def _():
                    act(other_x * 8 + other_y * 4 + branch, other_x, other_y, branch)

            return 0

        lax.fori_loop(0, 4, each, 0)

    in_plane(lambda slot, *to: signal(barrier, plane_device(*to)))
    for step in range(1, 8):
        signal(barrier, line(lax.rem(z + step, 8)))

    rows, cols, width = pair_ref.shape

    def pick(sp, _):
        for p in range(2):
            for side in range(2):
                block = x_ref[sp * 2 + p, :, side * 128 : side * 128 + 128]
                x_s[p * 2 + side] = block.astype(F32)
            for side in range(2):
                for k in range(2):
                    res_s[side, pl.ds(sp * 4 + k * 2 + p, 64, stride=16), :] = x_s[
                        p * 2 + side, pl.ds(branch * 2 + k, 64, stride=8), :
                    ]
        return 0

    lax.fori_loop(0, 4, pick, 0)
    for side in range(2):
        resb_s[:, :, side * 128 : side * 128 + 128] = (
            res_s[side].reshape(64, 16, 128).astype(BF16)
        )
    values = pair_ref[...].astype(F32).reshape(rows * cols, width)
    normed = normalize(values).astype(BF16)
    res = dot(weight_ref[...], normed, TN)
    for i in range(rows):
        tile = res[:, i * cols : (i + 1) * cols].astype(BF16)
        block_s[:, :, i, :] = tile.reshape(4, 2, cols)
    pl.semaphore_wait(barrier, 31 + 7)
    for step in range(1, 8):
        signal(ready, line(lax.rem(z + step, 8)))
    for turn in range(1, 8):
        other_z = z_turn(z, turn)
        remote(block_s, line_s.at[:, z], z_send.at[turn], z_recv.at[z], line(other_z))
    pltpu.make_async_copy(block_s, line_s.at[:, z], z_recv.at[z]).start()
    across = (lax.rem(branch + 2, 4), dap)
    partner = (branch // 2 * 2 + 1 - branch % 2, dap)
    far = lax.rem(branch + 2, 4)
    remote(wcol_ref, wall_ref.at[branch], w_send.at[0], w_recv.at[0], partner)
    remote(wcol_ref, wall_ref.at[branch], w_send.at[1], w_recv.at[1], across)
    own = pltpu.make_async_copy(wcol_ref, wall_ref.at[branch], w_recv.at[3])
    own.start()

    def project(sp, _):
        normed = []
        for p in range(2):
            normed.append(normalize(x_ref[sp * 2 + p].astype(F32)).astype(BF16))
        both = jnp.concatenate(normed, axis=1)
        projected = dot(both, wrow_ref[...])
        q_s[sp] = (projected[:, :128] * QUERY_SCALE).astype(BF16)
        k_s[sp] = projected[:, 128:256].astype(BF16)
        values = projected[:, 256:384].astype(BF16)
        g_s[sp] = jax.nn.sigmoid(projected[:, 384:])
        for n in range(4):
            rhs_s[sp, n * SEQS : (n + 1) * SEQS, :128] = values * lane_block(n)
            rhs_s[sp, n * SEQS : (n + 1) * SEQS, 128:] = jnp.broadcast_to(
                lane_block(n), (SEQS, 128)
            )
        return 0

    lax.fori_loop(0, 4, project, 0)

    for other_z in range(8):
        arrived(line_s.at[:, other_z], z_recv.at[other_z])
    odd = x % 2

    def plane_turn(t):
        return lax.rem(x + t // 2 * 2, 4) + t % 2 * (1 - 2 * odd)

    def post(t, _):
        other_x = plane_turn(t)
        for step_y in range(2):
            other_y = lax.rem(y_lo + step_y, 2)
            for step in range(4):
                other_b = lax.rem(branch + step, 4)
                source, target = line_s.at[other_b], bias_s.at[x, y_lo, branch]
                slot = other_x * 8 + other_y * 4 + other_b

                def go():
                    to = plane_device(other_x, other_y, other_b)
                    remote(source, target, p_send.at[slot], p_recv.at[mine], to)

                if step:
                    go()
                else:
                    pl.when(slot != mine)(go)
        return 0

    lax.fori_loop(0, 4, post, 0)
    pltpu.make_async_copy(line_s.at[branch], bias_s.at[x, y_lo, branch], p_recv.at[mine]).start()
    arrived(wall_ref.at[far], w_recv.at[1])
    remote(wall_ref.at[far], wall_ref.at[far], w_send.at[2], w_recv.at[2], partner)
    pl.semaphore_wait(ready, 7)

    def post_res(turn, _):
        other_z = z_turn(z, turn)

        def each(step_x, _):
            other_x = lax.rem(x + step_x, 4)
            for step_y in range(2):
                other_d = other_x * 16 + other_z * 2 + lax.rem(y_lo + step_y, 2)

                @pl.when(other_d != dap)
                def _():
                    source = resb_s.at[other_d]
                    remote(source, resid_ref.at[dap], res_send, res_recv, (branch, other_d))

            return 0

        return lax.fori_loop(0, 4, each, 0)

    lax.fori_loop(0, 8, post_res, 0)
    pltpu.make_async_copy(resb_s.at[dap], resid_ref.at[dap], res_recv).start()

    def step(t, _):
        other_x = plane_turn(t)
        span = pl.ds(pl.multiple_of(other_x * 128, 128), 128)
        masks = [lane_block(n) for n in range(4)]

        for slot in range(8):
            landed = bias_s.at[other_x, slot // 4, slot % 4]
            arrived(landed, p_recv.at[other_x * 8 + slot])
        for h in range(2):
            for b in range(4):
                sides = [bias_s[other_x, y, b, :, h].astype(F32) for y in range(2)]
                piece = jnp.stack(sides, axis=1).reshape(128, 128)
                wide_s[h, :, b * 128 : b * 128 + 128] = piece * LOG2E

        def some(u, _):
            for v in range(2):
                sp = u * 2 + v

                def extra(n):
                    return wide_s[n % 2] + off_ref[sp, pl.ds(n // 2, 1), :]

                out = attend_tile(q_s[sp, span, :], k_s[sp], rhs_s.at[sp], masks, extra)
                o_s[v] = out * g_s[sp, span, :]
                for k in range(2):
                    buf_s[pl.ds(sp * 2 + k, 64, stride=8), :] = o_s[v, pl.ds(k, 64, stride=2), :]
            return 0

        lax.fori_loop(0, 2, some, 0)
        base = other_x * 64
        out_s[pl.ds(base, 64)] = buf_s[...].reshape(64, 8, 128).astype(BF16)

        def post_out(turn, _):
            for step_y in range(2):
                other_d = other_x * 16 + z_turn(z, turn) * 2 + lax.rem(y_lo + step_y, 2)
                for step in range(1, 4):
                    other_b = lax.rem(branch + step, 4)
                    source = out_s.at[other_d * 4 + other_b]
                    remote(source, heads_ref.at[me], out_send, out_recv, (other_b, other_d))

                @pl.when(other_d != dap)
                def _():
                    source = out_s.at[other_d * 4 + branch]
                    remote(source, heads_ref.at[me], out_send, out_recv, (branch, other_d))

            return 0

        lax.fori_loop(0, 8, post_out, 0)

        @pl.when(t == 0)
        def _():
            pltpu.make_async_copy(out_s.at[me], heads_ref.at[me], out_recv).start()

        return 0

    lax.fori_loop(0, 4, step, 0)

    for turn in range(1, 8):
        arrived(block_s, z_send.at[turn])
    in_plane(lambda slot, *to: arrived(line_s.at[0], p_send.at[slot]))
    own.wait()
    for n in range(3):
        arrived(wcol_ref, w_send.at[n])
    arrived(wcol_ref, w_recv.at[0])
    arrived(wcol_ref, w_recv.at[2])
    arrived(resb_s.at[pl.ds(0, 63)], res_send)
    arrived(resid_ref, res_recv)
    arrived(out_s.at[pl.ds(0, 255)], out_send)
    arrived(heads_ref, out_recv)


def column_kernel(
    a_ref,
    res_ref,
    wrow_ref,
    wcol_ref,
    wout_ref,
    wfac_ref,
    maskcol_ref,
    maskrow_ref,
    upd_ref,
    left_ref,
    right_ref,
    x_s,
    res_s,
    msa_s,
    n_s,
    q_s,
    k_s,
    g_s,
    rhs_s,
    o_s,
    heads_s,
):
    k = pl.program_id(0)

    @pl.when(k == 0)
    def _():
        pieces = [a_ref[:, b].astype(F32).reshape(SEQS, 128).astype(BF16) for b in range(4)]
        x = dot(jnp.concatenate(pieces, axis=1), wrow_ref[...])
        for j in range(4):
            x_s[j] = x[:, j * 128 : (j + 1) * 128]
        for side in range(2):
            block = res_ref[:, :, side * 128 : side * 128 + 128].astype(F32)
            res_s[side] = block.reshape(1024, 128)

    mine = [x_s[j, pl.ds(k, 256, stride=2), :] for j in range(4)]
    rows = jnp.concatenate(
        [jnp.concatenate(mine[:2], axis=1), jnp.concatenate(mine[2:], axis=1)], axis=0
    )
    base = jnp.concatenate(
        [
            jnp.concatenate(
                [res_s[side, pl.ds(k * 2 + p, 256, stride=4), :] for side in range(2)], axis=1
            )
            for p in range(2)
        ],
        axis=0,
    )
    msa = (rows + base).astype(BF16).astype(F32)
    msa_s[...] = msa
    n_s[...] = normalize(msa).astype(BF16)
    fill_ones(rhs_s, maskcol_ref[0])
    for group in range(2):
        lanes = slice(group * 128, group * 128 + 128)

        def project(part):
            at = part * 256 + group * 128
            return dot(n_s[...], wcol_ref[:, at : at + 128])

        q_s[...] = (project(0) * QUERY_SCALE).astype(BF16)
        k_s[...] = project(1).astype(BF16)
        fill_values(rhs_s, project(2).astype(BF16), maskcol_ref[0])
        g_s[...] = jax.nn.sigmoid(project(3))
        attend(q_s, k_s, g_s, rhs_s, o_s, None, lambda n: maskrow_ref[0])
        heads_s[:, lanes] = o_s[...].astype(BF16)
    updated = (msa_s[...] + dot(heads_s[...], wout_ref[...])).astype(BF16)
    upd_ref[0] = updated
    outer = normalize(updated.astype(F32)).astype(BF16)
    factors = dot(wfac_ref[...], outer, TN) * maskrow_ref[0]
    left_ref[0] = factors[:FACTOR].astype(BF16)
    right_ref[0] = factors[FACTOR:].astype(BF16)


def outer_kernel(
    left_ref,
    right_ref,
    upd_ref,
    weight_ref,
    gather_ref,
    pair_ref,
    l_s,
    lp_s,
    r_s,
    perm_s,
    wide_s,
    lhs_s,
    send_s,
    relay_s,
    l_send,
    l_recv,
    up_send,
    down_send,
    x_recv,
    r_send,
    r_recv,
    f_send,
    f_recv,
    u_send,
    u_recv,
    p_send,
    p_recv,
):
    at = place()
    branch, dap, y_hi, core = at["branch"], at["dap"], at["y_hi"], at["core"]
    x, z, y_lo = at["x"], at["z"], at["y_lo"]
    barrier = pltpu.get_barrier_semaphore()

    def greet(index, _):
        to = (index // 8, (index // 2) % 4 * 16 + z * 2 + index % 2)

        @pl.when(jnp.logical_or(to[0] != branch, to[1] != dap))
        def _():
            signal(barrier, to)

        return 0

    lax.fori_loop(0, 32, greet, 0)

    def greet_line(index, _):
        other_z = index // 2

        @pl.when(other_z != z)
        def _():
            signal(barrier, (y_hi * 2 + index % 2, x * 16 + other_z * 2 + y_lo))

        return 0

    lax.fori_loop(0, 16, greet_line, 0)
    pl.semaphore_wait(barrier, 31 + 14)

    def elsewhere(to):
        return jnp.logical_or(to[0] != branch, to[1] != dap)

    def send(src, dst, send_sem, recv_sem, to):
        other = elsewhere(to)

        @pl.when(other)
        def _():
            remote(src, dst, send_sem, recv_sem, to)

        @pl.when(jnp.logical_not(other))
        def _():
            pltpu.make_async_copy(src, dst, recv_sem).start()

    def sent(src, send_sem, to):
        @pl.when(elsewhere(to))
        def _():
            arrived(src, send_sem)

    def to_left(slot):
        return (slot // 2 * 2 + y_lo, x * 16 + z * 2 + slot % 2)

    def to_right(slot):
        return (branch, x * 16 + slot * 2 + y_lo)

    def to_pair(slot):
        return (x, slot * 16 + z * 2 + core)

    def x_line(other_x):
        return (branch, other_x * 16 + z * 2 + y_lo)

    def y_line(step):
        other = lax.rem(y_hi * 2 + y_lo + step, 4)
        return (other // 2 * 2 + core, x * 16 + z * 2 + other % 2)

    partner = (y_hi * 2 + 1 - core, dap)
    far = lax.rem(branch + 2, 4)
    for step in range(4):
        slot = lax.rem(y_hi * 2 + y_lo + step, 4)
        send(left_ref, l_s.at[x, branch], l_send.at[slot], l_recv.at[branch], to_left(slot))
    for turn in range(8):
        slot = z_turn(z, turn)
        send(right_ref, r_s.at[z, core], r_send.at[slot], r_recv.at[z, core], to_right(slot))

    def rows_of(way, piece):
        return pl.ds(way * 512 + piece * 256, 256)

    steps = (1, 3)
    for piece in range(2):
        for way in range(2):
            remote(
                upd_ref.at[rows_of(way, piece)],
                relay_s.at[way, piece],
                u_send.at[0, way, piece],
                u_recv.at[0, way, piece],
                y_line(steps[way]),
            )
    remote(upd_ref, gather_ref.at[branch], u_send.at[3, 0, 0], u_recv.at[3, 0, 0], partner)
    own = pltpu.make_async_copy(upd_ref, gather_ref.at[branch], u_recv.at[3, 0, 1])
    own.start()

    wide_s[...] = jnp.zeros_like(wide_s)

    def widen(c, _):
        block = weight_ref[pl.ds(pl.multiple_of(c * 32, 32), 32), :]
        for j in range(4):
            rows = pl.ds(pl.multiple_of(c * 128 + j * 32, 32), 32)
            wide_s[rows, j * 128 : (j + 1) * 128] = block
        return 0

    lax.fori_loop(0, 32, widen, 0)

    def permute(c, _):
        source = lax.broadcasted_iota(jnp.int32, (32, 1024), 1)
        wanted = lax.broadcasted_iota(jnp.int32, (32, 1024), 0) * 32 + c
        rows = pl.ds(pl.multiple_of(c * 32, 32), 32)
        perm_s[rows, :] = (source == wanted).astype(F32).astype(BF16)
        return 0

    lax.fori_loop(0, 32, permute, 0)

    above, below = lax.rem(x + 1, 4), lax.rem(x + 3, 4)

    def half(other_x, h):
        return l_s.at[other_x, pl.ds(h * 2, 2)]

    def pass_x(origin, h, send_sem, to):
        region = half(origin, h)
        remote(region, region, send_sem, x_recv.at[origin, h], x_line(to))

    for slot in range(4):
        arrived(l_s.at[x, slot], l_recv.at[slot])
    for h in range(2):
        pass_x(x, h, up_send.at[h], above)
        pass_x(x, 1 - h, down_send.at[1 - h], below)

    def relay(way, piece):
        region = relay_s.at[way, piece]
        arrived(region, u_recv.at[0, way, piece])
        to = y_line(steps[way])
        remote(
            region,
            gather_ref.at[lax.rem(to[0] + 2, 4), rows_of(way, piece)],
            u_send.at[1, way, piece],
            u_recv.at[1, way, piece],
            to,
        )

    for way in range(2):
        relay(way, 0)
    for slot in range(8):
        arrived(r_s.at[slot, core], r_recv.at[slot, core])
        remote(r_s.at[slot, core], r_s.at[slot, core], f_send.at[slot], f_recv.at[slot], partner)
    arrived(half(below, 0), x_recv.at[below, 0])
    pass_x(below, 0, up_send.at[2], above)
    arrived(half(above, 1), x_recv.at[above, 1])
    pass_x(above, 1, down_send.at[2], below)
    for way in range(2):
        relay(way, 1)
    arrived(half(below, 1), x_recv.at[below, 1])
    arrived(half(above, 0), x_recv.at[above, 0])
    opposite = lax.rem(x + 2, 4)
    for h in range(2):
        arrived(half(opposite, h), x_recv.at[opposite, h])
    lefts = l_s[...].reshape(1024, SEQS)
    lp_s[...] = dot(perm_s[...], lefts).astype(BF16)
    for slot in range(8):
        arrived(r_s.at[slot, 1 - core], f_recv.at[slot])

    def contract(jc, _):
        rights = r_s[pl.ds(jc * 2, 2)].reshape(256, SEQS)
        block = dot(lp_s[...], rights, NT)
        for c in range(32):
            for xi in range(4):
                rows = slice(c * 32 + xi * 8, c * 32 + xi * 8 + 8)
                tile = jnp.concatenate([block[rows, :128], block[rows, 128:]], axis=0)
                lhs_s[xi, jc, :, c * 128 : c * 128 + 128] = tile.astype(BF16)
        return 0

    lax.fori_loop(0, 4, contract, 0)
    update = dot(lhs_s[...].reshape(256, 4096), wide_s[...])
    send_s[...] = update.reshape(4, 8, 8, 512).astype(BF16)
    for step in range(4):
        slot = lax.rem(x + step, 4)
        send(
            send_s.at[slot],
            pair_ref.at[y_hi * 2 + y_lo],
            p_send.at[slot],
            p_recv.at[y_hi * 2 + y_lo],
            to_pair(slot),
        )
    for piece in range(2):
        for way in range(2):
            region = gather_ref.at[far, rows_of(way, piece)]
            arrived(region, u_recv.at[1, way, piece])
            remote(region, region, u_send.at[2, way, piece], u_recv.at[2, way, piece], partner)
    for slot in range(8):
        sent(right_ref, r_send.at[slot], to_right(slot))
        arrived(right_ref, f_send.at[slot])
    for slot in range(4):
        sent(left_ref, l_send.at[slot], to_left(slot))
        sent(send_s.at[slot], p_send.at[slot], to_pair(slot))
    for n in range(3):
        arrived(half(x, 0), up_send.at[n])
        arrived(half(x, 0), down_send.at[n])
    for way in range(2):
        for piece in range(2):
            for stage in range(3):
                arrived(relay_s.at[way, piece], u_send.at[stage, way, piece])
            arrived(relay_s.at[way, piece], u_recv.at[2, way, piece])
    arrived(upd_ref, u_send.at[3, 0, 0])
    arrived(upd_ref, u_recv.at[3, 0, 0])
    own.wait()
    for slot in range(4):
        arrived(pair_ref.at[slot], p_recv.at[slot])


def whole(shape):
    return pl.BlockSpec(shape, lambda *_: (0,) * len(shape))


def per_device(
    alignment,
    pair_rep,
    align_mask,
    residue_mask,
    bias_weight,
    row_proj_weight,
    row_out_weight,
    column_proj_weight,
    column_out_weight,
    outer_factor_weight,
    outer_out,
):
    branch = lax.axis_index("branch")
    dap = lax.axis_index("dap")
    vmem = pltpu.VMEM
    params = pltpu.CompilerParams(vmem_limit_bytes=VMEM_LIMIT)

    dma = pltpu.SemaphoreType.DMA
    half = jnp.transpose(row_proj_weight, (1, 0, 2))
    none = jnp.zeros_like(half)
    wrow = jnp.concatenate(
        [jnp.concatenate([half, none], axis=2), jnp.concatenate([none, half], axis=2)], axis=0
    ).reshape(512, 512)
    out_half = row_out_weight.reshape(4, 64, 256)
    out_none = jnp.zeros_like(out_half)
    wrow_out = jnp.concatenate(
        [
            jnp.concatenate([out_half, out_none], axis=2),
            jnp.concatenate([out_none, out_half], axis=2),
        ],
        axis=1,
    ).reshape(512, 512)

    seq_mask = lax.dynamic_slice_in_dim(align_mask, dap * 8, 8, 0).astype(F32)
    offset = ((seq_mask - 1.0) * 1e30).reshape(4, 2, SEQS)
    wcol_mine = jnp.transpose(column_proj_weight, (1, 0, 2)).reshape(256, 256)
    res_mask = lax.dynamic_slice_in_dim(align_mask, dap * 8 + branch * 2, 2, 1).astype(F32)
    res_mask = jnp.transpose(res_mask.reshape(256, 2, 2), (2, 1, 0)).reshape(2, 1, SEQS)
    col_maskcol = jnp.broadcast_to(res_mask.reshape(2, SEQS, 1), (2, SEQS, 128)).astype(BF16)

    attend_scratch = [
        vmem((SEQS, 128), BF16),
        vmem((SEQS, 128), BF16),
        vmem((SEQS, 128), F32),
        vmem((4 * SEQS, 256), BF16),
        vmem((SEQS, 128), F32),
    ]
    got, residual, wcol = pl.pallas_call(
        front_kernel,
        in_specs=[pl.BlockSpec(memory_space=vmem)] * 6,
        out_specs=(pl.BlockSpec(memory_space=vmem),) * 3,
        out_shape=(
            jax.ShapeDtypeStruct((256, 8, 128), BF16),
            jax.ShapeDtypeStruct((64, 16, 256), BF16),
            jax.ShapeDtypeStruct((4, 256, 256), BF16),
        ),
        scratch_shapes=[
            vmem((4, 2, 8, 128), BF16),
            vmem((4, 8, 2, 8, 128), BF16),
            vmem((4, 2, 4, 8, 2, 8, 128), BF16),
            vmem((2, 128, SEQS), F32),
            vmem((4, SEQS, 128), BF16),
            vmem((4, SEQS, 128), BF16),
            vmem((4, SEQS, 128), F32),
            vmem((4, 4 * SEQS, 256), BF16),
            vmem((4, SEQS, 128), F32),
            vmem((2, 1024, 128), F32),
            vmem((64, 16, 256), BF16),
            vmem((2, 128, 128), F32),
            vmem((SEQS, 128), F32),
            vmem((256, 8, 128), BF16),
            pltpu.SemaphoreType.REGULAR,
            dma((32,)),
            dma((32,)),
            dma((8,)),
            dma((8,)),
            dma((3,)),
            dma((4,)),
            dma,
            dma,
            dma,
            dma,
        ],
        compiler_params=pltpu.CompilerParams(
            vmem_limit_bytes=VMEM_LIMIT, collective_id=1, has_side_effects=True
        ),
        name="row_attention",
    )(pair_rep, bias_weight, wcol_mine, alignment, wrow, offset)
    wcol = jnp.transpose(wcol.reshape(4, 256, 4, 64), (1, 2, 0, 3)).reshape(256, 1024)

    updated, left, right = pl.pallas_call(
        column_kernel,
        grid=(2,),
        in_specs=[
            whole((64, 4, 8, 128)),
            whole((64, 16, 256)),
            whole((512, 512)),
            whole((256, 1024)),
            whole((256, 256)),
            whole((256, 64)),
            pl.BlockSpec((1, SEQS, 128), lambda i: (i, 0, 0)),
            pl.BlockSpec((1, 1, SEQS), lambda i: (i, 0, 0)),
        ],
        out_specs=(
            pl.BlockSpec((1, SEQS, 256), lambda i: (i, 0, 0)),
            pl.BlockSpec((1, FACTOR, SEQS), lambda i: (i, 0, 0)),
            pl.BlockSpec((1, FACTOR, SEQS), lambda i: (i, 0, 0)),
        ),
        out_shape=(
            jax.ShapeDtypeStruct((2, SEQS, 256), BF16),
            jax.ShapeDtypeStruct((2, FACTOR, SEQS), BF16),
            jax.ShapeDtypeStruct((2, FACTOR, SEQS), BF16),
        ),
        scratch_shapes=[
            vmem((4, SEQS, 128), F32),
            vmem((2, 1024, 128), F32),
            vmem((SEQS, 256), F32),
            vmem((SEQS, 256), BF16),
        ]
        + attend_scratch
        + [vmem((SEQS, 256), BF16)],
        compiler_params=params,
        name="column_attention",
    )(
        got.reshape(64, 4, 8, 128),
        residual,
        wrow_out,
        wcol,
        column_out_weight,
        outer_factor_weight,
        col_maskcol,
        res_mask,
    )

    gathered, pairs = pl.pallas_call(
        outer_kernel,
        in_specs=[pl.BlockSpec(memory_space=vmem)] * 4,
        out_specs=(pl.BlockSpec(memory_space=vmem),) * 2,
        out_shape=(
            jax.ShapeDtypeStruct((4, 2 * SEQS, 256), BF16),
            jax.ShapeDtypeStruct((4, 8, 8, 512), BF16),
        ),
        scratch_shapes=[
            vmem((4, 4, 64, SEQS), BF16),
            vmem((1024, SEQS), BF16),
            vmem((8, 2, 64, SEQS), BF16),
            vmem((1024, 1024), BF16),
            vmem((4096, 512), BF16),
            vmem((4, 4, 16, 4096), BF16),
            vmem((4, 8, 8, 512), BF16),
            vmem((2, 2, 256, 256), BF16),
            dma((4,)),
            dma((4,)),
            dma((3,)),
            dma((3,)),
            dma((4, 2)),
            dma((8,)),
            dma((8, 2)),
            dma((8,)),
            dma((8,)),
            dma((4, 2, 2)),
            dma((4, 2, 2)),
            dma((4,)),
            dma((4,)),
        ],
        compiler_params=pltpu.CompilerParams(
            vmem_limit_bytes=VMEM_LIMIT, collective_id=0, has_side_effects=True
        ),
        name="outer_product",
    )(
        left.reshape(2 * FACTOR, SEQS),
        right.reshape(2 * FACTOR, SEQS),
        updated.reshape(2 * SEQS, 256),
        outer_out,
    )

    rows = jnp.transpose(gathered.reshape(4, 2, 2, 256, 256), (3, 2, 0, 1, 4))
    updated_alignment = rows.reshape(SEQS, 8, 256)

    mask_rows = lax.dynamic_slice_in_dim(align_mask, dap * 8, 8, 1).astype(BF16)
    mask_cols = lax.dynamic_slice_in_dim(align_mask, branch * 128, 128, 1).astype(BF16)
    counts = jnp.einsum("si,sj->ij", mask_rows, mask_cols, preferred_element_type=F32)
    res_float = residue_mask.astype(F32)
    live_rows = lax.dynamic_slice_in_dim(res_float, dap * 8, 8, 0)
    live_cols = lax.dynamic_slice_in_dim(res_float, branch * 128, 128, 0)
    factor = live_rows[:, None] * live_cols[None, :] / (counts + count_eps)
    update = jnp.transpose(pairs.reshape(2, 2, 8, 8, 4, 128), (3, 2, 1, 0, 4, 5))
    update = update.reshape(8, 128, 128).astype(F32)
    pair_out = (pair_rep.astype(F32) + update * factor[:, :, None]).astype(BF16)
    return (updated_alignment, pair_out)


def solution(mesh):
    placed = (
        P("dap", None, None),
        P("dap", "branch", None),
        P(),
        P(),
        P(),
        P(None, None, "branch"),
        P(),
        P(None, None, "branch"),
        P(),
        P(),
        P(),
    )
    return jax.shard_map(
        per_device,
        mesh=mesh,
        in_specs=placed,
        out_specs=(P(None, "dap", None), P("dap", "branch", None)),
        check_vma=False,
    )
```

```python
import functools
import math

import jax
import jax.numpy as jnp
from jax import lax
from jax.experimental import pallas as pl
from jax.experimental.pallas import tpu as pltpu
from jax.sharding import PartitionSpec as P

HEADS = 8
HEAD = 32
FACTOR = 32
norm_eps = 1e-05
count_eps = 0.001
LOG2E = math.log2(math.e)
QUERY_SCALE = LOG2E / math.sqrt(HEAD)
F32 = jnp.float32
BF16 = jnp.bfloat16
MESH = pl.DeviceIdType.MESH
VMEM_LIMIT = 60 * 1024 * 1024
SEQS = 512
TILE = 256
NT = (((1,), (1,)), ((), ()))
TN = (((0,), (1,)), ((), ()))


def normalize(values):
    centre = jnp.mean(values, axis=-1, keepdims=True)
    centred = values - centre
    spread = jnp.mean(centred * centred, axis=-1, keepdims=True)
    return centred * lax.rsqrt(spread + norm_eps)


def dot(a, b, dims=(((1,), (0,)), ((), ()))):
    return lax.dot_general(a, b, dims, preferred_element_type=F32)


def lane_block(index):
    lanes = lax.broadcasted_iota(jnp.int32, (1, 128), 1)
    return (lanes // HEAD == index).astype(F32).astype(BF16)


def place():
    branch = lax.axis_index("branch")
    dap = lax.axis_index("dap")
    return dict(
        branch=branch,
        dap=dap,
        y_hi=branch // 2,
        core=branch % 2,
        x=dap // 16,
        z=(dap // 2) % 8,
        y_lo=dap % 2,
    )


def z_turn(z, turn):
    reach = (turn + 1) // 2
    odd = turn % 2
    return lax.rem(z + odd * reach + (1 - odd) * (8 - reach), 8)


def signal(semaphore, to):
    pl.semaphore_signal(semaphore, 1, device_id=to, device_id_type=MESH)


def remote(src, dst, send_sem, recv_sem, to):
    pltpu.make_async_remote_copy(
        src, dst, send_sem, recv_sem, device_id=to, device_id_type=MESH
    ).start()


def arrived(dst, semaphore):
    pltpu.make_async_copy(dst, dst, semaphore).wait()


def attend_tile(q, k, rhs_s, lane_masks, extra):
    total = None
    for n in range(4):
        scores = dot(q * lane_masks[n], k, NT) + extra(n)
        scores = scores - jnp.max(scores, axis=1, keepdims=True)
        raised = jnp.exp2(scores).astype(BF16)
        part = dot(raised, rhs_s[n * SEQS : (n + 1) * SEQS, :])
        total = part if total is None else total + part
    return total[:, :128] / total[:, 128:]


def front_kernel(
    pair_ref,
    weight_ref,
    wcol_ref,
    x_ref,
    wrow_ref,
    off_ref,
    heads_ref,
    resid_ref,
    wall_ref,
    block_s,
    line_s,
    bias_s,
    wide_s,
    q_s,
    k_s,
    g_s,
    rhs_s,
    x_s,
    res_s,
    resb_s,
    o_s,
    buf_s,
    out_s,
    ready,
    p_send,
    p_recv,
    z_send,
    z_recv,
    w_send,
    w_recv,
    res_send,
    res_recv,
    out_send,
    out_recv,
):
    at = place()
    branch, dap, x, z, y_lo = at["branch"], at["dap"], at["x"], at["z"], at["y_lo"]
    barrier = pltpu.get_barrier_semaphore()
    me = dap * 4 + branch
    mine = x * 8 + y_lo * 4 + branch

    def plane_device(other_x, other_y, other_b):
        return (other_b, other_x * 16 + z * 2 + other_y)

    def line(other_z):
        return (branch, x * 16 + other_z * 2 + y_lo)

    def in_plane(act):
        def each(step_x, _):
            other_x = lax.rem(x + step_x, 4)
            for step_y in range(2):
                other_y = lax.rem(y_lo + step_y, 2)
                for step in range(1, 4):
                    other_b = lax.rem(branch + step, 4)
                    act(other_x * 8 + other_y * 4 + other_b, other_x, other_y, other_b)

                @pl.when(jnp.logical_or(other_x != x, other_y != y_lo))
                def _():
                    act(other_x * 8 + other_y * 4 + branch, other_x, other_y, branch)

            return 0

        lax.fori_loop(0, 4, each, 0)

    in_plane(lambda slot, *to: signal(barrier, plane_device(*to)))
    for step in range(1, 8):
        signal(barrier, line(lax.rem(z + step, 8)))

    rows, cols, width = pair_ref.shape

    def pick(sp, _):
        for p in range(2):
            for side in range(2):
                block = x_ref[sp * 2 + p, :, side * 128 : side * 128 + 128]
                x_s[p * 2 + side] = block.astype(F32)
            for side in range(2):
                for k in range(2):
                    res_s[side, pl.ds(sp * 4 + k * 2 + p, 64, stride=16), :] = x_s[
                        p * 2 + side, pl.ds(branch * 2 + k, 64, stride=8), :
                    ]
        return 0

    lax.fori_loop(0, 4, pick, 0)
    for side in range(2):
        resb_s[:, :, side * 128 : side * 128 + 128] = (
            res_s[side].reshape(64, 16, 128).astype(BF16)
        )
    values = pair_ref[...].astype(F32).reshape(rows * cols, width)
    normed = normalize(values).astype(BF16)
    res = dot(weight_ref[...], normed, TN)
    for i in range(rows):
        tile = res[:, i * cols : (i + 1) * cols].astype(BF16)
        block_s[:, :, i, :] = tile.reshape(4, 2, cols)
    pl.semaphore_wait(barrier, 31 + 7)
    for step in range(1, 8):
        signal(ready, line(lax.rem(z + step, 8)))
    for turn in range(1, 8):
        other_z = z_turn(z, turn)
        remote(block_s, line_s.at[:, z], z_send.at[turn], z_recv.at[z], line(other_z))
    pltpu.make_async_copy(block_s, line_s.at[:, z], z_recv.at[z]).start()
    across = (lax.rem(branch + 2, 4), dap)
    partner = (branch // 2 * 2 + 1 - branch % 2, dap)
    far = lax.rem(branch + 2, 4)
    remote(wcol_ref, wall_ref.at[branch], w_send.at[0], w_recv.at[0], partner)
    remote(wcol_ref, wall_ref.at[branch], w_send.at[1], w_recv.at[1], across)
    own = pltpu.make_async_copy(wcol_ref, wall_ref.at[branch], w_recv.at[3])
    own.start()

    def project(sp, _):
        normed = []
        for p in range(2):
            normed.append(normalize(x_ref[sp * 2 + p].astype(F32)).astype(BF16))
        both = jnp.concatenate(normed, axis=1)
        projected = dot(both, wrow_ref[...])
        q_s[sp] = (projected[:, :128] * QUERY_SCALE).astype(BF16)
        k_s[sp] = projected[:, 128:256].astype(BF16)
        values = projected[:, 256:384].astype(BF16)
        g_s[sp] = jax.nn.sigmoid(projected[:, 384:])
        for n in range(4):
            rhs_s[sp, n * SEQS : (n + 1) * SEQS, :128] = values * lane_block(n)
            rhs_s[sp, n * SEQS : (n + 1) * SEQS, 128:] = jnp.broadcast_to(
                lane_block(n), (SEQS, 128)
            )
        return 0

    lax.fori_loop(0, 4, project, 0)

    for other_z in range(8):
        arrived(line_s.at[:, other_z], z_recv.at[other_z])
    odd = x % 2

    def plane_turn(t):
        return lax.rem(x + t // 2 * 2, 4) + t % 2 * (1 - 2 * odd)

    def post(t, _):
        other_x = plane_turn(t)
        for step_y in range(2):
            other_y = lax.rem(y_lo + step_y, 2)
            for step in range(4):
                other_b = lax.rem(branch + step, 4)
                source, target = line_s.at[other_b], bias_s.at[x, y_lo, branch]
                slot = other_x * 8 + other_y * 4 + other_b

                def go():
                    to = plane_device(other_x, other_y, other_b)
                    remote(source, target, p_send.at[slot], p_recv.at[mine], to)

                if step:
                    go()
                else:
                    pl.when(slot != mine)(go)
        return 0

    lax.fori_loop(0, 4, post, 0)
    pltpu.make_async_copy(line_s.at[branch], bias_s.at[x, y_lo, branch], p_recv.at[mine]).start()
    arrived(wall_ref.at[far], w_recv.at[1])
    remote(wall_ref.at[far], wall_ref.at[far], w_send.at[2], w_recv.at[2], partner)
    pl.semaphore_wait(ready, 7)

    def post_res(turn, _):
        other_z = z_turn(z, turn)

        def each(step_x, _):
            other_x = lax.rem(x + step_x, 4)
            for step_y in range(2):
                other_d = other_x * 16 + other_z * 2 + lax.rem(y_lo + step_y, 2)

                @pl.when(other_d != dap)
                def _():
                    source = resb_s.at[other_d]
                    remote(source, resid_ref.at[dap], res_send, res_recv, (branch, other_d))

            return 0

        return lax.fori_loop(0, 4, each, 0)

    lax.fori_loop(0, 8, post_res, 0)
    pltpu.make_async_copy(resb_s.at[dap], resid_ref.at[dap], res_recv).start()

    def step(t, _):
        other_x = plane_turn(t)
        span = pl.ds(pl.multiple_of(other_x * 128, 128), 128)
        masks = [lane_block(n) for n in range(4)]

        for slot in range(8):
            landed = bias_s.at[other_x, slot // 4, slot % 4]
            arrived(landed, p_recv.at[other_x * 8 + slot])
        for h in range(2):
            for b in range(4):
                sides = [bias_s[other_x, y, b, :, h].astype(F32) for y in range(2)]
                piece = jnp.stack(sides, axis=1).reshape(128, 128)
                wide_s[h, :, b * 128 : b * 128 + 128] = piece * LOG2E

        def some(u, _):
            for v in range(2):
                sp = u * 2 + v

                def extra(n):
                    return wide_s[n % 2] + off_ref[sp, pl.ds(n // 2, 1), :]

                out = attend_tile(q_s[sp, span, :], k_s[sp], rhs_s.at[sp], masks, extra)
                o_s[v] = out * g_s[sp, span, :]
                for k in range(2):
                    buf_s[pl.ds(sp * 2 + k, 64, stride=8), :] = o_s[v, pl.ds(k, 64, stride=2), :]
            return 0

        lax.fori_loop(0, 2, some, 0)
        base = other_x * 64
        out_s[pl.ds(base, 64)] = buf_s[...].reshape(64, 8, 128).astype(BF16)

        def post_out(turn, _):
            for step_y in range(2):
                other_d = other_x * 16 + z_turn(z, turn) * 2 + lax.rem(y_lo + step_y, 2)
                for step in range(1, 4):
                    other_b = lax.rem(branch + step, 4)
                    source = out_s.at[other_d * 4 + other_b]
                    remote(source, heads_ref.at[me], out_send, out_recv, (other_b, other_d))

                @pl.when(other_d != dap)
                def _():
                    source = out_s.at[other_d * 4 + branch]
                    remote(source, heads_ref.at[me], out_send, out_recv, (branch, other_d))

            return 0

        lax.fori_loop(0, 8, post_out, 0)

        @pl.when(t == 0)
        def _():
            pltpu.make_async_copy(out_s.at[me], heads_ref.at[me], out_recv).start()

        return 0

    lax.fori_loop(0, 4, step, 0)

    for turn in range(1, 8):
        arrived(block_s, z_send.at[turn])
    in_plane(lambda slot, *to: arrived(line_s.at[0], p_send.at[slot]))
    own.wait()
    for n in range(3):
        arrived(wcol_ref, w_send.at[n])
    arrived(wcol_ref, w_recv.at[0])
    arrived(wcol_ref, w_recv.at[2])
    arrived(resb_s.at[pl.ds(0, 63)], res_send)
    arrived(resid_ref, res_recv)
    arrived(out_s.at[pl.ds(0, 255)], out_send)
    arrived(heads_ref, out_recv)


def back_kernel(
    a_ref,
    res_ref,
    wrow_ref,
    wcol_ref,
    wout_ref,
    wfac_ref,
    mask_ref,
    weight_ref,
    gather_ref,
    pair_ref,
    x_s,
    res_s,
    msa_s,
    n_s,
    q_s,
    k_s,
    g_s,
    rhs_s,
    heads_s,
    left_s,
    right_s,
    upd_s,
    l_s,
    lp_s,
    r_s,
    perm_s,
    wide_s,
    lhs_s,
    send_s,
    relay_s,
    l_send,
    l_recv,
    up_send,
    down_send,
    x_recv,
    r_send,
    r_recv,
    f_send,
    f_recv,
    u_send,
    u_recv,
    g_send,
    g_recv,
    own_sem,
    p_send,
    p_recv,
):
    at = place()
    branch, dap, y_hi, core = at["branch"], at["dap"], at["y_hi"], at["core"]
    x, z, y_lo = at["x"], at["z"], at["y_lo"]
    barrier = pltpu.get_barrier_semaphore()

    def greet(step_x, _):
        other_x = lax.rem(x + step_x, 4)
        for step_y in range(2):
            other_d = other_x * 16 + z * 2 + lax.rem(y_lo + step_y, 2)
            for step in range(1, 4):
                signal(barrier, (lax.rem(branch + step, 4), other_d))

            @pl.when(other_d != dap)
            def _():
                signal(barrier, (branch, other_d))

        return 0

    lax.fori_loop(0, 4, greet, 0)
    for step in range(1, 8):
        other_z = lax.rem(z + step, 8)
        for other_core in range(2):
            signal(barrier, (y_hi * 2 + other_core, x * 16 + other_z * 2 + y_lo))

    def elsewhere(to):
        return jnp.logical_or(to[0] != branch, to[1] != dap)

    def send(src, dst, send_sem, recv_sem, to):
        other = elsewhere(to)

        @pl.when(other)
        def _():
            remote(src, dst, send_sem, recv_sem, to)

        @pl.when(jnp.logical_not(other))
        def _():
            pltpu.make_async_copy(src, dst, recv_sem).start()

    def sent(src, send_sem, to):
        @pl.when(elsewhere(to))
        def _():
            arrived(src, send_sem)

    def to_left(slot):
        return (slot // 2 * 2 + y_lo, x * 16 + z * 2 + slot % 2)

    def to_right(slot):
        return (branch, x * 16 + slot * 2 + y_lo)

    def to_pair(slot):
        return (x, slot * 16 + z * 2 + core)

    def x_line(other_x):
        return (branch, other_x * 16 + z * 2 + y_lo)

    def y_line(step):
        other = lax.rem(y_hi * 2 + y_lo + step, 4)
        return (other // 2 * 2 + core, x * 16 + z * 2 + other % 2)

    partner = (y_hi * 2 + 1 - core, dap)
    far = lax.rem(branch + 2, 4)
    above, below = lax.rem(x + 1, 4), lax.rem(x + 3, 4)
    opposite = lax.rem(x + 2, 4)
    steps = (1, 3)

    def part(way):
        return pl.ds(way * 256, 256)

    def half(other_x, h, k):
        return l_s.at[other_x, pl.ds(h * 2, 2), k]

    def pass_x(origin, h, k, send_sem, to):
        region = half(origin, h, k)
        remote(region, region, send_sem, x_recv.at[k, origin, h], x_line(to))

    def first(k):
        for step in range(4):
            slot = lax.rem(y_hi * 2 + y_lo + step, 4)
            send(
                left_s.at[k],
                l_s.at[x, branch, k],
                l_send.at[k, slot],
                l_recv.at[k, branch],
                to_left(slot),
            )
        for turn in range(8):
            slot = z_turn(z, turn)
            send(
                right_s.at[k],
                r_s.at[z, core, k],
                r_send.at[k, slot],
                r_recv.at[k, z],
                to_right(slot),
            )
        for way in range(2):
            remote(
                upd_s.at[k, part(way)],
                relay_s.at[way, k],
                u_send.at[0, way, k],
                u_recv.at[0, way, k],
                y_line(steps[way]),
            )
        remote(upd_s.at[k], gather_ref.at[branch, k], g_send.at[k], g_recv.at[k], partner)
        pltpu.make_async_copy(upd_s.at[k], gather_ref.at[branch, k], own_sem.at[k]).start()

    def second(k):
        for slot in range(4):
            arrived(l_s.at[x, slot, k], l_recv.at[k, slot])
        for h in range(2):
            pass_x(x, h, k, up_send.at[k, h], above)
            pass_x(x, 1 - h, k, down_send.at[k, 1 - h], below)
        for way in range(2):
            region = relay_s.at[way, k]
            arrived(region, u_recv.at[0, way, k])
            to = y_line(steps[way])
            remote(
                region,
                gather_ref.at[lax.rem(to[0] + 2, 4), k, part(way)],
                u_send.at[1, way, k],
                u_recv.at[1, way, k],
                to,
            )

    def third(k):
        for slot in range(8):
            region = r_s.at[slot, core, k]
            arrived(region, r_recv.at[k, slot])
            remote(region, region, f_send.at[k, slot], f_recv.at[k, slot], partner)
        arrived(half(below, 0, k), x_recv.at[k, below, 0])
        pass_x(below, 0, k, up_send.at[k, 2], above)
        arrived(half(above, 1, k), x_recv.at[k, above, 1])
        pass_x(above, 1, k, down_send.at[k, 2], below)

    def fourth(k):
        for way in range(2):
            region = gather_ref.at[far, k, part(way)]
            arrived(region, u_recv.at[1, way, k])
            remote(region, region, u_send.at[2, way, k], u_recv.at[2, way, k], partner)

    pieces = [a_ref[:, b].astype(F32).reshape(SEQS, 128).astype(BF16) for b in range(4)]
    moved = dot(jnp.concatenate(pieces, axis=1), wrow_ref[...])
    for j in range(4):
        x_s[j] = moved[:, j * 128 : (j + 1) * 128]
    for side in range(2):
        block = res_ref[:, :, side * 128 : side * 128 + 128].astype(F32)
        res_s[side] = block.reshape(1024, 128)
    for group in range(2):
        for n in range(4):
            rhs_s[group, n * SEQS : (n + 1) * SEQS, 128:] = jnp.broadcast_to(
                lane_block(n), (SEQS, 128)
            )

    for k in range(2):
        mine = [x_s[j, pl.ds(k, 256, stride=2), :] for j in range(4)]
        rows = jnp.concatenate(
            [jnp.concatenate(mine[:2], axis=1), jnp.concatenate(mine[2:], axis=1)], axis=0
        )
        base = jnp.concatenate(
            [
                jnp.concatenate(
                    [res_s[side, pl.ds(k * 2 + p, 256, stride=4), :] for side in range(2)], axis=1
                )
                for p in range(2)
            ],
            axis=0,
        )
        msa = (rows + base).astype(BF16).astype(F32)
        msa_s[...] = msa
        n_s[...] = normalize(msa).astype(BF16)
        for group in range(2):

            def project(part_index):
                start = part_index * 256 + group * 128
                return dot(n_s[...], wcol_ref[:, start : start + 128])

            q_s[group] = (project(0) * QUERY_SCALE).astype(BF16)
            k_s[group] = project(1).astype(BF16)
            values = project(2).astype(BF16)
            g_s[group] = jax.nn.sigmoid(project(3))
            for n in range(4):
                rhs_s[group, n * SEQS : (n + 1) * SEQS, :128] = values * lane_block(n)
        offset = (mask_ref[k] - 1.0) * 1e30

        def tile(t, _):
            span = pl.ds(pl.multiple_of(t * 128, 128), 128)
            masks = [lane_block(n) for n in range(4)]
            for group in range(2):
                out = attend_tile(
                    q_s[group, span, :], k_s[group], rhs_s.at[group], masks, lambda n: offset
                )
                heads_s[span, group * 128 : group * 128 + 128] = (
                    out * g_s[group, span, :]
                ).astype(BF16)
            if k == 1:
                pl.when(t == 0)(lambda: second(0))
                pl.when(t == 2)(lambda: third(0))
                pl.when(t == 3)(lambda: fourth(0))
            return 0

        lax.fori_loop(0, 4, tile, 0)
        updated = (msa_s[...] + dot(heads_s[...], wout_ref[...])).astype(BF16)
        upd_s[k] = updated
        outer = normalize(updated.astype(F32)).astype(BF16)
        factors = dot(wfac_ref[...], outer, TN) * mask_ref[k]
        left_s[k] = factors[:FACTOR].astype(BF16)
        right_s[k] = factors[FACTOR:].astype(BF16)
        if k == 0:
            pl.semaphore_wait(barrier, 31 + 14)
        first(k)

    wide_s[...] = jnp.zeros_like(wide_s)

    def widen(c, _):
        block = weight_ref[pl.ds(pl.multiple_of(c * 32, 32), 32), :]
        for j in range(4):
            rows = pl.ds(pl.multiple_of(c * 128 + j * 32, 32), 32)
            wide_s[rows, j * 128 : (j + 1) * 128] = block
        return 0

    lax.fori_loop(0, 32, widen, 0)
    second(1)

    def permute(c, _):
        source = lax.broadcasted_iota(jnp.int32, (32, 1024), 1)
        wanted = lax.broadcasted_iota(jnp.int32, (32, 1024), 0) * 32 + c
        rows = pl.ds(pl.multiple_of(c * 32, 32), 32)
        perm_s[rows, :] = (source == wanted).astype(F32).astype(BF16)
        return 0

    lax.fori_loop(0, 32, permute, 0)
    third(1)
    for k in range(2):
        arrived(half(below, 1, k), x_recv.at[k, below, 1])
        arrived(half(above, 0, k), x_recv.at[k, above, 0])
        for h in range(2):
            arrived(half(opposite, h, k), x_recv.at[k, opposite, h])
    lp_s[...] = dot(perm_s[...], l_s[...].reshape(1024, SEQS)).astype(BF16)
    for k in range(2):
        for slot in range(8):
            arrived(r_s.at[slot, 1 - core, k], f_recv.at[k, slot])
    fourth(1)

    def contract(jc, _):
        rights = r_s[pl.ds(jc * 2, 2)].reshape(256, SEQS)
        block = dot(lp_s[...], rights, NT)
        for c in range(32):
            for xi in range(4):
                rows = slice(c * 32 + xi * 8, c * 32 + xi * 8 + 8)
                tile = jnp.concatenate([block[rows, :128], block[rows, 128:]], axis=0)
                lhs_s[xi, jc, :, c * 128 : c * 128 + 128] = tile.astype(BF16)
        return 0

    lax.fori_loop(0, 4, contract, 0)
    update = dot(lhs_s[...].reshape(256, 4096), wide_s[...])
    send_s[...] = update.reshape(4, 8, 8, 512).astype(BF16)
    for step in range(4):
        slot = lax.rem(x + step, 4)
        send(
            send_s.at[slot],
            pair_ref.at[y_hi * 2 + y_lo],
            p_send.at[slot],
            p_recv.at[y_hi * 2 + y_lo],
            to_pair(slot),
        )
    for k in range(2):
        for slot in range(8):
            sent(right_s.at[k], r_send.at[k, slot], to_right(slot))
            arrived(right_s.at[k], f_send.at[k, slot])
        for slot in range(4):
            sent(left_s.at[k], l_send.at[k, slot], to_left(slot))
        for n in range(3):
            arrived(half(x, 0, k), up_send.at[k, n])
            arrived(half(x, 0, k), down_send.at[k, n])
        for way in range(2):
            for stage in range(3):
                arrived(relay_s.at[way, k], u_send.at[stage, way, k])
            arrived(relay_s.at[way, k], u_recv.at[2, way, k])
        arrived(upd_s.at[k], g_send.at[k])
        arrived(upd_s.at[k], g_recv.at[k])
        arrived(upd_s.at[k], own_sem.at[k])
    for slot in range(4):
        sent(send_s.at[slot], p_send.at[slot], to_pair(slot))
        arrived(pair_ref.at[slot], p_recv.at[slot])


def whole(shape):
    return pl.BlockSpec(shape, lambda *_: (0,) * len(shape))


def per_device(
    alignment,
    pair_rep,
    align_mask,
    residue_mask,
    bias_weight,
    row_proj_weight,
    row_out_weight,
    column_proj_weight,
    column_out_weight,
    outer_factor_weight,
    outer_out,
):
    branch = lax.axis_index("branch")
    dap = lax.axis_index("dap")
    vmem = pltpu.VMEM

    dma = pltpu.SemaphoreType.DMA
    half = jnp.transpose(row_proj_weight, (1, 0, 2))
    none = jnp.zeros_like(half)
    wrow = jnp.concatenate(
        [jnp.concatenate([half, none], axis=2), jnp.concatenate([none, half], axis=2)], axis=0
    ).reshape(512, 512)
    out_half = row_out_weight.reshape(4, 64, 256)
    out_none = jnp.zeros_like(out_half)
    wrow_out = jnp.concatenate(
        [
            jnp.concatenate([out_half, out_none], axis=2),
            jnp.concatenate([out_none, out_half], axis=2),
        ],
        axis=1,
    ).reshape(512, 512)

    seq_mask = lax.dynamic_slice_in_dim(align_mask, dap * 8, 8, 0).astype(F32)
    offset = ((seq_mask - 1.0) * 1e30).reshape(4, 2, SEQS)
    wcol_mine = jnp.transpose(column_proj_weight, (1, 0, 2)).reshape(256, 256)
    res_mask = lax.dynamic_slice_in_dim(align_mask, dap * 8 + branch * 2, 2, 1).astype(F32)
    res_mask = jnp.transpose(res_mask.reshape(256, 2, 2), (2, 1, 0)).reshape(2, 1, SEQS)
    got, residual, wcol = pl.pallas_call(
        front_kernel,
        in_specs=[pl.BlockSpec(memory_space=vmem)] * 6,
        out_specs=(pl.BlockSpec(memory_space=vmem),) * 3,
        out_shape=(
            jax.ShapeDtypeStruct((256, 8, 128), BF16),
            jax.ShapeDtypeStruct((64, 16, 256), BF16),
            jax.ShapeDtypeStruct((4, 256, 256), BF16),
        ),
        scratch_shapes=[
            vmem((4, 2, 8, 128), BF16),
            vmem((4, 8, 2, 8, 128), BF16),
            vmem((4, 2, 4, 8, 2, 8, 128), BF16),
            vmem((2, 128, SEQS), F32),
            vmem((4, SEQS, 128), BF16),
            vmem((4, SEQS, 128), BF16),
            vmem((4, SEQS, 128), F32),
            vmem((4, 4 * SEQS, 256), BF16),
            vmem((4, SEQS, 128), F32),
            vmem((2, 1024, 128), F32),
            vmem((64, 16, 256), BF16),
            vmem((2, 128, 128), F32),
            vmem((SEQS, 128), F32),
            vmem((256, 8, 128), BF16),
            pltpu.SemaphoreType.REGULAR,
            dma((32,)),
            dma((32,)),
            dma((8,)),
            dma((8,)),
            dma((3,)),
            dma((4,)),
            dma,
            dma,
            dma,
            dma,
        ],
        compiler_params=pltpu.CompilerParams(
            vmem_limit_bytes=VMEM_LIMIT, collective_id=1, has_side_effects=True
        ),
        name="row_attention",
    )(pair_rep, bias_weight, wcol_mine, alignment, wrow, offset)
    wcol = jnp.transpose(wcol.reshape(4, 256, 4, 64), (1, 2, 0, 3)).reshape(256, 1024)

    gathered, pairs = pl.pallas_call(
        back_kernel,
        in_specs=[pl.BlockSpec(memory_space=vmem)] * 8,
        out_specs=(pl.BlockSpec(memory_space=vmem),) * 2,
        out_shape=(
            jax.ShapeDtypeStruct((4, 2, SEQS, 256), BF16),
            jax.ShapeDtypeStruct((4, 8, 8, 512), BF16),
        ),
        scratch_shapes=[
            vmem((4, SEQS, 128), F32),
            vmem((2, 1024, 128), F32),
            vmem((SEQS, 256), F32),
            vmem((SEQS, 256), BF16),
            vmem((2, SEQS, 128), BF16),
            vmem((2, SEQS, 128), BF16),
            vmem((2, SEQS, 128), F32),
            vmem((2, 4 * SEQS, 256), BF16),
            vmem((SEQS, 256), BF16),
            vmem((2, FACTOR, SEQS), BF16),
            vmem((2, FACTOR, SEQS), BF16),
            vmem((2, SEQS, 256), BF16),
            vmem((4, 4, 2, FACTOR, SEQS), BF16),
            vmem((1024, SEQS), BF16),
            vmem((8, 2, 2, FACTOR, SEQS), BF16),
            vmem((1024, 1024), BF16),
            vmem((4096, 512), BF16),
            vmem((4, 4, 16, 4096), BF16),
            vmem((4, 8, 8, 512), BF16),
            vmem((2, 2, 256, 256), BF16),
            dma((2, 4)),
            dma((2, 4)),
            dma((2, 3)),
            dma((2, 3)),
            dma((2, 4, 2)),
            dma((2, 8)),
            dma((2, 8)),
            dma((2, 8)),
            dma((2, 8)),
            dma((3, 2, 2)),
            dma((3, 2, 2)),
            dma((2,)),
            dma((2,)),
            dma((2,)),
            dma((4,)),
            dma((4,)),
        ],
        compiler_params=pltpu.CompilerParams(
            vmem_limit_bytes=VMEM_LIMIT, collective_id=0, has_side_effects=True
        ),
        name="column_outer",
    )(
        got.reshape(64, 4, 8, 128),
        residual,
        wrow_out,
        wcol,
        column_out_weight,
        outer_factor_weight,
        res_mask,
        outer_out,
    )

    rows = jnp.transpose(gathered.reshape(4, 2, 2, 256, 256), (3, 2, 0, 1, 4))
    updated_alignment = rows.reshape(SEQS, 8, 256)

    mask_rows = lax.dynamic_slice_in_dim(align_mask, dap * 8, 8, 1).astype(BF16)
    mask_cols = lax.dynamic_slice_in_dim(align_mask, branch * 128, 128, 1).astype(BF16)
    counts = jnp.einsum("si,sj->ij", mask_rows, mask_cols, preferred_element_type=F32)
    res_float = residue_mask.astype(F32)
    live_rows = lax.dynamic_slice_in_dim(res_float, dap * 8, 8, 0)
    live_cols = lax.dynamic_slice_in_dim(res_float, branch * 128, 128, 0)
    factor = live_rows[:, None] * live_cols[None, :] / (counts + count_eps)
    update = jnp.transpose(pairs.reshape(2, 2, 8, 8, 4, 128), (3, 2, 1, 0, 4, 5))
    update = update.reshape(8, 128, 128).astype(F32)
    pair_out = (pair_rep.astype(F32) + update * factor[:, :, None]).astype(BF16)
    return (updated_alignment, pair_out)


def solution(mesh):
    placed = (
        P("dap", None, None),
        P("dap", "branch", None),
        P(),
        P(),
        P(),
        P(None, None, "branch"),
        P(),
        P(None, None, "branch"),
        P(),
        P(),
        P(),
    )
    return jax.shard_map(
        per_device,
        mesh=mesh,
        in_specs=placed,
        out_specs=(P(None, "dap", None), P("dap", "branch", None)),
        check_vma=False,
    )
```

```python
import functools
import math

import jax
import jax.numpy as jnp
from jax import lax
from jax.experimental import pallas as pl
from jax.experimental.pallas import tpu as pltpu
from jax.sharding import PartitionSpec as P

HEADS = 8
HEAD = 32
FACTOR = 32
norm_eps = 1e-05
count_eps = 0.001
LOG2E = math.log2(math.e)
QUERY_SCALE = LOG2E / math.sqrt(HEAD)
F32 = jnp.float32
BF16 = jnp.bfloat16
MESH = pl.DeviceIdType.MESH
VMEM_LIMIT = 60 * 1024 * 1024
SEQS = 512
TILE = 256
NT = (((1,), (1,)), ((), ()))
TN = (((0,), (1,)), ((), ()))


def normalize(values):
    centre = jnp.mean(values, axis=-1, keepdims=True)
    centred = values - centre
    spread = jnp.mean(centred * centred, axis=-1, keepdims=True)
    return centred * lax.rsqrt(spread + norm_eps)


def dot(a, b, dims=(((1,), (0,)), ((), ()))):
    return lax.dot_general(a, b, dims, preferred_element_type=F32)


def lane_block(index):
    lanes = lax.broadcasted_iota(jnp.int32, (1, 128), 1)
    return (lanes // HEAD == index).astype(F32).astype(BF16)


def place():
    branch = lax.axis_index("branch")
    dap = lax.axis_index("dap")
    return dict(
        branch=branch,
        dap=dap,
        y_hi=branch // 2,
        core=branch % 2,
        x=dap // 16,
        z=(dap // 2) % 8,
        y_lo=dap % 2,
    )


def z_turn(z, turn):
    reach = (turn + 1) // 2
    odd = turn % 2
    return lax.rem(z + odd * reach + (1 - odd) * (8 - reach), 8)


def signal(semaphore, to):
    pl.semaphore_signal(semaphore, 1, device_id=to, device_id_type=MESH)


def remote(src, dst, send_sem, recv_sem, to):
    pltpu.make_async_remote_copy(
        src, dst, send_sem, recv_sem, device_id=to, device_id_type=MESH
    ).start()


def arrived(dst, semaphore):
    pltpu.make_async_copy(dst, dst, semaphore).wait()


def attend_tile(q, k, rhs_s, lane_masks, extra):
    total = None
    for n in range(4):
        scores = dot(q * lane_masks[n], k, NT) + extra(n)
        scores = scores - jnp.max(scores, axis=1, keepdims=True)
        raised = jnp.exp2(scores).astype(BF16)
        part = dot(raised, rhs_s[n * SEQS : (n + 1) * SEQS, :])
        total = part if total is None else total + part
    return total[:, :128] / total[:, 128:]


def beside(first, second):
    return jnp.concatenate([first.astype(F32), second.astype(F32)], axis=1).astype(BF16)


def front_kernel(
    pair_ref,
    weight_ref,
    column_ref,
    x_ref,
    row_ref,
    mask_ref,
    heads_ref,
    resid_ref,
    wall_ref,
    block_s,
    line_s,
    bias_s,
    wide_s,
    q_s,
    k_s,
    g_s,
    rhs_s,
    x_s,
    res_s,
    resb_s,
    o_s,
    buf_s,
    out_s,
    wcol_ref,
    wrow_ref,
    mask_s,
    off_ref,
    mask_sem,
    ready,
    p_send,
    p_recv,
    z_send,
    z_recv,
    w_send,
    w_recv,
    res_send,
    res_recv,
    out_send,
    out_recv,
):
    at = place()
    branch, dap, x, z, y_lo = at["branch"], at["dap"], at["x"], at["z"], at["y_lo"]
    barrier = pltpu.get_barrier_semaphore()
    me = dap * 4 + branch
    mine = x * 8 + y_lo * 4 + branch

    def plane_device(other_x, other_y, other_b):
        return (other_b, other_x * 16 + z * 2 + other_y)

    def line(other_z):
        return (branch, x * 16 + other_z * 2 + y_lo)

    def in_plane(act):
        def each(step_x, _):
            other_x = lax.rem(x + step_x, 4)
            for step_y in range(2):
                other_y = lax.rem(y_lo + step_y, 2)
                for step in range(1, 4):
                    other_b = lax.rem(branch + step, 4)
                    act(other_x * 8 + other_y * 4 + other_b, other_x, other_y, other_b)

                @pl.when(jnp.logical_or(other_x != x, other_y != y_lo))
                def _():
                    act(other_x * 8 + other_y * 4 + branch, other_x, other_y, branch)

            return 0

        lax.fori_loop(0, 4, each, 0)

    in_plane(lambda slot, *to: signal(barrier, plane_device(*to)))
    for step in range(1, 8):
        signal(barrier, line(lax.rem(z + step, 8)))

    rows, cols, width = pair_ref.shape
    mask_rows = mask_ref.at[pl.ds(pl.multiple_of(dap * 8, 8), 8)]
    fetch = pltpu.make_async_copy(mask_rows, mask_s, mask_sem)
    fetch.start()
    empty = jnp.zeros((256, 64), BF16)
    for t in range(4):
        lanes = slice(t * 128, t * 128 + 128)
        wrow_ref[:256, lanes] = beside(row_ref[t], empty)
        wrow_ref[256:, lanes] = beside(empty, row_ref[t])
    for t in range(2):
        wcol_ref[t] = beside(column_ref[2 * t], column_ref[2 * t + 1])

    def pick(sp, _):
        for p in range(2):
            for side in range(2):
                block = x_ref[sp * 2 + p, :, side * 128 : side * 128 + 128]
                x_s[p * 2 + side] = block.astype(F32)
            for side in range(2):
                for k in range(2):
                    res_s[side, pl.ds(sp * 4 + k * 2 + p, 64, stride=16), :] = x_s[
                        p * 2 + side, pl.ds(branch * 2 + k, 64, stride=8), :
                    ]
        return 0

    lax.fori_loop(0, 4, pick, 0)
    for side in range(2):
        resb_s[:, :, side * 128 : side * 128 + 128] = (
            res_s[side].reshape(64, 16, 128).astype(BF16)
        )
    fetch.wait()
    off_ref[...] = (mask_s[...].astype(F32) - 1.0) * 1e30
    values = pair_ref[...].astype(F32).reshape(rows * cols, width)
    normed = normalize(values).astype(BF16)
    res = dot(weight_ref[...], normed, TN)
    for i in range(rows):
        tile = res[:, i * cols : (i + 1) * cols].astype(BF16)
        block_s[:, :, i, :] = tile.reshape(4, 2, cols)
    pl.semaphore_wait(barrier, 31 + 7)
    for step in range(1, 8):
        signal(ready, line(lax.rem(z + step, 8)))
    for turn in range(1, 8):
        other_z = z_turn(z, turn)
        remote(block_s, line_s.at[:, z], z_send.at[turn], z_recv.at[z], line(other_z))
    pltpu.make_async_copy(block_s, line_s.at[:, z], z_recv.at[z]).start()
    across = (lax.rem(branch + 2, 4), dap)
    partner = (branch // 2 * 2 + 1 - branch % 2, dap)
    far = lax.rem(branch + 2, 4)
    remote(wcol_ref, wall_ref.at[branch], w_send.at[0], w_recv.at[0], partner)
    remote(wcol_ref, wall_ref.at[branch], w_send.at[1], w_recv.at[1], across)
    own = pltpu.make_async_copy(wcol_ref, wall_ref.at[branch], w_recv.at[3])
    own.start()

    def project(sp, _):
        normed = []
        for p in range(2):
            normed.append(normalize(x_ref[sp * 2 + p].astype(F32)).astype(BF16))
        both = jnp.concatenate(normed, axis=1)
        projected = dot(both, wrow_ref[...])
        q_s[sp] = (projected[:, :128] * QUERY_SCALE).astype(BF16)
        k_s[sp] = projected[:, 128:256].astype(BF16)
        values = projected[:, 256:384].astype(BF16)
        g_s[sp] = jax.nn.sigmoid(projected[:, 384:])
        for n in range(4):
            rhs_s[sp, n * SEQS : (n + 1) * SEQS, :128] = values * lane_block(n)
            rhs_s[sp, n * SEQS : (n + 1) * SEQS, 128:] = jnp.broadcast_to(
                lane_block(n), (SEQS, 128)
            )
        return 0

    lax.fori_loop(0, 4, project, 0)

    for other_z in range(8):
        arrived(line_s.at[:, other_z], z_recv.at[other_z])
    odd = x % 2

    def plane_turn(t):
        return lax.rem(x + t // 2 * 2, 4) + t % 2 * (1 - 2 * odd)

    def post(t, _):
        other_x = plane_turn(t)
        for step_y in range(2):
            other_y = lax.rem(y_lo + step_y, 2)
            for step in range(4):
                other_b = lax.rem(branch + step, 4)
                source, target = line_s.at[other_b], bias_s.at[x, y_lo, branch]
                slot = other_x * 8 + other_y * 4 + other_b

                def go():
                    to = plane_device(other_x, other_y, other_b)
                    remote(source, target, p_send.at[slot], p_recv.at[mine], to)

                if step:
                    go()
                else:
                    pl.when(slot != mine)(go)
        return 0

    lax.fori_loop(0, 4, post, 0)
    pltpu.make_async_copy(line_s.at[branch], bias_s.at[x, y_lo, branch], p_recv.at[mine]).start()
    arrived(wall_ref.at[far], w_recv.at[1])
    remote(wall_ref.at[far], wall_ref.at[far], w_send.at[2], w_recv.at[2], partner)
    pl.semaphore_wait(ready, 7)

    def post_res(turn, _):
        other_z = z_turn(z, turn)

        def each(step_x, _):
            other_x = lax.rem(x + step_x, 4)
            for step_y in range(2):
                other_d = other_x * 16 + other_z * 2 + lax.rem(y_lo + step_y, 2)

                @pl.when(other_d != dap)
                def _():
                    source = resb_s.at[other_d]
                    remote(source, resid_ref.at[dap], res_send, res_recv, (branch, other_d))

            return 0

        return lax.fori_loop(0, 4, each, 0)

    lax.fori_loop(0, 8, post_res, 0)
    pltpu.make_async_copy(resb_s.at[dap], resid_ref.at[dap], res_recv).start()

    def step(t, _):
        other_x = plane_turn(t)
        span = pl.ds(pl.multiple_of(other_x * 128, 128), 128)
        masks = [lane_block(n) for n in range(4)]

        for slot in range(8):
            landed = bias_s.at[other_x, slot // 4, slot % 4]
            arrived(landed, p_recv.at[other_x * 8 + slot])
        for h in range(2):
            for b in range(4):
                sides = [bias_s[other_x, y, b, :, h].astype(F32) for y in range(2)]
                piece = jnp.stack(sides, axis=1).reshape(128, 128)
                wide_s[h, :, b * 128 : b * 128 + 128] = piece * LOG2E

        def some(u, _):
            for v in range(2):
                sp = u * 2 + v

                def extra(n):
                    return wide_s[n % 2] + off_ref[pl.ds(sp * 2 + n // 2, 1), :]

                out = attend_tile(q_s[sp, span, :], k_s[sp], rhs_s.at[sp], masks, extra)
                o_s[v] = out * g_s[sp, span, :]
                for k in range(2):
                    buf_s[pl.ds(sp * 2 + k, 64, stride=8), :] = o_s[v, pl.ds(k, 64, stride=2), :]
            return 0

        lax.fori_loop(0, 2, some, 0)
        base = other_x * 64
        out_s[pl.ds(base, 64)] = buf_s[...].reshape(64, 8, 128).astype(BF16)

        def post_out(turn, _):
            for step_y in range(2):
                other_d = other_x * 16 + z_turn(z, turn) * 2 + lax.rem(y_lo + step_y, 2)
                for step in range(1, 4):
                    other_b = lax.rem(branch + step, 4)
                    source = out_s.at[other_d * 4 + other_b]
                    remote(source, heads_ref.at[me], out_send, out_recv, (other_b, other_d))

                @pl.when(other_d != dap)
                def _():
                    source = out_s.at[other_d * 4 + branch]
                    remote(source, heads_ref.at[me], out_send, out_recv, (branch, other_d))

            return 0

        lax.fori_loop(0, 8, post_out, 0)

        @pl.when(t == 0)
        def _():
            pltpu.make_async_copy(out_s.at[me], heads_ref.at[me], out_recv).start()

        return 0

    lax.fori_loop(0, 4, step, 0)

    for turn in range(1, 8):
        arrived(block_s, z_send.at[turn])
    in_plane(lambda slot, *to: arrived(line_s.at[0], p_send.at[slot]))
    own.wait()
    for n in range(3):
        arrived(wcol_ref, w_send.at[n])
    arrived(wcol_ref, w_recv.at[0])
    arrived(wcol_ref, w_recv.at[2])
    arrived(resb_s.at[pl.ds(0, 63)], res_send)
    arrived(resid_ref, res_recv)
    arrived(out_s.at[pl.ds(0, 255)], out_send)
    arrived(heads_ref, out_recv)


def back_kernel(
    a_ref,
    res_ref,
    wrow_ref,
    wcol_ref,
    wout_ref,
    wfac_ref,
    mask_ref,
    weight_ref,
    gather_ref,
    pair_ref,
    x_s,
    res_s,
    msa_s,
    n_s,
    q_s,
    k_s,
    g_s,
    rhs_s,
    heads_s,
    wcol_s,
    left_s,
    right_s,
    upd_s,
    l_s,
    lp_s,
    r_s,
    perm_s,
    wide_s,
    lhs_s,
    send_s,
    relay_s,
    l_send,
    l_recv,
    up_send,
    down_send,
    x_recv,
    r_send,
    r_recv,
    f_send,
    f_recv,
    u_send,
    u_recv,
    g_send,
    g_recv,
    own_sem,
    p_send,
    p_recv,
):
    at = place()
    branch, dap, y_hi, core = at["branch"], at["dap"], at["y_hi"], at["core"]
    x, z, y_lo = at["x"], at["z"], at["y_lo"]
    barrier = pltpu.get_barrier_semaphore()

    def greet(step_x, _):
        other_x = lax.rem(x + step_x, 4)
        for step_y in range(2):
            other_d = other_x * 16 + z * 2 + lax.rem(y_lo + step_y, 2)
            for step in range(1, 4):
                signal(barrier, (lax.rem(branch + step, 4), other_d))

            @pl.when(other_d != dap)
            def _():
                signal(barrier, (branch, other_d))

        return 0

    lax.fori_loop(0, 4, greet, 0)
    for step in range(1, 8):
        other_z = lax.rem(z + step, 8)
        for other_core in range(2):
            signal(barrier, (y_hi * 2 + other_core, x * 16 + other_z * 2 + y_lo))

    def elsewhere(to):
        return jnp.logical_or(to[0] != branch, to[1] != dap)

    def send(src, dst, send_sem, recv_sem, to):
        other = elsewhere(to)

        @pl.when(other)
        def _():
            remote(src, dst, send_sem, recv_sem, to)

        @pl.when(jnp.logical_not(other))
        def _():
            pltpu.make_async_copy(src, dst, recv_sem).start()

    def sent(src, send_sem, to):
        @pl.when(elsewhere(to))
        def _():
            arrived(src, send_sem)

    def to_left(slot):
        return (slot // 2 * 2 + y_lo, x * 16 + z * 2 + slot % 2)

    def to_right(slot):
        return (branch, x * 16 + slot * 2 + y_lo)

    def to_pair(slot):
        return (x, slot * 16 + z * 2 + core)

    def x_line(other_x):
        return (branch, other_x * 16 + z * 2 + y_lo)

    def y_line(step):
        other = lax.rem(y_hi * 2 + y_lo + step, 4)
        return (other // 2 * 2 + core, x * 16 + z * 2 + other % 2)

    partner = (y_hi * 2 + 1 - core, dap)
    far = lax.rem(branch + 2, 4)
    above, below = lax.rem(x + 1, 4), lax.rem(x + 3, 4)
    opposite = lax.rem(x + 2, 4)
    steps = (1, 3)

    def part(way):
        return pl.ds(way * 256, 256)

    def half(other_x, h, k):
        return l_s.at[other_x, pl.ds(h * 2, 2), k]

    def pass_x(origin, h, k, send_sem, to):
        region = half(origin, h, k)
        remote(region, region, send_sem, x_recv.at[k, origin, h], x_line(to))

    def first(k):
        for step in range(4):
            slot = lax.rem(y_hi * 2 + y_lo + step, 4)
            send(
                left_s.at[k],
                l_s.at[x, branch, k],
                l_send.at[k, slot],
                l_recv.at[k, branch],
                to_left(slot),
            )
        for turn in range(8):
            slot = z_turn(z, turn)
            send(
                right_s.at[k],
                r_s.at[z, core, k],
                r_send.at[k, slot],
                r_recv.at[k, z],
                to_right(slot),
            )
        for way in range(2):
            remote(
                upd_s.at[k, part(way)],
                relay_s.at[way, k],
                u_send.at[0, way, k],
                u_recv.at[0, way, k],
                y_line(steps[way]),
            )
        remote(upd_s.at[k], gather_ref.at[branch, k], g_send.at[k], g_recv.at[k], partner)
        pltpu.make_async_copy(upd_s.at[k], gather_ref.at[branch, k], own_sem.at[k]).start()

    def second(k):
        for slot in range(4):
            arrived(l_s.at[x, slot, k], l_recv.at[k, slot])
        for h in range(2):
            pass_x(x, h, k, up_send.at[k, h], above)
            pass_x(x, 1 - h, k, down_send.at[k, 1 - h], below)
        for way in range(2):
            region = relay_s.at[way, k]
            arrived(region, u_recv.at[0, way, k])
            to = y_line(steps[way])
            remote(
                region,
                gather_ref.at[lax.rem(to[0] + 2, 4), k, part(way)],
                u_send.at[1, way, k],
                u_recv.at[1, way, k],
                to,
            )

    def third(k):
        for slot in range(8):
            region = r_s.at[slot, core, k]
            arrived(region, r_recv.at[k, slot])
            remote(region, region, f_send.at[k, slot], f_recv.at[k, slot], partner)
        arrived(half(below, 0, k), x_recv.at[k, below, 0])
        pass_x(below, 0, k, up_send.at[k, 2], above)
        arrived(half(above, 1, k), x_recv.at[k, above, 1])
        pass_x(above, 1, k, down_send.at[k, 2], below)

    def fourth(k):
        for way in range(2):
            region = gather_ref.at[far, k, part(way)]
            arrived(region, u_recv.at[1, way, k])
            remote(region, region, u_send.at[2, way, k], u_recv.at[2, way, k], partner)

    for part_index in range(4):
        for group in range(2):
            start = part_index * 256 + group * 128
            lanes = slice(part_index % 2 * 64, part_index % 2 * 64 + 64)
            wcol_s[:, start : start + 128] = beside(
                wcol_ref[2 * group, part_index // 2, :, lanes],
                wcol_ref[2 * group + 1, part_index // 2, :, lanes],
            )
    pieces = [a_ref[:, b].astype(F32).reshape(SEQS, 128).astype(BF16) for b in range(4)]
    moved = dot(jnp.concatenate(pieces, axis=1), wrow_ref[...])
    for j in range(4):
        x_s[j] = moved[:, j * 128 : (j + 1) * 128]
    for side in range(2):
        block = res_ref[:, :, side * 128 : side * 128 + 128].astype(F32)
        res_s[side] = block.reshape(1024, 128)
    for group in range(2):
        for n in range(4):
            rhs_s[group, n * SEQS : (n + 1) * SEQS, 128:] = jnp.broadcast_to(
                lane_block(n), (SEQS, 128)
            )

    for k in range(2):
        mine = [x_s[j, pl.ds(k, 256, stride=2), :] for j in range(4)]
        rows = jnp.concatenate(
            [jnp.concatenate(mine[:2], axis=1), jnp.concatenate(mine[2:], axis=1)], axis=0
        )
        base = jnp.concatenate(
            [
                jnp.concatenate(
                    [res_s[side, pl.ds(k * 2 + p, 256, stride=4), :] for side in range(2)], axis=1
                )
                for p in range(2)
            ],
            axis=0,
        )
        msa = (rows + base).astype(BF16).astype(F32)
        msa_s[...] = msa
        n_s[...] = normalize(msa).astype(BF16)
        for group in range(2):

            def project(part_index):
                start = part_index * 256 + group * 128
                return dot(n_s[...], wcol_s[:, start : start + 128])

            q_s[group] = (project(0) * QUERY_SCALE).astype(BF16)
            k_s[group] = project(1).astype(BF16)
            values = project(2).astype(BF16)
            g_s[group] = jax.nn.sigmoid(project(3))
            for n in range(4):
                rhs_s[group, n * SEQS : (n + 1) * SEQS, :128] = values * lane_block(n)
        offset = (mask_ref[k] - 1.0) * 1e30

        def tile(t, _):
            span = pl.ds(pl.multiple_of(t * 128, 128), 128)
            masks = [lane_block(n) for n in range(4)]
            for group in range(2):
                out = attend_tile(
                    q_s[group, span, :], k_s[group], rhs_s.at[group], masks, lambda n: offset
                )
                heads_s[span, group * 128 : group * 128 + 128] = (
                    out * g_s[group, span, :]
                ).astype(BF16)
            if k == 1:
                pl.when(t == 0)(lambda: second(0))
                pl.when(t == 2)(lambda: third(0))
                pl.when(t == 3)(lambda: fourth(0))
            return 0

        lax.fori_loop(0, 4, tile, 0)
        updated = (msa_s[...] + dot(heads_s[...], wout_ref[...])).astype(BF16)
        upd_s[k] = updated
        outer = normalize(updated.astype(F32)).astype(BF16)
        factors = dot(wfac_ref[...], outer, TN) * mask_ref[k]
        left_s[k] = factors[:FACTOR].astype(BF16)
        right_s[k] = factors[FACTOR:].astype(BF16)
        if k == 0:
            pl.semaphore_wait(barrier, 31 + 14)
        first(k)

    wide_s[...] = jnp.zeros_like(wide_s)

    def widen(c, _):
        block = weight_ref[pl.ds(pl.multiple_of(c * 32, 32), 32), :]
        for j in range(4):
            rows = pl.ds(pl.multiple_of(c * 128 + j * 32, 32), 32)
            wide_s[rows, j * 128 : (j + 1) * 128] = block
        return 0

    lax.fori_loop(0, 32, widen, 0)
    second(1)

    def permute(c, _):
        source = lax.broadcasted_iota(jnp.int32, (32, 1024), 1)
        wanted = lax.broadcasted_iota(jnp.int32, (32, 1024), 0) * 32 + c
        rows = pl.ds(pl.multiple_of(c * 32, 32), 32)
        perm_s[rows, :] = (source == wanted).astype(F32).astype(BF16)
        return 0

    lax.fori_loop(0, 32, permute, 0)
    third(1)
    for k in range(2):
        arrived(half(below, 1, k), x_recv.at[k, below, 1])
        arrived(half(above, 0, k), x_recv.at[k, above, 0])
        for h in range(2):
            arrived(half(opposite, h, k), x_recv.at[k, opposite, h])
    lp_s[...] = dot(perm_s[...], l_s[...].reshape(1024, SEQS)).astype(BF16)
    for k in range(2):
        for slot in range(8):
            arrived(r_s.at[slot, 1 - core, k], f_recv.at[k, slot])
    fourth(1)

    def contract(jc, _):
        rights = r_s[pl.ds(jc * 2, 2)].reshape(256, SEQS)
        block = dot(lp_s[...], rights, NT)
        for c in range(32):
            for xi in range(4):
                rows = slice(c * 32 + xi * 8, c * 32 + xi * 8 + 8)
                tile = jnp.concatenate([block[rows, :128], block[rows, 128:]], axis=0)
                lhs_s[xi, jc, :, c * 128 : c * 128 + 128] = tile.astype(BF16)
        return 0

    lax.fori_loop(0, 4, contract, 0)
    update = dot(lhs_s[...].reshape(256, 4096), wide_s[...])
    send_s[...] = update.reshape(4, 8, 8, 512).astype(BF16)
    for step in range(4):
        slot = lax.rem(x + step, 4)
        send(
            send_s.at[slot],
            pair_ref.at[y_hi * 2 + y_lo],
            p_send.at[slot],
            p_recv.at[y_hi * 2 + y_lo],
            to_pair(slot),
        )
    for k in range(2):
        for slot in range(8):
            sent(right_s.at[k], r_send.at[k, slot], to_right(slot))
            arrived(right_s.at[k], f_send.at[k, slot])
        for slot in range(4):
            sent(left_s.at[k], l_send.at[k, slot], to_left(slot))
        for n in range(3):
            arrived(half(x, 0, k), up_send.at[k, n])
            arrived(half(x, 0, k), down_send.at[k, n])
        for way in range(2):
            for stage in range(3):
                arrived(relay_s.at[way, k], u_send.at[stage, way, k])
            arrived(relay_s.at[way, k], u_recv.at[2, way, k])
        arrived(upd_s.at[k], g_send.at[k])
        arrived(upd_s.at[k], g_recv.at[k])
        arrived(upd_s.at[k], own_sem.at[k])
    for slot in range(4):
        sent(send_s.at[slot], p_send.at[slot], to_pair(slot))
        arrived(pair_ref.at[slot], p_recv.at[slot])


def whole(shape):
    return pl.BlockSpec(shape, lambda *_: (0,) * len(shape))


def per_device(
    alignment,
    pair_rep,
    align_mask,
    residue_mask,
    bias_weight,
    row_proj_weight,
    row_out_weight,
    column_proj_weight,
    column_out_weight,
    outer_factor_weight,
    outer_out,
):
    branch = lax.axis_index("branch")
    dap = lax.axis_index("dap")
    vmem = pltpu.VMEM

    dma = pltpu.SemaphoreType.DMA
    out_half = row_out_weight.reshape(4, 64, 256)
    out_none = jnp.zeros_like(out_half)
    wrow_out = jnp.concatenate(
        [
            jnp.concatenate([out_half, out_none], axis=2),
            jnp.concatenate([out_none, out_half], axis=2),
        ],
        axis=1,
    ).reshape(512, 512)

    res_mask = lax.dynamic_slice_in_dim(align_mask, dap * 8 + branch * 2, 2, 1).astype(F32)
    res_mask = jnp.transpose(res_mask.reshape(256, 2, 2), (2, 1, 0)).reshape(2, 1, SEQS)
    got, residual, wcol = pl.pallas_call(
        front_kernel,
        in_specs=[pl.BlockSpec(memory_space=vmem)] * 5 + [pl.BlockSpec(memory_space=pl.ANY)],
        out_specs=(pl.BlockSpec(memory_space=vmem),) * 3,
        out_shape=(
            jax.ShapeDtypeStruct((256, 8, 128), BF16),
            jax.ShapeDtypeStruct((64, 16, 256), BF16),
            jax.ShapeDtypeStruct((4, 2, 256, 128), BF16),
        ),
        scratch_shapes=[
            vmem((4, 2, 8, 128), BF16),
            vmem((4, 8, 2, 8, 128), BF16),
            vmem((4, 2, 4, 8, 2, 8, 128), BF16),
            vmem((2, 128, SEQS), F32),
            vmem((4, SEQS, 128), BF16),
            vmem((4, SEQS, 128), BF16),
            vmem((4, SEQS, 128), F32),
            vmem((4, 4 * SEQS, 256), BF16),
            vmem((4, SEQS, 128), F32),
            vmem((2, 1024, 128), F32),
            vmem((64, 16, 256), BF16),
            vmem((2, 128, 128), F32),
            vmem((SEQS, 128), F32),
            vmem((256, 8, 128), BF16),
            vmem((2, 256, 128), BF16),
            vmem((SEQS, SEQS), BF16),
            vmem((8, SEQS), jnp.int32),
            vmem((8, SEQS), F32),
            dma,
            pltpu.SemaphoreType.REGULAR,
            dma((32,)),
            dma((32,)),
            dma((8,)),
            dma((8,)),
            dma((3,)),
            dma((4,)),
            dma,
            dma,
            dma,
            dma,
        ],
        compiler_params=pltpu.CompilerParams(
            vmem_limit_bytes=VMEM_LIMIT, collective_id=1, has_side_effects=True
        ),
        name="row_attention",
    )(pair_rep, bias_weight, column_proj_weight, alignment, row_proj_weight, align_mask)

    gathered, pairs = pl.pallas_call(
        back_kernel,
        in_specs=[pl.BlockSpec(memory_space=vmem)] * 8,
        out_specs=(pl.BlockSpec(memory_space=vmem),) * 2,
        out_shape=(
            jax.ShapeDtypeStruct((4, 2, SEQS, 256), BF16),
            jax.ShapeDtypeStruct((4, 8, 8, 512), BF16),
        ),
        scratch_shapes=[
            vmem((4, SEQS, 128), F32),
            vmem((2, 1024, 128), F32),
            vmem((SEQS, 256), F32),
            vmem((SEQS, 256), BF16),
            vmem((2, SEQS, 128), BF16),
            vmem((2, SEQS, 128), BF16),
            vmem((2, SEQS, 128), F32),
            vmem((2, 4 * SEQS, 256), BF16),
            vmem((SEQS, 256), BF16),
            vmem((256, 1024), BF16),
            vmem((2, FACTOR, SEQS), BF16),
            vmem((2, FACTOR, SEQS), BF16),
            vmem((2, SEQS, 256), BF16),
            vmem((4, 4, 2, FACTOR, SEQS), BF16),
            vmem((1024, SEQS), BF16),
            vmem((8, 2, 2, FACTOR, SEQS), BF16),
            vmem((1024, 1024), BF16),
            vmem((4096, 512), BF16),
            vmem((4, 4, 16, 4096), BF16),
            vmem((4, 8, 8, 512), BF16),
            vmem((2, 2, 256, 256), BF16),
            dma((2, 4)),
            dma((2, 4)),
            dma((2, 3)),
            dma((2, 3)),
            dma((2, 4, 2)),
            dma((2, 8)),
            dma((2, 8)),
            dma((2, 8)),
            dma((2, 8)),
            dma((3, 2, 2)),
            dma((3, 2, 2)),
            dma((2,)),
            dma((2,)),
            dma((2,)),
            dma((4,)),
            dma((4,)),
        ],
        compiler_params=pltpu.CompilerParams(
            vmem_limit_bytes=VMEM_LIMIT, collective_id=0, has_side_effects=True
        ),
        name="column_outer",
    )(
        got.reshape(64, 4, 8, 128),
        residual,
        wrow_out,
        wcol,
        column_out_weight,
        outer_factor_weight,
        res_mask,
        outer_out,
    )

    rows = jnp.transpose(gathered.reshape(4, 2, 2, 256, 256), (3, 2, 0, 1, 4))
    updated_alignment = rows.reshape(SEQS, 8, 256)

    mask_rows = lax.dynamic_slice_in_dim(align_mask, dap * 8, 8, 1).astype(BF16)
    mask_cols = lax.dynamic_slice_in_dim(align_mask, branch * 128, 128, 1).astype(BF16)
    counts = jnp.einsum("si,sj->ij", mask_rows, mask_cols, preferred_element_type=F32)
    res_float = residue_mask.astype(F32)
    live_rows = lax.dynamic_slice_in_dim(res_float, dap * 8, 8, 0)
    live_cols = lax.dynamic_slice_in_dim(res_float, branch * 128, 128, 0)
    factor = live_rows[:, None] * live_cols[None, :] / (counts + count_eps)
    update = jnp.transpose(pairs.reshape(2, 2, 8, 8, 4, 128), (3, 2, 1, 0, 4, 5))
    update = update.reshape(8, 128, 128).astype(F32)
    pair_out = (pair_rep.astype(F32) + update * factor[:, :, None]).astype(BF16)
    return (updated_alignment, pair_out)


def solution(mesh):
    placed = (
        P("dap", None, None),
        P("dap", "branch", None),
        P(),
        P(),
        P(),
        P(None, None, "branch"),
        P(),
        P(None, None, "branch"),
        P(),
        P(),
        P(),
    )
    return jax.shard_map(
        per_device,
        mesh=mesh,
        in_specs=placed,
        out_specs=(P(None, "dap", None), P("dap", "branch", None)),
        check_vma=False,
    )
```

```python
import functools
import math

import jax
import jax.numpy as jnp
from jax import lax
from jax.experimental import pallas as pl
from jax.experimental.pallas import tpu as pltpu
from jax.sharding import PartitionSpec as P

HEADS = 8
HEAD = 32
FACTOR = 32
norm_eps = 1e-05
count_eps = 0.001
LOG2E = math.log2(math.e)
QUERY_SCALE = LOG2E / math.sqrt(HEAD)
F32 = jnp.float32
BF16 = jnp.bfloat16
MESH = pl.DeviceIdType.MESH
VMEM_LIMIT = 60 * 1024 * 1024
SEQS = 512
TILE = 256
NT = (((1,), (1,)), ((), ()))
TN = (((0,), (1,)), ((), ()))


def normalize(values):
    centre = jnp.mean(values, axis=-1, keepdims=True)
    centred = values - centre
    spread = jnp.mean(centred * centred, axis=-1, keepdims=True)
    return centred * lax.rsqrt(spread + norm_eps)


def dot(a, b, dims=(((1,), (0,)), ((), ()))):
    return lax.dot_general(a, b, dims, preferred_element_type=F32)


def lane_block(index):
    lanes = lax.broadcasted_iota(jnp.int32, (1, 128), 1)
    return (lanes // HEAD == index).astype(F32).astype(BF16)


def place():
    branch = lax.axis_index("branch")
    dap = lax.axis_index("dap")
    return dict(
        branch=branch,
        dap=dap,
        y_hi=branch // 2,
        core=branch % 2,
        x=dap // 16,
        z=(dap // 2) % 8,
        y_lo=dap % 2,
    )


def z_turn(z, turn):
    reach = (turn + 1) // 2
    odd = turn % 2
    return lax.rem(z + odd * reach + (1 - odd) * (8 - reach), 8)


def signal(semaphore, to):
    pl.semaphore_signal(semaphore, 1, device_id=to, device_id_type=MESH)


def remote(src, dst, send_sem, recv_sem, to):
    pltpu.make_async_remote_copy(
        src, dst, send_sem, recv_sem, device_id=to, device_id_type=MESH
    ).start()


def arrived(dst, semaphore):
    pltpu.make_async_copy(dst, dst, semaphore).wait()


def attend_tile(q, k, rhs_s, lane_masks, extra):
    total = None
    for n in range(4):
        scores = dot(q * lane_masks[n], k, NT) + extra(n)
        scores = scores - jnp.max(scores, axis=1, keepdims=True)
        raised = jnp.exp2(scores).astype(BF16)
        part = dot(raised, rhs_s[n * SEQS : (n + 1) * SEQS, :])
        total = part if total is None else total + part
    return total[:, :128] / total[:, 128:]


def beside(first, second):
    return jnp.concatenate([first.astype(F32), second.astype(F32)], axis=1).astype(BF16)


def front_kernel(
    pair_ref,
    weight_ref,
    column_ref,
    x_ref,
    row_ref,
    mask_ref,
    heads_ref,
    resid_ref,
    wall_ref,
    block_s,
    line_s,
    bias_s,
    wide_s,
    q_s,
    k_s,
    g_s,
    rhs_s,
    x_s,
    res_s,
    resb_s,
    o_s,
    buf_s,
    out_s,
    wcol_ref,
    wrow_ref,
    mask_s,
    off_ref,
    mask_sem,
    ready,
    p_send,
    p_recv,
    z_send,
    z_recv,
    w_send,
    w_recv,
    res_send,
    res_recv,
    out_send,
    out_recv,
):
    at = place()
    branch, dap, x, z, y_lo = at["branch"], at["dap"], at["x"], at["z"], at["y_lo"]
    barrier = pltpu.get_barrier_semaphore()
    me = dap * 4 + branch
    mine = x * 8 + y_lo * 4 + branch

    def plane_device(other_x, other_y, other_b):
        return (other_b, other_x * 16 + z * 2 + other_y)

    def line(other_z):
        return (branch, x * 16 + other_z * 2 + y_lo)

    def in_plane(act):
        def each(step_x, _):
            other_x = lax.rem(x + step_x, 4)
            for step_y in range(2):
                other_y = lax.rem(y_lo + step_y, 2)
                for step in range(1, 4):
                    other_b = lax.rem(branch + step, 4)
                    act(other_x * 8 + other_y * 4 + other_b, other_x, other_y, other_b)

                @pl.when(jnp.logical_or(other_x != x, other_y != y_lo))
                def _():
                    act(other_x * 8 + other_y * 4 + branch, other_x, other_y, branch)

            return 0

        lax.fori_loop(0, 4, each, 0)

    in_plane(lambda slot, *to: signal(barrier, plane_device(*to)))
    for step in range(1, 8):
        signal(barrier, line(lax.rem(z + step, 8)))

    rows, cols, width = pair_ref.shape
    mask_rows = mask_ref.at[pl.ds(pl.multiple_of(dap * 8, 8), 8)]
    fetch = pltpu.make_async_copy(mask_rows, mask_s, mask_sem)
    fetch.start()
    empty = jnp.zeros((256, 64), BF16)
    for t in range(4):
        lanes = slice(t * 128, t * 128 + 128)
        wrow_ref[:256, lanes] = beside(row_ref[t], empty)
        wrow_ref[256:, lanes] = beside(empty, row_ref[t])
    for t in range(2):
        wcol_ref[t] = beside(column_ref[2 * t], column_ref[2 * t + 1])

    def pick(sp, _):
        for p in range(2):
            for side in range(2):
                block = x_ref[sp * 2 + p, :, side * 128 : side * 128 + 128]
                x_s[p * 2 + side] = block.astype(F32)
            for side in range(2):
                for k in range(2):
                    res_s[side, pl.ds(sp * 4 + k * 2 + p, 64, stride=16), :] = x_s[
                        p * 2 + side, pl.ds(branch * 2 + k, 64, stride=8), :
                    ]
        return 0

    lax.fori_loop(0, 4, pick, 0)
    for side in range(2):
        resb_s[:, :, side * 128 : side * 128 + 128] = (
            res_s[side].reshape(64, 16, 128).astype(BF16)
        )
    fetch.wait()
    off_ref[...] = (mask_s[...].astype(F32) - 1.0) * 1e30
    values = pair_ref[...].astype(F32).reshape(rows * cols, width)
    normed = normalize(values).astype(BF16)
    res = dot(weight_ref[...], normed, TN)
    for i in range(rows):
        tile = res[:, i * cols : (i + 1) * cols].astype(BF16)
        block_s[:, :, i, :] = tile.reshape(4, 2, cols)
    pl.semaphore_wait(barrier, 31 + 7)
    for step in range(1, 8):
        signal(ready, line(lax.rem(z + step, 8)))
    for turn in range(1, 8):
        other_z = z_turn(z, turn)
        remote(block_s, line_s.at[:, z], z_send.at[turn], z_recv.at[z], line(other_z))
    pltpu.make_async_copy(block_s, line_s.at[:, z], z_recv.at[z]).start()
    across = (lax.rem(branch + 2, 4), dap)
    partner = (branch // 2 * 2 + 1 - branch % 2, dap)
    far = lax.rem(branch + 2, 4)
    remote(wcol_ref, wall_ref.at[branch], w_send.at[0], w_recv.at[0], partner)
    remote(wcol_ref, wall_ref.at[branch], w_send.at[1], w_recv.at[1], across)
    own = pltpu.make_async_copy(wcol_ref, wall_ref.at[branch], w_recv.at[3])
    own.start()

    def project(sp, _):
        normed = []
        for p in range(2):
            normed.append(normalize(x_ref[sp * 2 + p].astype(F32)).astype(BF16))
        both = jnp.concatenate(normed, axis=1)
        projected = dot(both, wrow_ref[...])
        q_s[sp] = (projected[:, :128] * QUERY_SCALE).astype(BF16)
        k_s[sp] = projected[:, 128:256].astype(BF16)
        values = projected[:, 256:384].astype(BF16)
        g_s[sp] = jax.nn.sigmoid(projected[:, 384:])
        for n in range(4):
            rhs_s[sp, n * SEQS : (n + 1) * SEQS, :128] = values * lane_block(n)
            rhs_s[sp, n * SEQS : (n + 1) * SEQS, 128:] = jnp.broadcast_to(
                lane_block(n), (SEQS, 128)
            )
        return 0

    lax.fori_loop(0, 4, project, 0)

    for other_z in range(8):
        arrived(line_s.at[:, other_z], z_recv.at[other_z])
    odd = x % 2

    def plane_turn(t):
        return lax.rem(x + t // 2 * 2, 4) + t % 2 * (1 - 2 * odd)

    def post(t, _):
        other_x = plane_turn(t)
        for step_y in range(2):
            other_y = lax.rem(y_lo + step_y, 2)
            for step in range(4):
                other_b = lax.rem(branch + step, 4)
                source, target = line_s.at[other_b], bias_s.at[x, y_lo, branch]
                slot = other_x * 8 + other_y * 4 + other_b

                def go():
                    to = plane_device(other_x, other_y, other_b)
                    remote(source, target, p_send.at[slot], p_recv.at[mine], to)

                if step:
                    go()
                else:
                    pl.when(slot != mine)(go)
        return 0

    lax.fori_loop(0, 4, post, 0)
    pltpu.make_async_copy(line_s.at[branch], bias_s.at[x, y_lo, branch], p_recv.at[mine]).start()
    arrived(wall_ref.at[far], w_recv.at[1])
    remote(wall_ref.at[far], wall_ref.at[far], w_send.at[2], w_recv.at[2], partner)
    pl.semaphore_wait(ready, 7)

    def post_res(turn, _):
        other_z = z_turn(z, turn)

        def each(step_x, _):
            other_x = lax.rem(x + step_x, 4)
            for step_y in range(2):
                other_d = other_x * 16 + other_z * 2 + lax.rem(y_lo + step_y, 2)

                @pl.when(other_d != dap)
                def _():
                    source = resb_s.at[other_d]
                    remote(source, resid_ref.at[dap], res_send, res_recv, (branch, other_d))

            return 0

        return lax.fori_loop(0, 4, each, 0)

    lax.fori_loop(0, 8, post_res, 0)
    pltpu.make_async_copy(resb_s.at[dap], resid_ref.at[dap], res_recv).start()

    def step(t, _):
        other_x = plane_turn(t)
        span = pl.ds(pl.multiple_of(other_x * 128, 128), 128)
        masks = [lane_block(n) for n in range(4)]

        for slot in range(8):
            landed = bias_s.at[other_x, slot // 4, slot % 4]
            arrived(landed, p_recv.at[other_x * 8 + slot])
        for h in range(2):
            for b in range(4):
                sides = [bias_s[other_x, y, b, :, h].astype(F32) for y in range(2)]
                piece = jnp.stack(sides, axis=1).reshape(128, 128)
                wide_s[h, :, b * 128 : b * 128 + 128] = piece * LOG2E

        def some(u, _):
            for v in range(2):
                sp = u * 2 + v

                def extra(n):
                    return wide_s[n % 2] + off_ref[pl.ds(sp * 2 + n // 2, 1), :]

                out = attend_tile(q_s[sp, span, :], k_s[sp], rhs_s.at[sp], masks, extra)
                o_s[v] = out * g_s[sp, span, :]
                for k in range(2):
                    buf_s[pl.ds(sp * 2 + k, 64, stride=8), :] = o_s[v, pl.ds(k, 64, stride=2), :]
            return 0

        lax.fori_loop(0, 2, some, 0)
        base = other_x * 64
        out_s[pl.ds(base, 64)] = buf_s[...].reshape(64, 8, 128).astype(BF16)

        def post_out(turn, _):
            for step_y in range(2):
                other_d = other_x * 16 + z_turn(z, turn) * 2 + lax.rem(y_lo + step_y, 2)
                for step in range(1, 4):
                    other_b = lax.rem(branch + step, 4)
                    source = out_s.at[other_d * 4 + other_b]
                    remote(source, heads_ref.at[me], out_send, out_recv, (other_b, other_d))

                @pl.when(other_d != dap)
                def _():
                    source = out_s.at[other_d * 4 + branch]
                    remote(source, heads_ref.at[me], out_send, out_recv, (branch, other_d))

            return 0

        lax.fori_loop(0, 8, post_out, 0)

        @pl.when(t == 0)
        def _():
            pltpu.make_async_copy(out_s.at[me], heads_ref.at[me], out_recv).start()

        return 0

    lax.fori_loop(0, 4, step, 0)

    for turn in range(1, 8):
        arrived(block_s, z_send.at[turn])
    in_plane(lambda slot, *to: arrived(line_s.at[0], p_send.at[slot]))
    own.wait()
    for n in range(3):
        arrived(wcol_ref, w_send.at[n])
    arrived(wcol_ref, w_recv.at[0])
    arrived(wcol_ref, w_recv.at[2])
    arrived(resb_s.at[pl.ds(0, 63)], res_send)
    arrived(resid_ref, res_recv)
    arrived(out_s.at[pl.ds(0, 255)], out_send)
    arrived(heads_ref, out_recv)


def back_kernel(
    a_ref,
    res_ref,
    wrow_ref,
    wcol_ref,
    wout_ref,
    wfac_ref,
    mask_ref,
    weight_ref,
    gather_ref,
    pair_ref,
    x_s,
    res_s,
    msa_s,
    n_s,
    q_s,
    k_s,
    g_s,
    rhs_s,
    heads_s,
    wcol_s,
    left_s,
    right_s,
    upd_s,
    l_s,
    lp_s,
    r_s,
    perm_s,
    wide_s,
    lhs_s,
    send_s,
    relay_s,
    l_send,
    l_recv,
    up_send,
    down_send,
    x_recv,
    r_send,
    r_recv,
    f_send,
    f_recv,
    u_send,
    u_recv,
    g_send,
    g_recv,
    own_sem,
    p_send,
    p_recv,
):
    at = place()
    branch, dap, y_hi, core = at["branch"], at["dap"], at["y_hi"], at["core"]
    x, z, y_lo = at["x"], at["z"], at["y_lo"]
    barrier = pltpu.get_barrier_semaphore()

    def greet(step_x, _):
        other_x = lax.rem(x + step_x, 4)
        for step_y in range(2):
            other_d = other_x * 16 + z * 2 + lax.rem(y_lo + step_y, 2)
            for step in range(1, 4):
                signal(barrier, (lax.rem(branch + step, 4), other_d))

            @pl.when(other_d != dap)
            def _():
                signal(barrier, (branch, other_d))

        return 0

    lax.fori_loop(0, 4, greet, 0)
    for step in range(1, 8):
        other_z = lax.rem(z + step, 8)
        for other_core in range(2):
            signal(barrier, (y_hi * 2 + other_core, x * 16 + other_z * 2 + y_lo))

    def elsewhere(to):
        return jnp.logical_or(to[0] != branch, to[1] != dap)

    def send(src, dst, send_sem, recv_sem, to):
        other = elsewhere(to)

        @pl.when(other)
        def _():
            remote(src, dst, send_sem, recv_sem, to)

        @pl.when(jnp.logical_not(other))
        def _():
            pltpu.make_async_copy(src, dst, recv_sem).start()

    def sent(src, send_sem, to):
        @pl.when(elsewhere(to))
        def _():
            arrived(src, send_sem)

    def to_left(slot):
        return (slot // 2 * 2 + y_lo, x * 16 + z * 2 + slot % 2)

    def to_right(slot):
        return (branch, x * 16 + slot * 2 + y_lo)

    def to_pair(slot):
        return (x, slot * 16 + z * 2 + core)

    def x_line(other_x):
        return (branch, other_x * 16 + z * 2 + y_lo)

    def y_line(step):
        other = lax.rem(y_hi * 2 + y_lo + step, 4)
        return (other // 2 * 2 + core, x * 16 + z * 2 + other % 2)

    partner = (y_hi * 2 + 1 - core, dap)
    far = lax.rem(branch + 2, 4)
    above, below = lax.rem(x + 1, 4), lax.rem(x + 3, 4)
    opposite = lax.rem(x + 2, 4)
    steps = (1, 3)

    def part(way):
        return pl.ds(way * 256, 256)

    def half(other_x, h, k):
        return l_s.at[other_x, pl.ds(h * 2, 2), k]

    def pass_x(origin, h, k, send_sem, to):
        region = half(origin, h, k)
        remote(region, region, send_sem, x_recv.at[k, origin, h], x_line(to))

    def first(k):
        for step in range(4):
            slot = lax.rem(y_hi * 2 + y_lo + step, 4)
            send(
                left_s.at[k],
                l_s.at[x, branch, k],
                l_send.at[k, slot],
                l_recv.at[k, branch],
                to_left(slot),
            )
        for turn in range(8):
            slot = z_turn(z, turn)
            send(
                right_s.at[k],
                r_s.at[z, core, k],
                r_send.at[k, slot],
                r_recv.at[k, z],
                to_right(slot),
            )
        for way in range(2):
            remote(
                upd_s.at[k, part(way)],
                relay_s.at[way, k],
                u_send.at[0, way, k],
                u_recv.at[0, way, k],
                y_line(steps[way]),
            )
        remote(upd_s.at[k], gather_ref.at[branch, k], g_send.at[k], g_recv.at[k], partner)
        pltpu.make_async_copy(upd_s.at[k], gather_ref.at[branch, k], own_sem.at[k]).start()

    def second(k):
        for slot in range(4):
            arrived(l_s.at[x, slot, k], l_recv.at[k, slot])
        for h in range(2):
            pass_x(x, h, k, up_send.at[k, h], above)
            pass_x(x, 1 - h, k, down_send.at[k, 1 - h], below)
        for way in range(2):
            region = relay_s.at[way, k]
            arrived(region, u_recv.at[0, way, k])
            to = y_line(steps[way])
            remote(
                region,
                gather_ref.at[lax.rem(to[0] + 2, 4), k, part(way)],
                u_send.at[1, way, k],
                u_recv.at[1, way, k],
                to,
            )

    def third(k):
        for slot in range(8):
            region = r_s.at[slot, core, k]
            arrived(region, r_recv.at[k, slot])
            remote(region, region, f_send.at[k, slot], f_recv.at[k, slot], partner)
        arrived(half(below, 0, k), x_recv.at[k, below, 0])
        pass_x(below, 0, k, up_send.at[k, 2], above)
        arrived(half(above, 1, k), x_recv.at[k, above, 1])
        pass_x(above, 1, k, down_send.at[k, 2], below)

    def fourth(k):
        for way in range(2):
            region = gather_ref.at[far, k, part(way)]
            arrived(region, u_recv.at[1, way, k])
            remote(region, region, u_send.at[2, way, k], u_recv.at[2, way, k], partner)

    for part_index in range(4):
        for group in range(2):
            start = part_index * 256 + group * 128
            lanes = slice(part_index % 2 * 64, part_index % 2 * 64 + 64)
            wcol_s[:, start : start + 128] = beside(
                wcol_ref[2 * group, part_index // 2, :, lanes],
                wcol_ref[2 * group + 1, part_index // 2, :, lanes],
            )
    pieces = [a_ref[:, b].astype(F32).reshape(SEQS, 128).astype(BF16) for b in range(4)]
    moved = dot(jnp.concatenate(pieces, axis=1), wrow_ref[...])
    for j in range(4):
        x_s[j] = moved[:, j * 128 : (j + 1) * 128]
    for side in range(2):
        block = res_ref[:, :, side * 128 : side * 128 + 128].astype(F32)
        res_s[side] = block.reshape(1024, 128)
    for group in range(2):
        for n in range(4):
            rhs_s[group, n * SEQS : (n + 1) * SEQS, 128:] = jnp.broadcast_to(
                lane_block(n), (SEQS, 128)
            )

    for k in range(2):
        mine = [x_s[j, pl.ds(k, 256, stride=2), :] for j in range(4)]
        rows = jnp.concatenate(
            [jnp.concatenate(mine[:2], axis=1), jnp.concatenate(mine[2:], axis=1)], axis=0
        )
        base = jnp.concatenate(
            [
                jnp.concatenate(
                    [res_s[side, pl.ds(k * 2 + p, 256, stride=4), :] for side in range(2)], axis=1
                )
                for p in range(2)
            ],
            axis=0,
        )
        msa = (rows + base).astype(BF16).astype(F32)
        msa_s[...] = msa
        n_s[...] = normalize(msa).astype(BF16)
        for group in range(2):

            def project(part_index):
                start = part_index * 256 + group * 128
                return dot(n_s[...], wcol_s[:, start : start + 128])

            q_s[group] = (project(0) * QUERY_SCALE).astype(BF16)
            k_s[group] = project(1).astype(BF16)
            values = project(2).astype(BF16)
            g_s[group] = jax.nn.sigmoid(project(3))
            for n in range(4):
                rhs_s[group, n * SEQS : (n + 1) * SEQS, :128] = values * lane_block(n)
        offset = (mask_ref[k] - 1.0) * 1e30

        def tile(t, _):
            span = pl.ds(pl.multiple_of(t * 128, 128), 128)
            masks = [lane_block(n) for n in range(4)]
            for group in range(2):
                out = attend_tile(
                    q_s[group, span, :], k_s[group], rhs_s.at[group], masks, lambda n: offset
                )
                heads_s[span, group * 128 : group * 128 + 128] = (
                    out * g_s[group, span, :]
                ).astype(BF16)
            if k == 1:
                pl.when(t == 0)(lambda: second(0))
                pl.when(t == 2)(lambda: third(0))
                pl.when(t == 3)(lambda: fourth(0))
            return 0

        lax.fori_loop(0, 4, tile, 0)
        updated = (msa_s[...] + dot(heads_s[...], wout_ref[...])).astype(BF16)
        upd_s[k] = updated
        outer = normalize(updated.astype(F32)).astype(BF16)
        factors = dot(wfac_ref[...], outer, TN) * mask_ref[k]
        left_s[k] = factors[:FACTOR].astype(BF16)
        right_s[k] = factors[FACTOR:].astype(BF16)
        if k == 0:
            pl.semaphore_wait(barrier, 31 + 14)
        first(k)

    wide_s[...] = jnp.zeros_like(wide_s)

    def widen(c, _):
        block = weight_ref[pl.ds(pl.multiple_of(c * 32, 32), 32), :]
        for j in range(4):
            rows = pl.ds(pl.multiple_of(c * 128 + j * 32, 32), 32)
            wide_s[rows, j * 128 : (j + 1) * 128] = block
        return 0

    lax.fori_loop(0, 32, widen, 0)
    second(1)

    def permute(c, _):
        source = lax.broadcasted_iota(jnp.int32, (32, 1024), 1)
        wanted = lax.broadcasted_iota(jnp.int32, (32, 1024), 0) * 32 + c
        rows = pl.ds(pl.multiple_of(c * 32, 32), 32)
        perm_s[rows, :] = (source == wanted).astype(F32).astype(BF16)
        return 0

    lax.fori_loop(0, 32, permute, 0)
    third(1)
    for k in range(2):
        arrived(half(below, 1, k), x_recv.at[k, below, 1])
        arrived(half(above, 0, k), x_recv.at[k, above, 0])
        for h in range(2):
            arrived(half(opposite, h, k), x_recv.at[k, opposite, h])
    lp_s[...] = dot(perm_s[...], l_s[...].reshape(1024, SEQS)).astype(BF16)
    for k in range(2):
        for slot in range(8):
            arrived(r_s.at[slot, 1 - core, k], f_recv.at[k, slot])
    fourth(1)

    def contract(jc, _):
        rights = r_s[pl.ds(jc * 2, 2)].reshape(256, SEQS)
        block = dot(lp_s[...], rights, NT)
        for c in range(32):
            for xi in range(4):
                rows = slice(c * 32 + xi * 8, c * 32 + xi * 8 + 8)
                tile = jnp.concatenate([block[rows, :128], block[rows, 128:]], axis=0)
                lhs_s[xi, jc, :, c * 128 : c * 128 + 128] = tile.astype(BF16)
        return 0

    lax.fori_loop(0, 4, contract, 0)
    update = dot(lhs_s[...].reshape(256, 4096), wide_s[...])
    send_s[...] = update.reshape(4, 8, 8, 512).astype(BF16)
    for step in range(4):
        slot = lax.rem(x + step, 4)
        send(
            send_s.at[slot],
            pair_ref.at[y_hi * 2 + y_lo],
            p_send.at[slot],
            p_recv.at[y_hi * 2 + y_lo],
            to_pair(slot),
        )
    for k in range(2):
        for slot in range(8):
            sent(right_s.at[k], r_send.at[k, slot], to_right(slot))
            arrived(right_s.at[k], f_send.at[k, slot])
        for slot in range(4):
            sent(left_s.at[k], l_send.at[k, slot], to_left(slot))
        for n in range(3):
            arrived(half(x, 0, k), up_send.at[k, n])
            arrived(half(x, 0, k), down_send.at[k, n])
        for way in range(2):
            for stage in range(3):
                arrived(relay_s.at[way, k], u_send.at[stage, way, k])
            arrived(relay_s.at[way, k], u_recv.at[2, way, k])
        arrived(upd_s.at[k], g_send.at[k])
        arrived(upd_s.at[k], g_recv.at[k])
        arrived(upd_s.at[k], own_sem.at[k])
    for slot in range(4):
        sent(send_s.at[slot], p_send.at[slot], to_pair(slot))
        arrived(pair_ref.at[slot], p_recv.at[slot])


def assemble_kernel(in_ref, out_ref, rows_s):
    for b in range(4):
        for k in range(2):
            for p in range(2):
                for side in range(2):
                    block = in_ref[b, k, p, :, side * 128 : side * 128 + 128].astype(F32)
                    rows_s[side, pl.ds(p * 8 + b * 2 + k, 32, stride=16), :] = block
    for side in range(2):
        block = rows_s[side].reshape(64, 8, 128)
        out_ref[:, :, side * 128 : side * 128 + 128] = block.astype(BF16)


def per_device(
    alignment,
    pair_rep,
    align_mask,
    residue_mask,
    bias_weight,
    row_proj_weight,
    row_out_weight,
    column_proj_weight,
    column_out_weight,
    outer_factor_weight,
    outer_out,
):
    branch = lax.axis_index("branch")
    dap = lax.axis_index("dap")
    vmem = pltpu.VMEM

    dma = pltpu.SemaphoreType.DMA
    out_half = row_out_weight.reshape(4, 64, 256)
    out_none = jnp.zeros_like(out_half)
    wrow_out = jnp.concatenate(
        [
            jnp.concatenate([out_half, out_none], axis=2),
            jnp.concatenate([out_none, out_half], axis=2),
        ],
        axis=1,
    ).reshape(512, 512)

    res_mask = lax.dynamic_slice_in_dim(align_mask, dap * 8 + branch * 2, 2, 1).astype(F32)
    res_mask = jnp.transpose(res_mask.reshape(256, 2, 2), (2, 1, 0)).reshape(2, 1, SEQS)
    got, residual, wcol = pl.pallas_call(
        front_kernel,
        in_specs=[pl.BlockSpec(memory_space=vmem)] * 5 + [pl.BlockSpec(memory_space=pl.ANY)],
        out_specs=(pl.BlockSpec(memory_space=vmem),) * 3,
        out_shape=(
            jax.ShapeDtypeStruct((256, 8, 128), BF16),
            jax.ShapeDtypeStruct((64, 16, 256), BF16),
            jax.ShapeDtypeStruct((4, 2, 256, 128), BF16),
        ),
        scratch_shapes=[
            vmem((4, 2, 8, 128), BF16),
            vmem((4, 8, 2, 8, 128), BF16),
            vmem((4, 2, 4, 8, 2, 8, 128), BF16),
            vmem((2, 128, SEQS), F32),
            vmem((4, SEQS, 128), BF16),
            vmem((4, SEQS, 128), BF16),
            vmem((4, SEQS, 128), F32),
            vmem((4, 4 * SEQS, 256), BF16),
            vmem((4, SEQS, 128), F32),
            vmem((2, 1024, 128), F32),
            vmem((64, 16, 256), BF16),
            vmem((2, 128, 128), F32),
            vmem((SEQS, 128), F32),
            vmem((256, 8, 128), BF16),
            vmem((2, 256, 128), BF16),
            vmem((SEQS, SEQS), BF16),
            vmem((8, SEQS), jnp.int32),
            vmem((8, SEQS), F32),
            dma,
            pltpu.SemaphoreType.REGULAR,
            dma((32,)),
            dma((32,)),
            dma((8,)),
            dma((8,)),
            dma((3,)),
            dma((4,)),
            dma,
            dma,
            dma,
            dma,
        ],
        compiler_params=pltpu.CompilerParams(
            vmem_limit_bytes=VMEM_LIMIT, collective_id=1, has_side_effects=True
        ),
        name="row_attention",
    )(pair_rep, bias_weight, column_proj_weight, alignment, row_proj_weight, align_mask)

    gathered, pairs = pl.pallas_call(
        back_kernel,
        in_specs=[pl.BlockSpec(memory_space=vmem)] * 8,
        out_specs=(pl.BlockSpec(memory_space=vmem),) * 2,
        out_shape=(
            jax.ShapeDtypeStruct((4, 2, SEQS, 256), BF16),
            jax.ShapeDtypeStruct((4, 8, 8, 512), BF16),
        ),
        scratch_shapes=[
            vmem((4, SEQS, 128), F32),
            vmem((2, 1024, 128), F32),
            vmem((SEQS, 256), F32),
            vmem((SEQS, 256), BF16),
            vmem((2, SEQS, 128), BF16),
            vmem((2, SEQS, 128), BF16),
            vmem((2, SEQS, 128), F32),
            vmem((2, 4 * SEQS, 256), BF16),
            vmem((SEQS, 256), BF16),
            vmem((256, 1024), BF16),
            vmem((2, FACTOR, SEQS), BF16),
            vmem((2, FACTOR, SEQS), BF16),
            vmem((2, SEQS, 256), BF16),
            vmem((4, 4, 2, FACTOR, SEQS), BF16),
            vmem((1024, SEQS), BF16),
            vmem((8, 2, 2, FACTOR, SEQS), BF16),
            vmem((1024, 1024), BF16),
            vmem((4096, 512), BF16),
            vmem((4, 4, 16, 4096), BF16),
            vmem((4, 8, 8, 512), BF16),
            vmem((2, 2, 256, 256), BF16),
            dma((2, 4)),
            dma((2, 4)),
            dma((2, 3)),
            dma((2, 3)),
            dma((2, 4, 2)),
            dma((2, 8)),
            dma((2, 8)),
            dma((2, 8)),
            dma((2, 8)),
            dma((3, 2, 2)),
            dma((3, 2, 2)),
            dma((2,)),
            dma((2,)),
            dma((2,)),
            dma((4,)),
            dma((4,)),
        ],
        compiler_params=pltpu.CompilerParams(
            vmem_limit_bytes=VMEM_LIMIT, collective_id=0, has_side_effects=True
        ),
        name="column_outer",
    )(
        got.reshape(64, 4, 8, 128),
        residual,
        wrow_out,
        wcol,
        column_out_weight,
        outer_factor_weight,
        res_mask,
        outer_out,
    )

    updated_alignment = pl.pallas_call(
        assemble_kernel,
        grid=(8,),
        in_specs=[pl.BlockSpec((4, 2, 2, 32, 256), lambda i: (0, 0, 0, i, 0))],
        out_specs=pl.BlockSpec((64, 8, 256), lambda i: (i, 0, 0)),
        out_shape=jax.ShapeDtypeStruct((SEQS, 8, 256), BF16),
        scratch_shapes=[vmem((2, 512, 128), F32)],
        name="assemble",
    )(gathered.reshape(4, 2, 2, 256, 256))

    mask_rows = lax.dynamic_slice_in_dim(align_mask, dap * 8, 8, 1).astype(BF16)
    mask_cols = lax.dynamic_slice_in_dim(align_mask, branch * 128, 128, 1).astype(BF16)
    counts = jnp.einsum("si,sj->ij", mask_rows, mask_cols, preferred_element_type=F32)
    res_float = residue_mask.astype(F32)
    live_rows = lax.dynamic_slice_in_dim(res_float, dap * 8, 8, 0)
    live_cols = lax.dynamic_slice_in_dim(res_float, branch * 128, 128, 0)
    factor = live_rows[:, None] * live_cols[None, :] / (counts + count_eps)
    update = jnp.transpose(pairs.reshape(2, 2, 8, 8, 4, 128), (3, 2, 1, 0, 4, 5))
    update = update.reshape(8, 128, 128).astype(F32)
    pair_out = (pair_rep.astype(F32) + update * factor[:, :, None]).astype(BF16)
    return (updated_alignment, pair_out)


def solution(mesh):
    placed = (
        P("dap", None, None),
        P("dap", "branch", None),
        P(),
        P(),
        P(),
        P(None, None, "branch"),
        P(),
        P(None, None, "branch"),
        P(),
        P(),
        P(),
    )
    return jax.shard_map(
        per_device,
        mesh=mesh,
        in_specs=placed,
        out_specs=(P(None, "dap", None), P("dap", "branch", None)),
        check_vma=False,
    )
```
